32 devices in a mesh: parts: 2 (over y), grp: 4 (over x, core), ep: 4 (over z).
Axes of the slice: x: 2, y: 2, z: 4, core: 2. Of those that a mesh axis runs over, the one named last changes fastest.
Arguments:
- tokens: bfloat16 [4096, 1024], P(('parts', 'grp', 'ep')), parts along dimension 0, may hold values from -6 to 6
- cotangent: bfloat16 [4096, 1024], P(('parts', 'grp', 'ep')), parts along dimension 0, may hold values from -6 to 6
- expert_ids: int32 [4096, 5], P(('parts', 'grp', 'ep')), parts along dimension 0, may hold values from 0 to 15, all different within a row; in each aligned block of 128 rows (0 to 127, 128 to 255, ...) at most 80 rows name the same one
- route_weights: float32 [4096, 5], P(('parts', 'grp', 'ep')), parts along dimension 0, may hold values from 0.1 to 1
- w_gate: bfloat16 [16, 1024, 512], P(('grp', 'ep')), may hold values from -0.1875 to 0.1875
- w_up: bfloat16 [16, 1024, 512], P(('grp', 'ep')), may hold values from -0.1875 to 0.1875
- w_down: bfloat16 [16, 512, 1024], P(('grp', 'ep')), may hold values from -0.25 to 0.25
Outputs:
- grad_tokens: bfloat16 [4096, 1024], P(('parts', 'grp', 'ep')), parts along dimension 0
- grad_weights: bfloat16 [4096, 5], P(('parts', 'grp', 'ep')), parts along dimension 0
The draws below stay inside these ranges and needn't reach their ends.
There are 2 independent parts, one for each index of `parts`. The reference program is written for one: setup_inputs(seed, part) draws one part's arguments, and reference() takes and returns one part's arrays. A program takes and returns all parts, laid end to end along the dimension named above; an argument that names none is the same for every part. Nothing has to cross between parts.
Inputs may be any that keep to these rules, and one draw needn't show every extreme that they name: `expert_ids`: each row names 5 different experts. In each aligned block of 128 rows (the rows of one device) no expert is named by more than 80 rows, a bound that some block reaches.
All inputs are finite; a program needn't handle non-finite values.
Results may differ from the reference program's by a relative error of at most 0.0057.
Values may be sent and summed in bfloat16 or wider, within the bound.
A program may use at most 64 MiB of HBM per device.

```python
import math
import jax
import jax.numpy as jnp
import numpy as np
from jax import lax

D = 1024
FF = 512
TOPK = 5
TOK_DEV = 128
EXPERTS = 16
CAP = 80
TOKENS = 2048
N_GRP = 4
N_EP = 4


def block_levels(rng, extent, split, least, largest):
    def one(axis_at, parts):
        steps = jax.random.uniform(jax.random.fold_in(jax.random.fold_in(rng, 6), axis_at), (parts,), jnp.float32, least / len(split), largest / len(split))
        return jnp.repeat(jnp.exp(steps), extent[axis_at] // parts).reshape((-1,) + (1,) * (len(extent) - axis_at - 1))

    factor_of = one(*split[0])
    for cut in split[1:]:
        factor_of = factor_of * one(*cut)
    return factor_of


def assign_block(rng, own, number, rows, amount, top, limit, slope):
    ranking = jax.random.permutation(rng, amount)
    crowded, ordinary = load_shares(amount, rows * top, limit, slope, True), load_shares(amount, rows * top, limit, slope, False)
    places = jnp.arange(amount)

    def named(sizes, turn):
        used = int((sizes > 0).sum())
        fixed = max(1, used // 4)
        shifted = fixed + (places - fixed + turn * (used - fixed)) % max(1, amount - fixed)
        return jnp.zeros((amount,), jnp.int32).at[ranking[jnp.where(places < fixed, places, shifted)]].set(jnp.asarray(sizes, jnp.int32))

    sizes = jnp.where(number % 4 == 0, named(crowded, number // 4), named(ordinary, number - number // 4 - 1))
    mixed = jax.random.permutation(jax.random.fold_in(own, 3), amount)
    source_of, taker = mixed[0:amount // 2 * 2:2], mixed[1:amount // 2 * 2:2]
    slack = jnp.minimum(sizes[source_of] - 1, limit - sizes[taker]) // 2
    slack = jnp.where((source_of == ranking[0]) | (taker == ranking[0]) | (sizes[taker] == 0), 0, jnp.maximum(slack, 0))
    shifted = jax.random.randint(jax.random.fold_in(own, 4), (amount // 2,), 0, 1 << 20) % (slack + 1)
    sizes = sizes.at[source_of].add(-shifted).at[taker].add(shifted)
    items = jnp.searchsorted(jnp.cumsum(sizes), jnp.arange(rows * top), side="right").astype(jnp.int32)
    grid = items.reshape(top, rows).T
    grid = grid[jax.random.permutation(jax.random.fold_in(own, 1), rows)]
    turn = jax.random.randint(jax.random.fold_in(own, 2), (rows, 1), 0, top)
    return jnp.take_along_axis(grid, (jnp.arange(top)[None, :] + turn) % top, axis=1)


def load_shares(count, total, most, skew, full):
    weights = [(1 << 20) // math.isqrt(standing ** skew) + 1 for standing in range(1, count + 1)]
    largest = most if full else min(most, max(-(-total // count), total * weights[0] // sum(weights)))
    least = 1 if total - largest >= count - 1 else 0
    holding, spare = [largest] + [least] * (count - 1), total - largest - least * (count - 1)
    while spare > 0:
        movable = [i for i in range(1, count) if holding[i] < largest] or [i for i in range(1, count) if holding[i] < most]
        whole, budget = sum([weights[i] for i in movable]), spare
        for i in movable:
            more = min(most - holding[i], max(1, budget * weights[i] // whole), spare)
            holding[i] = holding[i] + more
            spare = spare - more
    return np.array(holding)


def gaussian(rng, dims, scale, most, split=(), kind=jnp.bfloat16):
    values = scale * jax.random.normal(rng, dims, jnp.float32)
    if split:
        values = values * block_levels(rng, dims, split, -0.22, 0.18)
    return jnp.clip(values, -most, most).astype(kind)


def setup_inputs(seed: int = 0, part: int = 0) -> dict:
    key_of = jax.random.split(jax.random.key(seed), 8)
    part_splits = jax.random.split(jax.random.fold_in(key_of[7], part), 8)
    tokens = gaussian(part_splits[0], (TOKENS, D), 1.0, 6.0, ((0, 16),))
    cotangent = gaussian(part_splits[1], (TOKENS, D), 1.0, 6.0, ((0, 16),))
    expert_ids_keys = jax.random.split(jax.random.fold_in(part_splits[2], 1), TOKENS // TOK_DEV)
    expert_ids_turns = jax.random.permutation(jax.random.fold_in(part_splits[2], 3), TOKENS // TOK_DEV)
    expert_ids = jax.vmap(lambda own, number: assign_block(jax.random.fold_in(part_splits[2], 2), own, number, TOK_DEV, EXPERTS, TOPK, CAP, 2))(expert_ids_keys, expert_ids_turns).reshape((TOKENS, TOPK))
    route_weights = jnp.clip(jnp.exp(math.log(1.0) - 2.3025851 * jax.random.uniform(part_splits[3], (TOKENS, TOPK), jnp.float32) ** block_levels(part_splits[3], (TOKENS, TOPK), ((0, 16),), -0.2, 0.2)), 0.1, 1.0)
    w_gate = gaussian(key_of[4], (EXPERTS, D, FF), D ** -0.5, 0.1875, ((0, 16),))
    w_up = gaussian(key_of[5], (EXPERTS, D, FF), D ** -0.5, 0.1875, ((0, 16),))
    w_down = gaussian(key_of[6], (EXPERTS, FF, D), FF ** -0.5, 0.25, ((0, 16),))
    return {"tokens": tokens, "cotangent": cotangent, "expert_ids": expert_ids, "route_weights": route_weights, "w_gate": w_gate, "w_up": w_up, "w_down": w_down}


def expert_grads(rows_in, grads_in, w_gate, w_up, w_down):
    contract = (((1,), (1,)), ((), ()))
    gate_pre = jnp.dot(rows_in, w_gate, preferred_element_type=jnp.float32)
    up_pre = jnp.dot(rows_in, w_up, preferred_element_type=jnp.float32)
    hidden_grad = lax.dot_general(grads_in, w_down, contract, preferred_element_type=jnp.float32)
    sigmoid_gate = jax.nn.sigmoid(gate_pre)
    activation = gate_pre * sigmoid_gate
    hidden = activation * up_pre
    weight_grad = jnp.sum(hidden_grad * hidden, axis=-1).astype(jnp.bfloat16)
    grad_up = (hidden_grad * activation).astype(jnp.bfloat16)
    grad_gate = (hidden_grad * up_pre * sigmoid_gate * (1.0 + gate_pre * (1.0 - sigmoid_gate))).astype(jnp.bfloat16)
    row_terms = (lax.dot_general(grad_gate, w_gate, contract, preferred_element_type=jnp.float32)
                 + lax.dot_general(grad_up, w_up, contract, preferred_element_type=jnp.float32)).astype(jnp.bfloat16)
    return row_terms, weight_grad


def reference(tokens, cotangent, expert_ids, route_weights, w_gate, w_up, w_down):
    token_count, top_count = expert_ids.shape
    model_width = tokens.shape[1]
    experts = w_gate.shape[0]
    expert_slots = N_GRP * N_EP * CAP
    flat_ids = expert_ids.reshape(-1).astype(jnp.int32)
    pair_count = flat_ids.shape[0]
    sort_order = jnp.argsort(flat_ids, stable=True).astype(jnp.int32)
    counts = jnp.zeros((experts,), jnp.int32).at[flat_ids].add(1)
    starts = jnp.cumsum(counts) - counts
    sorted_ids = flat_ids[sort_order]
    slot_rank = (jnp.arange(pair_count, dtype=jnp.int32) - starts[sorted_ids]).astype(jnp.int32)
    slot_table = jnp.full((experts, expert_slots), pair_count, jnp.int32).at[sorted_ids, slot_rank].set(sort_order)
    token_pad = jnp.concatenate([tokens, jnp.zeros((1, model_width), tokens.dtype)], 0)
    grad_pad = jnp.concatenate([cotangent, jnp.zeros((1, model_width), cotangent.dtype)], 0)
    weight_pad = jnp.concatenate([route_weights.reshape(-1), jnp.zeros((1,), route_weights.dtype)], 0)

    def visit(state_pair, expert):
        token_acc, weight_acc = state_pair
        slot_pairs = slot_table[expert]
        tok_idx = jnp.where(slot_pairs < pair_count, slot_pairs // top_count, token_count).astype(jnp.int32)
        row_terms, weight_grad = expert_grads(token_pad[tok_idx], grad_pad[tok_idx],
                                              w_gate[expert], w_up[expert], w_down[expert])
        slot_weight = weight_pad[slot_pairs]
        token_acc = token_acc.at[tok_idx].add(slot_weight[:, None] * row_terms.astype(jnp.float32))
        weight_acc = weight_acc.at[slot_pairs].set(weight_grad)
        return (token_acc, weight_acc), None

    start_state = (jnp.zeros((token_count + 1, model_width), jnp.float32),
                   jnp.zeros((pair_count + 1,), jnp.bfloat16))
    final_state, unused = lax.scan(visit, start_state, jnp.arange(experts, dtype=jnp.int32))
    token_acc, weight_acc = final_state
    return token_acc[:token_count].astype(jnp.bfloat16), weight_acc[:pair_count].reshape(token_count, top_count)
```

```python
import functools

import jax
import jax.numpy as jnp
from jax import lax
from jax.experimental import pallas as pl
from jax.experimental.pallas import tpu as pltpu
from jax.sharding import PartitionSpec as P

LANES = 128
CORES = 2
VMEM_ROOM = 56 * 1024 * 1024


def expert_grads(rows_in, grads_in, w_gate, w_up, w_down):
    contract = (((1,), (1,)), ((), ()))
    gate_pre = jnp.dot(rows_in, w_gate, preferred_element_type=jnp.float32)
    up_pre = jnp.dot(rows_in, w_up, preferred_element_type=jnp.float32)
    hidden_grad = lax.dot_general(grads_in, w_down, contract, preferred_element_type=jnp.float32)
    sigmoid_gate = jax.nn.sigmoid(gate_pre)
    activation = gate_pre * sigmoid_gate
    hidden = activation * up_pre
    weight_grad = jnp.sum(hidden_grad * hidden, axis=-1).astype(jnp.bfloat16)
    grad_up = (hidden_grad * activation).astype(jnp.bfloat16)
    grad_gate = (
        hidden_grad * up_pre * sigmoid_gate * (1.0 + gate_pre * (1.0 - sigmoid_gate))
    ).astype(jnp.bfloat16)
    row_terms = (
        lax.dot_general(grad_gate, w_gate, contract, preferred_element_type=jnp.float32)
        + lax.dot_general(grad_up, w_up, contract, preferred_element_type=jnp.float32)
    ).astype(jnp.bfloat16)
    return (row_terms, weight_grad)


def slot_plan(routes, experts, capacity):
    tok_rows, top_count = routes.shape
    flat_ids = routes.reshape(-1)
    pad_pair = flat_ids.shape[0]
    pair_ids = jnp.arange(pad_pair, dtype=jnp.int32)
    sort_order = jnp.argsort(flat_ids, stable=True)
    sorted_ids = flat_ids[sort_order]
    onehot = (flat_ids[:, None] == jnp.arange(experts, dtype=jnp.int32)[None, :]).astype(jnp.int32)
    counts = jnp.sum(onehot, axis=0)
    earlier = jnp.tri(experts, k=-1, dtype=jnp.int32)
    starts = jnp.sum(earlier * counts[None, :], axis=1)
    sorted_rank = pair_ids - starts[sorted_ids]
    sorted_slot = sorted_ids * capacity + sorted_rank
    slot_of_pair = jnp.zeros((pad_pair,), jnp.int32).at[sort_order].set(sorted_slot)
    slot_pair = jnp.full((experts * capacity,), pad_pair, jnp.int32).at[sorted_slot].set(sort_order)
    slot_token = jnp.where(slot_pair < pad_pair, slot_pair // top_count, tok_rows)
    return (slot_of_pair, slot_token, slot_pair)


def place_rows(source_rows, slot_token):
    padded = jnp.concatenate(
        [source_rows, jnp.zeros((1, source_rows.shape[1]), source_rows.dtype)], 0
    )
    return padded[slot_token]


def dispatch_plan(tokens, cotangent, expert_ids, route_weights, w_gate, w_up, w_down):
    group_count = lax.axis_size("grp")
    lane_count = lax.axis_size("ep")
    experts = group_count * lane_count
    tok_rows, top_count = expert_ids.shape
    model_width = tokens.shape[1]
    capacity = 2 * tok_rows * top_count // experts
    slot_of_pair, slot_token, unused_pairs = slot_plan(expert_ids, experts, capacity)
    send_rows = place_rows(tokens, slot_token).reshape(
        group_count, lane_count, capacity, model_width
    )
    send_grads = place_rows(cotangent, slot_token).reshape(
        group_count, lane_count, capacity, model_width
    )
    send_rows, send_grads = (
        lax.all_to_all(send_rows, "grp", split_axis=0, concat_axis=0, tiled=True),
        lax.all_to_all(send_grads, "grp", split_axis=0, concat_axis=0, tiled=True),
    )
    rows_in = lax.all_to_all(send_rows, "ep", split_axis=1, concat_axis=1, tiled=True)
    grads_in = lax.all_to_all(send_grads, "ep", split_axis=1, concat_axis=1, tiled=True)
    leading = rows_in.shape[:3]
    row_terms, weight_grad = expert_grads(
        rows_in.reshape(-1, model_width),
        grads_in.reshape(-1, model_width),
        w_gate[0],
        w_up[0],
        w_down[0],
    )
    row_terms = row_terms.reshape(leading + (model_width,))
    weight_grad = weight_grad.reshape(leading)
    row_terms, weight_grad = (
        lax.all_to_all(row_terms, "ep", split_axis=1, concat_axis=1, tiled=True),
        lax.all_to_all(weight_grad, "ep", split_axis=1, concat_axis=1, tiled=True),
    )
    row_terms, weight_grad = (
        lax.all_to_all(row_terms, "grp", split_axis=0, concat_axis=0, tiled=True),
        lax.all_to_all(weight_grad, "grp", split_axis=0, concat_axis=0, tiled=True),
    )
    row_terms = row_terms.reshape(experts * capacity, model_width)
    weight_grad = weight_grad.reshape(experts * capacity)
    picked = row_terms[slot_of_pair].reshape(tok_rows, top_count, model_width)
    grad_tokens = jnp.sum(route_weights[:, :, None] * picked.astype(jnp.float32), axis=1)
    grad_weights = weight_grad[slot_of_pair].reshape(tok_rows, top_count)
    return (grad_tokens.astype(jnp.bfloat16), grad_weights)


CUTS = 2


def gw_rows(experts):
    return -(-experts // 16) * 16


def gather_kernel(
    n_grp, n_ep, tok_hbm, cot_hbm, ids_ref, route_ref, wg_hbm, wu_hbm, wd_hbm,
    out_ref, gw_ref,
    buf, parts, r1, s2, r2, s3, r3, r4, mine, w_gate, w_up, w_down,
    load_sem, z_sem, far_sem, x_sem, c_sem, got_sem, half_sem,
    s1_sem, r1_sem, s2_sem, r2_sem, s3_sem, r3_sem, r4_sem,
):
    n_x = n_grp // CORES
    rows, width = out_ref.shape
    slabs, mark = width // LANES, rows * (width // LANES)
    named = gw_rows(n_grp * n_ep)
    middle = slabs // CUTS * rows
    spans = [(i * middle, (i + 1) * middle) for i in range(CUTS)]
    spans[-1] = (spans[-1][0], mark + named)
    g, z = lax.axis_index("grp"), lax.axis_index("ep")
    x, c = g // CORES, g % CORES
    other_c = 1 - c
    expert = g * n_ep + z
    core_peer = {"grp": x * CORES + other_c, "ep": z}

    def x_of(step):
        return lax.rem(x + step, n_x)

    def x_peer(step):
        return {"grp": x_of(step) * CORES + c, "ep": z}

    own = buf.at[z, x, c]
    loads = [
        pltpu.make_async_copy(
            ref.at[:, pl.ds(s * LANES, LANES)],
            own.at[pl.ds((half * slabs + s) * rows, rows)],
            load_sem.at[half * slabs + s],
        )
        for half, ref in enumerate((tok_hbm, cot_hbm)) for s in range(slabs)
    ]
    loads += [
        pltpu.make_async_copy(ref.at[0], target, load_sem.at[2 * slabs + i])
        for i, (ref, target) in enumerate(((wg_hbm, w_gate), (wu_hbm, w_up), (wd_hbm, w_down)))
    ]
    for load in loads:
        load.start()

    item = lax.broadcasted_iota(jnp.int32, (named, LANES), 0)
    routed = jnp.zeros((named, LANES), jnp.float32)
    for k in range(ids_ref.shape[0]):
        routed += jnp.where(item == ids_ref[k:k + 1, :], route_ref[k:k + 1, :], 0.0)
    high = routed.astype(jnp.bfloat16)
    buf[z, x, c, 2 * mark:2 * mark + named, :] = high
    buf[z, x, c, 2 * mark + named:, :] = (routed - high.astype(jnp.float32)).astype(jnp.bfloat16)

    barrier = pltpu.get_barrier_semaphore()
    peers = [core_peer] + [x_peer(step) for step in range(1, n_x)]
    peers += [{"grp": g, "ep": lax.rem(z + step, n_ep)} for step in range(1, n_ep)]
    for peer in peers:
        pl.semaphore_signal(barrier, inc=1, device_id=peer, device_id_type=pl.DeviceIdType.MESH)
    pl.semaphore_wait(barrier, len(peers))

    def remote(source, target, send, recv, peer):
        return pltpu.make_async_remote_copy(
            src_ref=source, dst_ref=target, send_sem=send, recv_sem=recv,
            device_id=peer, device_id_type=pl.DeviceIdType.MESH,
        )

    sides = jnp.minimum(z, n_ep - 1 - z)

    def place(k):
        near = jnp.where(k % 2 == 1, z - (k + 1) // 2, z + k // 2)
        far = jnp.where(2 * z < n_ep - 1, k, n_ep - 1 - k)
        return jnp.where(k <= 2 * sides, near, far)

    def via_z(zs):
        return jnp.logical_or(zs == 0, zs == n_ep - 1)

    half = 5 * (mark + named) // 64 * 16

    def near_half(ref):
        return ref.at[pl.ds(0, half)]

    def far_half(ref):
        return ref.at[pl.ds(half, 2 * (mark + named) - half)]

    def along_z(zs, step):
        block = buf.at[zs, x, c]
        return remote(block, block, z_sem.at[zs, (step + 1) // 2], got_sem.at[zs, x, c],
                      {"grp": g, "ep": z + step})

    def far_z(zs, xs, step):
        block = near_half(buf.at[zs, xs, c])
        return remote(block, block, far_sem.at[zs, xs, (step + 1) // 2], got_sem.at[zs, xs, c],
                      {"grp": g, "ep": z + step})

    def along_x(zs, step):
        block = buf.at[zs, x, c]
        return remote(block, block, x_sem.at[zs, step - 1], got_sem.at[zs, x, c], x_peer(step))

    def half_x(zs, step):
        block = far_half(buf.at[zs, x, c])
        return remote(block, block, x_sem.at[zs, step - 1], half_sem.at[zs, x], x_peer(step))

    def to_core(zs, xs):
        block = buf.at[zs, xs, c]
        return remote(block, block, c_sem.at[zs, xs], got_sem.at[zs, xs, c], core_peer)

    def arrived(zs, xs, cs):
        block = buf.at[zs, xs, cs]
        remote(block, block, z_sem.at[zs, 0], got_sem.at[zs, xs, cs], core_peer).wait_recv()

    def spread_up(zs):
        return jnp.logical_and(zs <= z, z < n_ep - 1)

    def spread_down(zs):
        return jnp.logical_and(zs >= z, z > 0)

    def crosses(zs):
        return jnp.logical_or(zs == z, jnp.logical_not(via_z(zs)))

    def each_near(zs, act):
        @pl.when(spread_up(zs))
        def _():
            act(along_z(zs, 1))

        @pl.when(spread_down(zs))
        def _():
            act(along_z(zs, -1))

        @pl.when(crosses(zs))
        def _():
            for step in range(1, n_x):
                act(along_x(zs, step))

        @pl.when(jnp.logical_not(crosses(zs)))
        def _():
            for step in range(1, n_x):
                act(half_x(zs, step))

        act(to_core(zs, x))

    def far_arrived(zs, xs):
        @pl.when(crosses(zs))
        def _():
            arrived(zs, xs, c)

        @pl.when(jnp.logical_not(crosses(zs)))
        def _():
            block = near_half(buf.at[zs, xs, c])
            remote(block, block, z_sem.at[zs, 0], got_sem.at[zs, xs, c], core_peer).wait_recv()

    def rest_arrived(zs, xs):
        @pl.when(jnp.logical_not(crosses(zs)))
        def _():
            block = far_half(buf.at[zs, xs, c])
            remote(block, block, z_sem.at[zs, 0], half_sem.at[zs, xs], core_peer).wait_recv()

    def each_far(zs, xs, act):
        @pl.when(jnp.logical_and(via_z(zs), spread_up(zs)))
        def _():
            act(far_z(zs, xs, 1))

        @pl.when(jnp.logical_and(via_z(zs), spread_down(zs)))
        def _():
            act(far_z(zs, xs, -1))

    def start(copy):
        copy.start()

    def wait_send(copy):
        copy.wait_send()

    def take(k):
        zs = place(k)
        arrived(zs, x, c)
        each_near(zs, start)

    contract = (((1,), (1,)), ((), ()))

    def compute(zs, xs):
        def at(low, high):
            return jnp.concatenate(
                [buf[zs, xs, :, s * rows:(s + 1) * rows, :].reshape(CORES * rows, LANES)
                 for s in range(low, high)], axis=1)

        rows_in = at(0, slabs)
        gate_pre = jnp.dot(rows_in, w_gate[...], preferred_element_type=jnp.float32)
        up_pre = jnp.dot(rows_in, w_up[...], preferred_element_type=jnp.float32)
        hidden_grad = lax.dot_general(at(slabs, 2 * slabs), w_down[...], contract,
                                      preferred_element_type=jnp.float32)
        sigmoid_gate = 1.0 / (1.0 + jnp.exp(-gate_pre))
        activation = gate_pre * sigmoid_gate
        product = hidden_grad * (activation * up_pre)
        lane_sums = product[:, :LANES]
        for low in range(LANES, product.shape[1], LANES):
            lane_sums += product[:, low:low + LANES]
        grad_up = (hidden_grad * activation).astype(jnp.bfloat16)
        grad_gate = (
            hidden_grad * up_pre * sigmoid_gate * (1.0 + gate_pre * (1.0 - sigmoid_gate))
        ).astype(jnp.bfloat16)
        terms = lax.dot_general(grad_gate, w_gate[...], contract, preferred_element_type=jnp.float32)
        terms += lax.dot_general(grad_up, w_up[...], contract, preferred_element_type=jnp.float32)
        for cs in range(CORES):
            mine_only = item == expert
            sent = buf[zs, xs, cs, 2 * mark:2 * mark + named, :].astype(jnp.float32)
            sent += buf[zs, xs, cs, 2 * mark + named:, :].astype(jnp.float32)
            weight = jnp.sum(jnp.where(mine_only, sent, 0.0), axis=0, keepdims=True)
            scale = jnp.broadcast_to(weight, (rows, LANES)).T
            here = slice(cs * rows, (cs + 1) * rows)
            for s in range(slabs):
                slab = terms[here, s * LANES:(s + 1) * LANES] * scale
                parts[zs, xs, cs, s * rows:(s + 1) * rows, :] = slab.astype(jnp.bfloat16)
            weight_grad = jnp.sum(lane_sums[here].T, axis=0, keepdims=True)
            parts[zs, xs, cs, mark:, :] = jnp.where(mine_only, weight_grad, 0.0).astype(jnp.bfloat16)

    def first_copy(zs, xs, cut):
        return remote(parts.at[zs, xs, other_c, cuts[cut]], r1.at[zs, xs, cuts[cut]],
                      s1_sem.at[zs, xs, cut], r1_sem.at[zs, xs, cut], core_peer)

    def second_copy(zs, step, cut):
        return remote(s2.at[zs, step - 1, cuts[cut]], r2.at[zs, step - 1, cuts[cut]],
                      s2_sem.at[zs, step - 1, cut], r2_sem.at[zs, step - 1, cut], x_peer(step))

    def third_copy(zs, cut):
        return remote(s3.at[zs, cuts[cut]], r3.at[z, cuts[cut]], s3_sem.at[zs, cut],
                      r3_sem.at[z, cut], {"grp": g, "ep": zs})

    def third_arrived(zs, cut):
        return remote(s3.at[zs, cuts[cut]], r3.at[zs, cuts[cut]], s3_sem.at[zs, cut],
                      r3_sem.at[zs, cut], core_peer)

    cuts = [pl.ds(low, high - low) for low, high in spans]

    def pair_sum(zs, xs, cut):
        low, high = spans[cut]
        return (parts[zs, xs, c, low:high].astype(jnp.float32)
                + r1[zs, xs, low:high].astype(jnp.float32))

    def through(zs):
        return jnp.logical_and(via_z(z), jnp.logical_not(via_z(zs)))

    def late(k):
        return jnp.logical_and(k == 0, jnp.logical_not(via_z(z)))

    def fourth_copy(zs, step, cut):
        return remote(s2.at[zs, step - 1, cuts[cut]], r4.at[z, step - 1, cuts[cut]],
                      s2_sem.at[zs, step - 1, cut], r4_sem.at[z, step - 1, cut],
                      {"grp": g, "ep": zs})

    def fourth_arrived(zs, step, cut):
        return remote(s2.at[zs, step - 1, cuts[cut]], r4.at[zs, step - 1, cuts[cut]],
                      s2_sem.at[zs, step - 1, cut], r4_sem.at[zs, step - 1, cut], core_peer)

    def second(k):
        zs = place(k)
        for cut, (low, high) in enumerate(spans):
            for step in range(1, n_x):
                xs = x_of(step)
                first_copy(zs, xs, cut).wait_recv()
                s2[zs, step - 1, low:high] = pair_sum(zs, xs, cut).astype(jnp.bfloat16)

                @pl.when(through(zs))
                def _():
                    fourth_copy(zs, step, cut).start()

                @pl.when(jnp.logical_not(through(zs)))
                def _():
                    second_copy(zs, step, cut).start()

    def late_second():
        for cut, (low, high) in enumerate(spans):
            for step in range(1, n_x):
                xs = x_of(step)
                first_copy(z, xs, cut).wait_recv()
                total = pair_sum(z, xs, cut)
                for end in (0, n_ep - 1):
                    fourth_arrived(end, step, cut).wait_recv()
                    total += r4[end, step - 1, low:high].astype(jnp.float32)
                s2[z, step - 1, low:high] = total.astype(jnp.bfloat16)
                second_copy(z, step, cut).start()

    def third(k):
        zs = place(k)
        for cut, (low, high) in enumerate(spans):
            first_copy(zs, x, cut).wait_recv()

            @pl.when(through(zs))
            def _():
                s3[zs, low:high] = pair_sum(zs, x, cut).astype(jnp.bfloat16)
                third_copy(zs, cut).start()

            @pl.when(jnp.logical_not(through(zs)))
            def _():
                total = pair_sum(zs, x, cut)
                for step in range(1, n_x):
                    second_copy(zs, step, cut).wait_recv()
                    total += r2[zs, step - 1, low:high].astype(jnp.float32)

                @pl.when(zs == z)
                def _():
                    mine[low:high] = total

                @pl.when(zs != z)
                def _():
                    s3[zs, low:high] = total.astype(jnp.bfloat16)
                    third_copy(zs, cut).start()

    for load in loads[:2 * slabs]:
        load.wait()
    each_near(z, start)
    ahead = jnp.where(sides >= 1, 2, 1)

    @pl.when(sides >= 1)
    def _():
        take(1)

    for load in loads[2 * slabs:]:
        load.wait()

    def turn(k, carry):
        zs = place(k)

        def column(i, carry):
            xs = x_of(i)

            @pl.when(i == 1)
            def _():
                @pl.when(k + ahead < n_ep)
                def _():
                    take(k + ahead)

            @pl.when(i >= 1)
            def _():
                far_arrived(zs, xs)
                each_far(zs, xs, start)
                rest_arrived(zs, xs)
                to_core(zs, xs).start()

            arrived(zs, xs, other_c)
            compute(zs, xs)
            for cut in range(len(spans)):
                first_copy(zs, xs, cut).start()
            return carry

        lax.fori_loop(0, n_x, column, 0)

        @pl.when(jnp.logical_and(k >= 2, jnp.logical_not(late(k - 2))))
        def _():
            third(k - 2)

        @pl.when(jnp.logical_not(late(k)))
        def _():
            second(k)

        return carry

    lax.fori_loop(0, n_ep, turn, 0)
    third(n_ep - 2)
    third(n_ep - 1)

    @pl.when(late(0))
    def _():
        late_second()
        third(0)

    for cut, (low, high) in enumerate(spans):
        total = mine[low:high]
        for step in range(1, n_ep):
            zs = lax.rem(z + step, n_ep)
            third_arrived(zs, cut).wait_recv()
            total += r3[zs, low:high].astype(jnp.float32)
        for s in range(slabs):
            if low <= s * rows and (s + 1) * rows <= high:
                at = s * rows - low
                out_ref[:, s * LANES:(s + 1) * LANES] = total[at:at + rows].astype(jnp.bfloat16)
        if high > mark:
            for k in range(ids_ref.shape[0]):
                picked = jnp.where(item == ids_ref[k:k + 1, :], total[mark - low:], 0.0)
                gw_ref[k:k + 1, :] = jnp.sum(picked, axis=0, keepdims=True).astype(jnp.bfloat16)

    def drain(zs, carry):
        each_near(zs, wait_send)
        for step in range(1, n_x):
            each_far(zs, x_of(step), wait_send)
            to_core(zs, x_of(step)).wait_send()
        for cut in range(len(spans)):
            first_copy(zs, x, cut).wait_send()
            for step in range(1, n_x):
                first_copy(zs, x_of(step), cut).wait_send()
                second_copy(zs, step, cut).wait_send()

            @pl.when(zs != z)
            def _():
                third_copy(zs, cut).wait_send()

        return carry

    lax.fori_loop(0, n_ep, drain, 0)


def gather_plan(tokens, cotangent, expert_ids, route_weights, w_gate, w_up, w_down):
    n_grp, n_ep = lax.axis_size("grp"), lax.axis_size("ep")
    n_x, named = n_grp // CORES, gw_rows(n_grp * n_ep)
    rows, width = tokens.shape
    mark = rows * (width // LANES)
    sent, back = 2 * mark + 2 * named, mark + named
    any_ref, vmem = pl.BlockSpec(memory_space=pl.ANY), pl.BlockSpec(memory_space=pltpu.VMEM)
    bf16, dma = jnp.bfloat16, pltpu.SemaphoreType.DMA
    grad_tokens, grad_weights = pl.pallas_call(
        functools.partial(gather_kernel, n_grp, n_ep),
        out_shape=(
            jax.ShapeDtypeStruct((rows, width), bf16),
            jax.ShapeDtypeStruct(expert_ids.shape[::-1], bf16),
        ),
        in_specs=[any_ref, any_ref, vmem, vmem, any_ref, any_ref, any_ref],
        out_specs=(vmem, vmem),
        scratch_shapes=[
            pltpu.VMEM((n_ep, n_x, CORES, sent, LANES), bf16),
            pltpu.VMEM((n_ep, n_x, CORES, back, LANES), bf16),
            pltpu.VMEM((n_ep, n_x, back, LANES), bf16),
            pltpu.VMEM((n_ep, n_x - 1, back, LANES), bf16),
            pltpu.VMEM((n_ep, n_x - 1, back, LANES), bf16),
            pltpu.VMEM((n_ep, back, LANES), bf16),
            pltpu.VMEM((n_ep, back, LANES), bf16),
            pltpu.VMEM((n_ep, n_x - 1, back, LANES), bf16),
            pltpu.VMEM((back, LANES), jnp.float32),
            pltpu.VMEM(w_gate.shape[1:], bf16),
            pltpu.VMEM(w_up.shape[1:], bf16),
            pltpu.VMEM(w_down.shape[1:], bf16),
            dma((2 * (width // LANES) + 3,)), dma((n_ep, 2)), dma((n_ep, n_x, 2)), dma((n_ep, n_x - 1)), dma((n_ep, n_x)),
            dma((n_ep, n_x, CORES)), dma((n_ep, n_x)),
            dma((n_ep, n_x, CUTS)), dma((n_ep, n_x, CUTS)),
            dma((n_ep, n_x - 1, CUTS)), dma((n_ep, n_x - 1, CUTS)),
            dma((n_ep, CUTS)), dma((n_ep, CUTS)), dma((n_ep, n_x - 1, CUTS)),
        ],
        compiler_params=pltpu.CompilerParams(
            collective_id=0, has_side_effects=True, vmem_limit_bytes=VMEM_ROOM
        ),
    )(tokens, cotangent, expert_ids.T, route_weights.T, w_gate, w_up, w_down)
    return grad_tokens, grad_weights.T


def on_device(tokens, cotangent, expert_ids, route_weights, w_gate, w_up, w_down):
    n_grp, n_ep = lax.axis_size("grp"), lax.axis_size("ep")
    rows, width = tokens.shape
    gathered = n_grp * n_ep * rows * 2 * (4 * width) * 2
    fits = gathered <= VMEM_ROOM and rows == LANES and width % LANES == 0
    plan = gather_plan if fits and n_grp > CORES else dispatch_plan
    return plan(tokens, cotangent, expert_ids, route_weights, w_gate, w_up, w_down)


def solution(mesh):
    in_specs = (
        P(("parts", "grp", "ep"), None),
        P(("parts", "grp", "ep"), None),
        P(("parts", "grp", "ep"), None),
        P(("parts", "grp", "ep"), None),
        P(("grp", "ep"), None, None),
        P(("grp", "ep"), None, None),
        P(("grp", "ep"), None, None),
    )
    out_specs = (P(("parts", "grp", "ep"), None), P(("parts", "grp", "ep"), None))
    return jax.shard_map(
        on_device, mesh=mesh, in_specs=in_specs, out_specs=out_specs, check_vma=False
    )
```

```python
import functools

import jax
import jax.numpy as jnp
from jax import lax
from jax.experimental import pallas as pl
from jax.experimental.pallas import tpu as pltpu
from jax.sharding import PartitionSpec as P

LANES = 128
CORES = 2
VMEM_ROOM = 56 * 1024 * 1024


def expert_grads(rows_in, grads_in, w_gate, w_up, w_down):
    contract = (((1,), (1,)), ((), ()))
    gate_pre = jnp.dot(rows_in, w_gate, preferred_element_type=jnp.float32)
    up_pre = jnp.dot(rows_in, w_up, preferred_element_type=jnp.float32)
    hidden_grad = lax.dot_general(grads_in, w_down, contract, preferred_element_type=jnp.float32)
    sigmoid_gate = jax.nn.sigmoid(gate_pre)
    activation = gate_pre * sigmoid_gate
    hidden = activation * up_pre
    weight_grad = jnp.sum(hidden_grad * hidden, axis=-1).astype(jnp.bfloat16)
    grad_up = (hidden_grad * activation).astype(jnp.bfloat16)
    grad_gate = (
        hidden_grad * up_pre * sigmoid_gate * (1.0 + gate_pre * (1.0 - sigmoid_gate))
    ).astype(jnp.bfloat16)
    row_terms = (
        lax.dot_general(grad_gate, w_gate, contract, preferred_element_type=jnp.float32)
        + lax.dot_general(grad_up, w_up, contract, preferred_element_type=jnp.float32)
    ).astype(jnp.bfloat16)
    return (row_terms, weight_grad)


def slot_plan(routes, experts, capacity):
    tok_rows, top_count = routes.shape
    flat_ids = routes.reshape(-1)
    pad_pair = flat_ids.shape[0]
    pair_ids = jnp.arange(pad_pair, dtype=jnp.int32)
    sort_order = jnp.argsort(flat_ids, stable=True)
    sorted_ids = flat_ids[sort_order]
    onehot = (flat_ids[:, None] == jnp.arange(experts, dtype=jnp.int32)[None, :]).astype(jnp.int32)
    counts = jnp.sum(onehot, axis=0)
    earlier = jnp.tri(experts, k=-1, dtype=jnp.int32)
    starts = jnp.sum(earlier * counts[None, :], axis=1)
    sorted_rank = pair_ids - starts[sorted_ids]
    sorted_slot = sorted_ids * capacity + sorted_rank
    slot_of_pair = jnp.zeros((pad_pair,), jnp.int32).at[sort_order].set(sorted_slot)
    slot_pair = jnp.full((experts * capacity,), pad_pair, jnp.int32).at[sorted_slot].set(sort_order)
    slot_token = jnp.where(slot_pair < pad_pair, slot_pair // top_count, tok_rows)
    return (slot_of_pair, slot_token, slot_pair)


def place_rows(source_rows, slot_token):
    padded = jnp.concatenate(
        [source_rows, jnp.zeros((1, source_rows.shape[1]), source_rows.dtype)], 0
    )
    return padded[slot_token]


def dispatch_plan(tokens, cotangent, expert_ids, route_weights, w_gate, w_up, w_down):
    group_count = lax.axis_size("grp")
    lane_count = lax.axis_size("ep")
    experts = group_count * lane_count
    tok_rows, top_count = expert_ids.shape
    model_width = tokens.shape[1]
    capacity = 2 * tok_rows * top_count // experts
    slot_of_pair, slot_token, unused_pairs = slot_plan(expert_ids, experts, capacity)
    send_rows = place_rows(tokens, slot_token).reshape(
        group_count, lane_count, capacity, model_width
    )
    send_grads = place_rows(cotangent, slot_token).reshape(
        group_count, lane_count, capacity, model_width
    )
    send_rows, send_grads = (
        lax.all_to_all(send_rows, "grp", split_axis=0, concat_axis=0, tiled=True),
        lax.all_to_all(send_grads, "grp", split_axis=0, concat_axis=0, tiled=True),
    )
    rows_in = lax.all_to_all(send_rows, "ep", split_axis=1, concat_axis=1, tiled=True)
    grads_in = lax.all_to_all(send_grads, "ep", split_axis=1, concat_axis=1, tiled=True)
    leading = rows_in.shape[:3]
    row_terms, weight_grad = expert_grads(
        rows_in.reshape(-1, model_width),
        grads_in.reshape(-1, model_width),
        w_gate[0],
        w_up[0],
        w_down[0],
    )
    row_terms = row_terms.reshape(leading + (model_width,))
    weight_grad = weight_grad.reshape(leading)
    row_terms, weight_grad = (
        lax.all_to_all(row_terms, "ep", split_axis=1, concat_axis=1, tiled=True),
        lax.all_to_all(weight_grad, "ep", split_axis=1, concat_axis=1, tiled=True),
    )
    row_terms, weight_grad = (
        lax.all_to_all(row_terms, "grp", split_axis=0, concat_axis=0, tiled=True),
        lax.all_to_all(weight_grad, "grp", split_axis=0, concat_axis=0, tiled=True),
    )
    row_terms = row_terms.reshape(experts * capacity, model_width)
    weight_grad = weight_grad.reshape(experts * capacity)
    picked = row_terms[slot_of_pair].reshape(tok_rows, top_count, model_width)
    grad_tokens = jnp.sum(route_weights[:, :, None] * picked.astype(jnp.float32), axis=1)
    grad_weights = weight_grad[slot_of_pair].reshape(tok_rows, top_count)
    return (grad_tokens.astype(jnp.bfloat16), grad_weights)


CUTS = 2
PIECES = 4
QUARTERS = 4


def gw_rows(experts):
    return -(-experts // 16) * 16


def task_list(n_ep):
    tasks = []
    for k in range(n_ep):
        tasks += [(k, 0, 0), (k, 0, 1)]
        if k == 1:
            tasks.append((0, 1, 0))
        if k >= 1:
            tasks.append((k, 1, 0))
    return tasks + [(k, 1, 1) for k in reversed(range(n_ep))]


def pick(index, values):
    chosen = jnp.int32(values[0])
    for at in range(1, len(values)):
        if values[at] != values[at - 1]:
            chosen = jnp.where(index >= at, jnp.int32(values[at]), chosen)
    return chosen


def swap_kernel(
    n_grp, n_ep, tok_hbm, cot_hbm, ids_ref, route_ref, wg_hbm, wu_hbm, wd_hbm,
    out_ref, gw_ref,
    tok, cot, rts, wgu, wdn, acc, sums, parts, parts_g, r1, r1_g, sent, sent_g, up, up_g, pair_g,
    load_sem, got_sem, z_sem, c_sem, wx_s, wx_r, wy_s, wy_r,
    s1_sem, r1_sem, s2_sem, r2_sem,
):
    rows, width = out_ref.shape
    unit = wgu.shape[3] // 2
    named = gw_rows(n_grp * n_ep)
    p, g, z = lax.axis_index("parts"), lax.axis_index("grp"), lax.axis_index("ep")
    x, c = g // CORES, g % CORES
    other_c = 1 - c
    experts = (g * n_ep + z, ((1 - x) * CORES + c) * n_ep + z)
    core_peer = {"parts": p, "grp": x * CORES + other_c, "ep": z}
    x_peer = {"parts": p, "grp": (1 - x) * CORES + c, "ep": z}
    y_peer = {"parts": 1 - p, "grp": g, "ep": z}

    def z_peer(step):
        return {"parts": p, "grp": g, "ep": z + step}

    loads = [
        pltpu.make_async_copy(tok_hbm, tok.at[z, c], load_sem.at[0]),
        pltpu.make_async_copy(cot_hbm, cot.at[z, c], load_sem.at[1]),
    ]
    for q in range(QUARTERS):
        span = pl.ds(q * unit, unit)
        for i, (source, target) in enumerate((
            (wg_hbm.at[0, :, span], wgu.at[0, q, :, pl.ds(0, unit)]),
            (wu_hbm.at[0, :, span], wgu.at[0, q, :, pl.ds(unit, unit)]),
            (wd_hbm.at[0, span, :], wdn.at[0, q]),
        )):
            loads.append(pltpu.make_async_copy(source, target, load_sem.at[2 + 3 * q + i]))
    for load in loads:
        load.start()

    item = lax.broadcasted_iota(jnp.int32, (named, LANES), 0)
    routed = jnp.zeros((named, LANES), jnp.float32)
    for k in range(ids_ref.shape[0]):
        routed += jnp.where(item == ids_ref[k:k + 1, :], route_ref[k:k + 1, :], 0.0)
    high = routed.astype(jnp.bfloat16)
    rts[z, c, 0:named, :] = high
    rts[z, c, named:2 * named, :] = (routed - high.astype(jnp.float32)).astype(jnp.bfloat16)

    barrier = pltpu.get_barrier_semaphore()

    def greet(peer):
        pl.semaphore_signal(barrier, inc=1, device_id=peer, device_id_type=pl.DeviceIdType.MESH)

    for peer in (core_peer, x_peer, y_peer):
        greet(peer)

    @pl.when(z > 0)
    def _():
        greet(z_peer(-1))

    @pl.when(z < n_ep - 1)
    def _():
        greet(z_peer(1))

    acc[...] = jnp.zeros_like(acc)
    sums[...] = jnp.zeros_like(sums)
    for load in loads:
        load.wait()
    near = jnp.where(z > 0, 1, 0) + jnp.where(z < n_ep - 1, 1, 0)
    pl.semaphore_wait(barrier, 3 + near)

    def remote(source, target, send, recv, peer):
        return pltpu.make_async_remote_copy(
            src_ref=source, dst_ref=target, send_sem=send, recv_sem=recv,
            device_id=peer, device_id_type=pl.DeviceIdType.MESH,
        )

    sides = jnp.minimum(z, n_ep - 1 - z)

    def place(k):
        near_k = jnp.where(k % 2 == 1, z - (k + 1) // 2, z + k // 2)
        far_k = jnp.where(2 * z < n_ep - 1, k, n_ep - 1 - k)
        return jnp.where(k <= 2 * sides, near_k, far_k)

    kinds = (tok, rts, cot)

    def along_z(kind, zs, step):
        block = kinds[kind].at[zs, c]
        return remote(block, block, z_sem.at[kind, zs, (step + 1) // 2], got_sem.at[kind, zs, c],
                      z_peer(step))

    def to_core(kind, zs):
        block = kinds[kind].at[zs, c]
        return remote(block, block, c_sem.at[kind, zs], got_sem.at[kind, zs, c], core_peer)

    def arrived(kind, zs, cs):
        block = kinds[kind].at[zs, cs]
        remote(block, block, c_sem.at[kind, zs], got_sem.at[kind, zs, cs], core_peer).wait_recv()

    def each_send(kind, zs, act):
        @pl.when(jnp.logical_and(zs <= z, z < n_ep - 1))
        def _():
            act(along_z(kind, zs, 1))

        @pl.when(jnp.logical_and(zs >= z, z > 0))
        def _():
            act(along_z(kind, zs, -1))

        act(to_core(kind, zs))

    def start(copy):
        copy.start()

    def wait_send(copy):
        copy.wait_send()

    def take(k, group):
        zs = place(k)
        for kind in group:
            arrived(kind, zs, c)
            each_send(kind, zs, start)

    first, last = (0, 1), (2,)

    def takes(n, group):
        @pl.when(sides == 0)
        def _():
            take(n, group)

        @pl.when(sides > 0)
        def _():
            if n == 1:
                take(1, group)
            if n + 1 < n_ep:
                take(n + 1, group)

    def piece(e, q, n):
        if n < PIECES:
            span = width // PIECES
            return wgu.at[e, q, pl.ds(n * span, span)]
        span = unit // 2
        return wdn.at[e, q, pl.ds((n - PIECES) * span, span)]

    per = PIECES + 2

    def over_x(j, n):
        q = 2 * j + p
        return remote(piece(0, q, n), piece(1, q, n), wx_s.at[j, n], wx_r.at[j, n], x_peer)

    def over_y(j, n):
        q = 2 * j + p
        return remote(piece(1, q, n), piece(1, q, n), wy_s.at[j, n], wy_r.at[j, n], y_peer)

    def relay(i):
        over_x(i // per, i % per).wait_recv()
        over_y(i // per, i % per).start()

    contract = (((1,), (1,)), ((), ()))
    both = CORES * rows

    def scale_of(zs, expert):
        columns = []
        for cs in range(CORES):
            routes = rts[zs, cs, 0:named, :].astype(jnp.float32)
            routes += rts[zs, cs, named:2 * named, :].astype(jnp.float32)
            weight = jnp.sum(jnp.where(item == expert, routes, 0.0), axis=0, keepdims=True)
            columns.append(jnp.broadcast_to(weight, (rows, LANES)).T)
        return jnp.concatenate(columns, axis=0)

    def compute(zs, e, j):
        expert = jnp.where(e == 0, experts[0], experts[1])
        scale = scale_of(zs, expert)
        rows_in = tok[zs].reshape(both, width)
        grads_in = cot[zs].reshape(both, width)
        w_down = jnp.concatenate([wdn[e, 2 * j], wdn[e, 2 * j + 1]], axis=0)
        hidden_grads = lax.dot_general(grads_in, w_down, contract, preferred_element_type=jnp.float32)
        lane_sums = jnp.zeros((both, LANES), jnp.float32)
        grads = []
        for h in range(2):
            pre = jnp.dot(rows_in, wgu[e, 2 * j + h], preferred_element_type=jnp.float32)
            gate_pre, up_pre = pre[:, :unit], pre[:, unit:]
            hidden_grad = hidden_grads[:, h * unit:(h + 1) * unit]
            sigmoid_gate = 1.0 / (1.0 + jnp.exp(-gate_pre))
            activation = gate_pre * sigmoid_gate
            lane_sums += hidden_grad * (activation * up_pre)
            hidden_grad = hidden_grad * scale
            grads.append((hidden_grad * up_pre * sigmoid_gate
                          * (1.0 + gate_pre * (1.0 - sigmoid_gate))).astype(jnp.bfloat16))
            grads.append((hidden_grad * activation).astype(jnp.bfloat16))
        sums[zs, e] += lane_sums
        terms = lax.dot_general(jnp.concatenate(grads[:2], axis=1), wgu[e, 2 * j], contract,
                                preferred_element_type=jnp.float32)
        terms += lax.dot_general(jnp.concatenate(grads[2:], axis=1), wgu[e, 2 * j + 1], contract,
                                 preferred_element_type=jnp.float32)
        acc[zs] += terms.reshape(CORES, rows, width)

    cut_rows = rows // CUTS
    cuts = [pl.ds(i * cut_rows, cut_rows) for i in range(CUTS)]

    def first_copy(zs, i):
        if i < CUTS:
            source, target = parts.at[zs, cuts[i]], r1.at[zs, cuts[i]]
        else:
            source, target = parts_g.at[zs], r1_g.at[zs]
        return remote(source, target, s1_sem.at[zs, i], r1_sem.at[zs, i], core_peer)

    def second_copy(zs, step, i):
        way = (step + 1) // 2
        if i < CUTS:
            source, target = sent.at[zs, cuts[i]], up.at[way, zs, cuts[i]]
        else:
            source, target = sent_g.at[zs], up_g.at[way, zs]
        return remote(source, target, s2_sem.at[zs, i], r2_sem.at[way, zs, i], z_peer(step))

    def finish(zs):
        parts[zs] = acc[zs, other_c].astype(jnp.bfloat16)
        for i in range(CUTS):
            first_copy(zs, i).start()
        for cs in range(CORES):
            here = slice(cs * rows, (cs + 1) * rows)
            found = jnp.zeros((named, LANES), jnp.float32)
            for e in range(2):
                weight_grad = jnp.sum(sums[zs, e, here, :].T, axis=0, keepdims=True)
                found += jnp.where(item == experts[e], weight_grad, 0.0)
            pair_g[zs, cs] = found.astype(jnp.bfloat16)
        parts_g[zs] = pair_g[zs, other_c]
        first_copy(zs, CUTS).start()

    def summed(zs, ways, i):
        first_copy(zs, i).wait_recv()
        for way in ways:
            second_copy(zs, 2 * way - 1, i).wait_recv()
        if i < CUTS:
            total = acc[zs, c, cuts[i]] + r1[zs, cuts[i]].astype(jnp.float32)
            for way in ways:
                total += up[way, zs, cuts[i]].astype(jnp.float32)
            return total
        total = pair_g[zs, c].astype(jnp.float32) + r1_g[zs].astype(jnp.float32)
        for way in ways:
            total += up_g[way, zs].astype(jnp.float32)
        return total

    def pass_on(zs, ways, step):
        for i in range(CUTS):
            sent[zs, cuts[i]] = summed(zs, ways, i).astype(jnp.bfloat16)
            second_copy(zs, step, i).start()
        sent_g[zs] = summed(zs, ways, CUTS).astype(jnp.bfloat16)
        second_copy(zs, step, CUTS).start()

    def send_back(k, inner):
        zs = place(k)

        @pl.when(zs > z)
        def _():
            pass_on(zs, [1] if inner else [], 1)

        @pl.when(zs < z)
        def _():
            pass_on(zs, [0] if inner else [], -1)

    def conclude(ways):
        for i in range(CUTS):
            out_ref[cuts[i], :] = summed(z, ways, i).astype(jnp.bfloat16)
        total = summed(z, ways, CUTS)
        for k in range(ids_ref.shape[0]):
            picked = jnp.where(item == ids_ref[k:k + 1, :], total, 0.0)
            gw_ref[k:k + 1, :] = jnp.sum(picked, axis=0, keepdims=True).astype(jnp.bfloat16)

    for j in range(2):
        for n in range(per):
            over_x(j, n).start()
    for kind in (0, 1, 2):
        each_send(kind, z, start)
    for kind in (0, 1, 2):
        arrived(kind, z, other_c)

    def block_here(k):
        for kind in (0, 1, 2):
            arrived(kind, place(k), other_c)

    def relays(low, high):
        for i in range(low, high):
            relay(i)

    def half_here(j):
        for n in range(per):
            over_y(j, n).wait_recv()

    tasks = task_list(n_ep)
    tail = len(tasks) - n_ep
    events = {task: [] for task in range(len(tasks))}

    def at(task, act, *args):
        events[tasks.index(task)].append((act, args))

    def relays_to(task, high):
        low = relayed[0]
        relayed[0] = high
        at(task, relays, low, high)

    relayed = [0]
    relays_to((0, 0, 1), 1)
    relays_to((1, 0, 0), 2)
    at((1, 0, 0), takes, 1, first)
    relays_to((1, 0, 0), 3)
    at((1, 0, 0), takes, 1, last)
    relays_to((1, 0, 0), 4)
    at((1, 0, 0), block_here, 1)
    relays_to((0, 1, 0), 6)
    if n_ep > 2:
        at((0, 1, 0), takes, 2, first)
    relays_to((0, 1, 0), 7)
    at((0, 1, 0), half_here, 0)
    for k in range(2, n_ep):
        at((k, 0, 0), takes, k, last)
        relays_to((k, 0, 0), min(2 * per, 4 * k))
        if k == n_ep - 1:
            relays_to((k, 0, 0), 2 * per)
        at((k, 0, 0), block_here, k)
        if k + 1 < n_ep:
            relays_to((k, 1, 0), min(2 * per, 4 * k + 2))
            at((k, 1, 0), takes, k + 1, first)
    relays_to((n_ep - 1, 1, 1), 2 * per)
    at((n_ep - 1, 1, 1), half_here, 1)

    def turn(i, carry):
        for index, acts in events.items():
            if acts:
                @pl.when(i == index)
                def _(acts=acts):
                    for act, args in acts:
                        act(*args)

        k, e, j = (pick(i, [task[field] for task in tasks]) for field in range(3))
        compute(place(k), e, j)

        @pl.when(i >= tail)
        def _():
            finish(place(k))

        @pl.when(jnp.logical_and(i > tail, sides == 0))
        def _():
            send_back(k + 1, False)

        return carry

    lax.fori_loop(0, len(tasks), turn, 0)

    @pl.when(sides > 0)
    def _():
        for k in [n_ep - 1] + list(range(1, n_ep - 1)):
            send_back(k, True)

    @pl.when(sides > 0)
    def _():
        conclude([1, 0])

    @pl.when(z == 0)
    def _():
        conclude([0])

    @pl.when(z == n_ep - 1)
    def _():
        conclude([1])

    def drain(zs, carry):
        for kind in (0, 1, 2):
            each_send(kind, zs, wait_send)
        for i in range(CUTS + 1):
            first_copy(zs, i).wait_send()

        @pl.when(zs != z)
        def _():
            for i in range(CUTS + 1):
                second_copy(zs, 1, i).wait_send()

        return carry

    lax.fori_loop(0, n_ep, drain, 0)
    for j in range(2):
        for n in range(per):
            over_x(j, n).wait_send()
            over_y(j, n).wait_send()


def swap_plan(tokens, cotangent, expert_ids, route_weights, w_gate, w_up, w_down):
    n_grp, n_ep = lax.axis_size("grp"), lax.axis_size("ep")
    named = gw_rows(n_grp * n_ep)
    rows, width = tokens.shape
    unit = w_gate.shape[2] // QUARTERS
    any_ref, vmem = pl.BlockSpec(memory_space=pl.ANY), pl.BlockSpec(memory_space=pltpu.VMEM)
    bf16, f32, dma = jnp.bfloat16, jnp.float32, pltpu.SemaphoreType.DMA
    per = PIECES + 2
    grad_tokens, grad_weights = pl.pallas_call(
        functools.partial(swap_kernel, n_grp, n_ep),
        out_shape=(
            jax.ShapeDtypeStruct((rows, width), bf16),
            jax.ShapeDtypeStruct(expert_ids.shape[::-1], bf16),
        ),
        in_specs=[any_ref, any_ref, vmem, vmem, any_ref, any_ref, any_ref],
        out_specs=(vmem, vmem),
        scratch_shapes=[
            pltpu.VMEM((n_ep, CORES, rows, width), bf16),
            pltpu.VMEM((n_ep, CORES, rows, width), bf16),
            pltpu.VMEM((n_ep, CORES, 2 * named, LANES), bf16),
            pltpu.VMEM((2, QUARTERS, width, 2 * unit), bf16),
            pltpu.VMEM((2, QUARTERS, unit, width), bf16),
            pltpu.VMEM((n_ep, CORES, rows, width), f32),
            pltpu.VMEM((n_ep, 2, CORES * rows, LANES), f32),
            pltpu.VMEM((n_ep, rows, width), bf16),
            pltpu.VMEM((n_ep, named, LANES), bf16),
            pltpu.VMEM((n_ep, rows, width), bf16),
            pltpu.VMEM((n_ep, named, LANES), bf16),
            pltpu.VMEM((n_ep, rows, width), bf16),
            pltpu.VMEM((n_ep, named, LANES), bf16),
            pltpu.VMEM((2, n_ep, rows, width), bf16),
            pltpu.VMEM((2, n_ep, named, LANES), bf16),
            pltpu.VMEM((n_ep, CORES, named, LANES), bf16),
            dma((2 + 3 * QUARTERS,)), dma((3, n_ep, CORES)), dma((3, n_ep, 2)), dma((3, n_ep)),
            dma((2, per)), dma((2, per)), dma((2, per)), dma((2, per)),
            dma((n_ep, CUTS + 1)), dma((n_ep, CUTS + 1)),
            dma((n_ep, CUTS + 1)), dma((2, n_ep, CUTS + 1)),
        ],
        compiler_params=pltpu.CompilerParams(
            collective_id=0, has_side_effects=True, vmem_limit_bytes=VMEM_ROOM
        ),
    )(tokens, cotangent, expert_ids.T, route_weights.T, w_gate, w_up, w_down)
    return grad_tokens, grad_weights.T


def on_device(tokens, cotangent, expert_ids, route_weights, w_gate, w_up, w_down):
    n_grp, n_ep = lax.axis_size("grp"), lax.axis_size("ep")
    rows, width = tokens.shape
    swaps = lax.axis_size("parts") == 2 and n_grp == 2 * CORES and 2 <= n_ep <= 4
    fits = rows == LANES and width % LANES == 0 and w_gate.shape[2] == QUARTERS * LANES
    held = 2 * (w_gate.size + w_up.size + w_down.size) * 2 + n_ep * rows * width * 28
    plan = swap_plan if swaps and fits and held <= VMEM_ROOM else dispatch_plan
    return plan(tokens, cotangent, expert_ids, route_weights, w_gate, w_up, w_down)


def solution(mesh):
    in_specs = (
        P(("parts", "grp", "ep"), None),
        P(("parts", "grp", "ep"), None),
        P(("parts", "grp", "ep"), None),
        P(("parts", "grp", "ep"), None),
        P(("grp", "ep"), None, None),
        P(("grp", "ep"), None, None),
        P(("grp", "ep"), None, None),
    )
    out_specs = (P(("parts", "grp", "ep"), None), P(("parts", "grp", "ep"), None))
    return jax.shard_map(
        on_device, mesh=mesh, in_specs=in_specs, out_specs=out_specs, check_vma=False
    )
```

```python
import functools

import jax
import jax.numpy as jnp
from jax import lax
from jax.experimental import pallas as pl
from jax.experimental.pallas import tpu as pltpu
from jax.sharding import PartitionSpec as P

LANES = 128
CORES = 2
VMEM_ROOM = 56 * 1024 * 1024


def expert_grads(rows_in, grads_in, w_gate, w_up, w_down):
    contract = (((1,), (1,)), ((), ()))
    gate_pre = jnp.dot(rows_in, w_gate, preferred_element_type=jnp.float32)
    up_pre = jnp.dot(rows_in, w_up, preferred_element_type=jnp.float32)
    hidden_grad = lax.dot_general(grads_in, w_down, contract, preferred_element_type=jnp.float32)
    sigmoid_gate = jax.nn.sigmoid(gate_pre)
    activation = gate_pre * sigmoid_gate
    hidden = activation * up_pre
    weight_grad = jnp.sum(hidden_grad * hidden, axis=-1).astype(jnp.bfloat16)
    grad_up = (hidden_grad * activation).astype(jnp.bfloat16)
    grad_gate = (
        hidden_grad * up_pre * sigmoid_gate * (1.0 + gate_pre * (1.0 - sigmoid_gate))
    ).astype(jnp.bfloat16)
    row_terms = (
        lax.dot_general(grad_gate, w_gate, contract, preferred_element_type=jnp.float32)
        + lax.dot_general(grad_up, w_up, contract, preferred_element_type=jnp.float32)
    ).astype(jnp.bfloat16)
    return (row_terms, weight_grad)


def slot_plan(routes, experts, capacity):
    tok_rows, top_count = routes.shape
    flat_ids = routes.reshape(-1)
    pad_pair = flat_ids.shape[0]
    pair_ids = jnp.arange(pad_pair, dtype=jnp.int32)
    sort_order = jnp.argsort(flat_ids, stable=True)
    sorted_ids = flat_ids[sort_order]
    onehot = (flat_ids[:, None] == jnp.arange(experts, dtype=jnp.int32)[None, :]).astype(jnp.int32)
    counts = jnp.sum(onehot, axis=0)
    earlier = jnp.tri(experts, k=-1, dtype=jnp.int32)
    starts = jnp.sum(earlier * counts[None, :], axis=1)
    sorted_rank = pair_ids - starts[sorted_ids]
    sorted_slot = sorted_ids * capacity + sorted_rank
    slot_of_pair = jnp.zeros((pad_pair,), jnp.int32).at[sort_order].set(sorted_slot)
    slot_pair = jnp.full((experts * capacity,), pad_pair, jnp.int32).at[sorted_slot].set(sort_order)
    slot_token = jnp.where(slot_pair < pad_pair, slot_pair // top_count, tok_rows)
    return (slot_of_pair, slot_token, slot_pair)


def place_rows(source_rows, slot_token):
    padded = jnp.concatenate(
        [source_rows, jnp.zeros((1, source_rows.shape[1]), source_rows.dtype)], 0
    )
    return padded[slot_token]


def dispatch_plan(tokens, cotangent, expert_ids, route_weights, w_gate, w_up, w_down):
    group_count = lax.axis_size("grp")
    lane_count = lax.axis_size("ep")
    experts = group_count * lane_count
    tok_rows, top_count = expert_ids.shape
    model_width = tokens.shape[1]
    capacity = 2 * tok_rows * top_count // experts
    slot_of_pair, slot_token, unused_pairs = slot_plan(expert_ids, experts, capacity)
    send_rows = place_rows(tokens, slot_token).reshape(
        group_count, lane_count, capacity, model_width
    )
    send_grads = place_rows(cotangent, slot_token).reshape(
        group_count, lane_count, capacity, model_width
    )
    send_rows, send_grads = (
        lax.all_to_all(send_rows, "grp", split_axis=0, concat_axis=0, tiled=True),
        lax.all_to_all(send_grads, "grp", split_axis=0, concat_axis=0, tiled=True),
    )
    rows_in = lax.all_to_all(send_rows, "ep", split_axis=1, concat_axis=1, tiled=True)
    grads_in = lax.all_to_all(send_grads, "ep", split_axis=1, concat_axis=1, tiled=True)
    leading = rows_in.shape[:3]
    row_terms, weight_grad = expert_grads(
        rows_in.reshape(-1, model_width),
        grads_in.reshape(-1, model_width),
        w_gate[0],
        w_up[0],
        w_down[0],
    )
    row_terms = row_terms.reshape(leading + (model_width,))
    weight_grad = weight_grad.reshape(leading)
    row_terms, weight_grad = (
        lax.all_to_all(row_terms, "ep", split_axis=1, concat_axis=1, tiled=True),
        lax.all_to_all(weight_grad, "ep", split_axis=1, concat_axis=1, tiled=True),
    )
    row_terms, weight_grad = (
        lax.all_to_all(row_terms, "grp", split_axis=0, concat_axis=0, tiled=True),
        lax.all_to_all(weight_grad, "grp", split_axis=0, concat_axis=0, tiled=True),
    )
    row_terms = row_terms.reshape(experts * capacity, model_width)
    weight_grad = weight_grad.reshape(experts * capacity)
    picked = row_terms[slot_of_pair].reshape(tok_rows, top_count, model_width)
    grad_tokens = jnp.sum(route_weights[:, :, None] * picked.astype(jnp.float32), axis=1)
    grad_weights = weight_grad[slot_of_pair].reshape(tok_rows, top_count)
    return (grad_tokens.astype(jnp.bfloat16), grad_weights)


CUTS = 2
PIECES = 4
QUARTERS = 4
KINDS = (0, 1, 2, 3)


def gw_rows(experts):
    return -(-experts // 16) * 16


def pick(index, values):
    chosen = jnp.int32(values[0])
    for at in range(1, len(values)):
        if values[at] != values[at - 1]:
            chosen = jnp.where(index >= at, jnp.int32(values[at]), chosen)
    return chosen


def swap_kernel(
    n_grp, n_ep, tok_hbm, cot_hbm, ids_ref, route_ref, wg_hbm, wu_hbm, wd_hbm,
    out_ref, gw_ref,
    tok, cot, rts, wgu, wdn, acc, sums, parts, parts_g, r1, r1_g, sent, sent_g, up, up_g, pair_g,
    load_sem, got_sem, z_sem, c_sem, wx_s, wx_r, wy_s, wy_r,
    s1_sem, r1_sem, s2_sem, r2_sem,
):
    rows, width = out_ref.shape
    unit = wgu.shape[3] // QUARTERS
    named = gw_rows(n_grp * n_ep)
    p, g, z = lax.axis_index("parts"), lax.axis_index("grp"), lax.axis_index("ep")
    x, c = g // CORES, g % CORES
    other_c = 1 - c
    experts = (g * n_ep + z, ((1 - x) * CORES + c) * n_ep + z)
    core_peer = {"parts": p, "grp": x * CORES + other_c, "ep": z}
    x_peer = {"parts": p, "grp": (1 - x) * CORES + c, "ep": z}
    y_peer = {"parts": 1 - p, "grp": g, "ep": z}

    def z_peer(step):
        return {"parts": p, "grp": g, "ep": z + step}

    loads = [
        pltpu.make_async_copy(tok_hbm, tok.at[z, c], load_sem.at[0]),
        pltpu.make_async_copy(cot_hbm, cot.at[z, c], load_sem.at[1]),
    ]
    for q in range(QUARTERS):
        span = pl.ds(q * unit, unit)
        for i, (source, target) in enumerate((
            (wg_hbm.at[0, :, span], wgu.at[0, q // 2, :, pl.ds(q % 2 * 2 * unit, unit)]),
            (wu_hbm.at[0, :, span], wgu.at[0, q // 2, :, pl.ds((q % 2 * 2 + 1) * unit, unit)]),
            (wd_hbm.at[0, span, :], wdn.at[0, q // 2, pl.ds(q % 2 * unit, unit)]),
        )):
            loads.append(pltpu.make_async_copy(source, target, load_sem.at[2 + 3 * q + i]))
    for load in loads:
        load.start()

    item = lax.broadcasted_iota(jnp.int32, (named, LANES), 0)
    routed = jnp.zeros((named, LANES), jnp.float32)
    for k in range(ids_ref.shape[0]):
        routed += jnp.where(item == ids_ref[k:k + 1, :], route_ref[k:k + 1, :], 0.0)
    high = routed.astype(jnp.bfloat16)
    rts[z, c, 0:named, :] = high
    rts[z, c, named:2 * named, :] = (routed - high.astype(jnp.float32)).astype(jnp.bfloat16)

    barrier = pltpu.get_barrier_semaphore()

    def greet(peer):
        pl.semaphore_signal(barrier, inc=1, device_id=peer, device_id_type=pl.DeviceIdType.MESH)

    for peer in (core_peer, x_peer, y_peer):
        greet(peer)

    @pl.when(z > 0)
    def _():
        greet(z_peer(-1))

    @pl.when(z < n_ep - 1)
    def _():
        greet(z_peer(1))

    acc[...] = jnp.zeros_like(acc)
    sums[...] = jnp.zeros_like(sums)
    for load in loads:
        load.wait()
    near = jnp.where(z > 0, 1, 0) + jnp.where(z < n_ep - 1, 1, 0)
    pl.semaphore_wait(barrier, 3 + near)

    def remote(source, target, send, recv, peer):
        return pltpu.make_async_remote_copy(
            src_ref=source, dst_ref=target, send_sem=send, recv_sem=recv,
            device_id=peer, device_id_type=pl.DeviceIdType.MESH,
        )

    sides = jnp.minimum(z, n_ep - 1 - z)

    low_half = 2 * z < n_ep - 1

    def place(k):
        step = jnp.where(k % 2 == 1, -((k + 1) // 2), k // 2)
        near_k = jnp.where(low_half, z + step, z - step)
        far_k = jnp.where(low_half, k, n_ep - 1 - k)
        return jnp.where(k <= 2 * sides, near_k, far_k)

    part = rows // 2

    def block(kind, zs, cs):
        if kind == 0:
            return tok.at[zs, cs]
        if kind == 1:
            return rts.at[zs, cs]
        return cot.at[zs, cs, pl.ds((kind - 2) * part, part)]

    def along_z(kind, zs, step):
        here = block(kind, zs, c)
        return remote(here, here, z_sem.at[kind, zs, (step + 1) // 2], got_sem.at[kind, zs, c],
                      z_peer(step))

    def to_core(kind, zs):
        here = block(kind, zs, c)
        return remote(here, here, c_sem.at[kind, zs], got_sem.at[kind, zs, c], core_peer)

    def arrived(kind, zs, cs):
        here = block(kind, zs, cs)
        remote(here, here, c_sem.at[kind, zs], got_sem.at[kind, zs, cs], core_peer).wait_recv()

    def each_z(kind, zs, act):
        @pl.when(jnp.logical_and(zs <= z, z < n_ep - 1))
        def _():
            act(along_z(kind, zs, 1))

        @pl.when(jnp.logical_and(zs >= z, z > 0))
        def _():
            act(along_z(kind, zs, -1))

    def start(copy):
        copy.start()

    def wait_send(copy):
        copy.wait_send()

    def take(k, *group):
        zs = place(k)
        for kind in group:
            arrived(kind, zs, c)
            each_z(kind, zs, start)
            to_core(kind, zs).start()

    def at_ends(act, *args):
        @pl.when(sides == 0)
        def _():
            act(*args)

    def inside(act, *args):
        @pl.when(sides > 0)
        def _():
            act(*args)

    per = PIECES + 2

    def piece(e, j, h, n):
        if n < PIECES:
            span = width // PIECES
            lanes = pl.ds(pl.multiple_of(h * 2 * unit, 2 * unit), 2 * unit)
            return wgu.at[e, j, pl.ds(n * span, span), lanes]
        span = unit // 2
        low = pl.multiple_of(h * unit + (n - PIECES) * span, span)
        return wdn.at[e, j, pl.ds(low, span)]

    crossing = [(j, p, n) for j in range(2) for n in range(per)] + [(1, 1 - p, per - 1)]
    relayed = 2 * per - 1

    def over_x(i):
        return remote(piece(0, *crossing[i]), piece(1, *crossing[i]), wx_s.at[i], wx_r.at[i], x_peer)

    def over_y(i):
        here = piece(1, *crossing[i])
        return remote(here, here, wy_s.at[i], wy_r.at[i], y_peer)

    def relay(i):
        over_x(i).wait_recv()
        over_y(i).start()

    contract = (((1,), (1,)), ((), ()))
    both = CORES * rows

    def scale_of(zs, expert):
        columns = []
        for cs in range(CORES):
            routes = rts[zs, cs, 0:named, :].astype(jnp.float32)
            routes += rts[zs, cs, named:2 * named, :].astype(jnp.float32)
            weight = jnp.sum(jnp.where(item == expert, routes, 0.0), axis=0, keepdims=True)
            columns.append(jnp.broadcast_to(weight, (rows, LANES)).T)
        return jnp.concatenate(columns, axis=0)

    def compute(zs, e, j):
        expert = jnp.where(e == 0, experts[0], experts[1])
        scale = scale_of(zs, expert)
        rows_in = tok[zs].reshape(both, width)
        grads_in = cot[zs].reshape(both, width)
        pres = jnp.dot(rows_in, wgu[e, j], preferred_element_type=jnp.float32)
        hidden_grads = lax.dot_general(grads_in, wdn[e, j], contract, preferred_element_type=jnp.float32)
        lane_sums = jnp.zeros((both, LANES), jnp.float32)
        grads = []
        for h in range(2):
            gate_pre = pres[:, 2 * h * unit:(2 * h + 1) * unit]
            up_pre = pres[:, (2 * h + 1) * unit:(2 * h + 2) * unit]
            hidden_grad = hidden_grads[:, h * unit:(h + 1) * unit]
            sigmoid_gate = 1.0 / (1.0 + jnp.exp(-gate_pre))
            activation = gate_pre * sigmoid_gate
            lane_sums += hidden_grad * (activation * up_pre)
            hidden_grad = hidden_grad * scale
            grads.append((hidden_grad * up_pre * sigmoid_gate
                          * (1.0 + gate_pre * (1.0 - sigmoid_gate))).astype(jnp.bfloat16))
            grads.append((hidden_grad * activation).astype(jnp.bfloat16))
        sums[zs, e] += lane_sums
        terms = lax.dot_general(jnp.concatenate(grads, axis=1), wgu[e, j], contract,
                                preferred_element_type=jnp.float32)
        acc[zs] += terms.reshape(CORES, rows, width)

    cut_rows = rows // CUTS
    cuts = [pl.ds(i * cut_rows, cut_rows) for i in range(CUTS)]

    def first_copy(zs, i):
        if i < CUTS:
            source, target = parts.at[zs, cuts[i]], r1.at[zs, cuts[i]]
        else:
            source, target = parts_g.at[zs], r1_g.at[zs]
        return remote(source, target, s1_sem.at[zs, i], r1_sem.at[zs, i], core_peer)

    def second_copy(zs, step, i):
        way = (step + 1) // 2
        if i < CUTS:
            source, target = sent.at[zs, cuts[i]], up.at[way, zs, cuts[i]]
        else:
            source, target = sent_g.at[zs], up_g.at[way, zs]
        return remote(source, target, s2_sem.at[zs, i], r2_sem.at[way, zs, i], z_peer(step))

    def finish(zs):
        parts[zs] = acc[zs, other_c].astype(jnp.bfloat16)
        for i in range(CUTS):
            first_copy(zs, i).start()
        for cs in range(CORES):
            here = slice(cs * rows, (cs + 1) * rows)
            found = jnp.zeros((named, LANES), jnp.float32)
            for e in range(2):
                weight_grad = jnp.sum(sums[zs, e, here, :].T, axis=0, keepdims=True)
                found += jnp.where(item == experts[e], weight_grad, 0.0)
            pair_g[zs, cs] = found.astype(jnp.bfloat16)
        parts_g[zs] = pair_g[zs, other_c]
        first_copy(zs, CUTS).start()

    def summed(zs, ways, i):
        first_copy(zs, i).wait_recv()
        for way in ways:
            second_copy(zs, 2 * way - 1, i).wait_recv()
        if i < CUTS:
            total = acc[zs, c, cuts[i]] + r1[zs, cuts[i]].astype(jnp.float32)
            for way in ways:
                total += up[way, zs, cuts[i]].astype(jnp.float32)
            return total
        total = pair_g[zs, c].astype(jnp.float32) + r1_g[zs].astype(jnp.float32)
        for way in ways:
            total += up_g[way, zs].astype(jnp.float32)
        return total

    def pass_on(zs, ways, step):
        for i in range(CUTS):
            sent[zs, cuts[i]] = summed(zs, ways, i).astype(jnp.bfloat16)
            second_copy(zs, step, i).start()
        sent_g[zs] = summed(zs, ways, CUTS).astype(jnp.bfloat16)
        second_copy(zs, step, CUTS).start()

    def send_back(k, inner):
        zs = place(k)

        @pl.when(zs > z)
        def _():
            pass_on(zs, [1] if inner else [], 1)

        @pl.when(zs < z)
        def _():
            pass_on(zs, [0] if inner else [], -1)

    def conclude(ways):
        for i in range(CUTS):
            out_ref[cuts[i], :] = summed(z, ways, i).astype(jnp.bfloat16)
        total = summed(z, ways, CUTS)
        for k in range(ids_ref.shape[0]):
            picked = jnp.where(item == ids_ref[k:k + 1, :], total, 0.0)
            gw_ref[k:k + 1, :] = jnp.sum(picked, axis=0, keepdims=True).astype(jnp.bfloat16)

    for kind in KINDS[:3]:
        each_z(kind, z, start)
    at_ends(each_z, KINDS[3], z, start)
    for i in range(len(crossing)):
        over_x(i).start()
    for kind in KINDS:
        to_core(kind, z).start()

    def own_rest(inward):
        @pl.when(low_half)
        def _():
            along_z(KINDS[3], z, inward).start()

        @pl.when(jnp.logical_not(low_half))
        def _():
            along_z(KINDS[3], z, -inward).start()

    def block_here(k):
        for kind in KINDS:
            arrived(kind, place(k), other_c)

    def half_here(j):
        for i in range(j * per, min((j + 1) * per, relayed)):
            over_y(i).wait_recv()
        if j == 1:
            for i in range(relayed, len(crossing)):
                over_x(i).wait_recv()

    far = n_ep - 1
    tasks = [(0, 0, 0), (0, 0, 1), (0, 1, 0)]
    for k in (far, far - 1):
        tasks += [(k, 0, 0), (k, 0, 1), (k, 1, 0)]
    tasks += [(far, 1, 1), (far - 1, 1, 1), (1, 0, 0), (1, 0, 1), (1, 1, 0), (1, 1, 1), (0, 1, 1)]
    events = {
        (0, 0, 0): [(block_here, 0)],
        (0, 0, 1): [(relay, 0)],
        (0, 1, 0): [
            (take, 1, 0, 1), (inside, take, far - 1, 0, 1), (relay, 1),
            (take, 1, 2), (inside, take, far - 1, 2), (relay, 2),
            (inside, take, 1, 3), (inside, own_rest, 1), (relay, 3),
            (at_ends, take, far - 1, 0, 1), (inside, take, far, 0, 1), (relay, 4),
            (at_ends, take, far - 1, 2), (inside, take, far, 2), (relay, 5),
            (inside, take, far, 3), (relay, 6), (half_here, 0),
        ],
        (far, 0, 0): [
            (at_ends, take, far, 0, 1), (inside, take, far - 1, 3),
            (inside, own_rest, -1), (relay, 7),
            (at_ends, take, far, 2), (relay, 8), (relay, 9),
            (at_ends, take, far, 3), (block_here, far),
        ],
        (far, 0, 1): [(relay, 10), (at_ends, take, far - 1, 3)],
        (far - 1, 0, 0): [(block_here, far - 1)],
        (far - 1, 1, 0): [(at_ends, take, 1, 3)],
        (far, 1, 1): [(half_here, 1)],
        (1, 0, 0): [(block_here, 1)],
    }
    finals = [i for i, task in enumerate(tasks) if task[1:] == (1, 1)]

    def is_one(i, values):
        return functools.reduce(jnp.logical_or, [i == value for value in values])

    def turn(i, carry):
        for task, acts in events.items():
            @pl.when(i == tasks.index(task))
            def _(acts=acts):
                for act, *args in acts:
                    act(*args)

        k, e, j = (pick(i, [task[field] for task in tasks]) for field in range(3))
        compute(place(k), e, j)

        @pl.when(is_one(i, finals))
        def _():
            finish(place(k))

        for done, later in zip(finals[:-1], finals[1:]):
            @pl.when(jnp.logical_and(i == done + 1, sides == 0))
            def _(done=done):
                send_back(tasks[done][0], False)

        return carry

    lax.fori_loop(0, len(tasks), turn, 0)

    @pl.when(sides > 0)
    def _():
        for k in [n_ep - 1] + list(range(1, n_ep - 1)):
            send_back(k, True)

    @pl.when(sides > 0)
    def _():
        conclude([1, 0])

    @pl.when(z == 0)
    def _():
        conclude([0])

    @pl.when(z == n_ep - 1)
    def _():
        conclude([1])

    def drain(zs, carry):
        for kind in KINDS:
            each_z(kind, zs, wait_send)
            to_core(kind, zs).wait_send()
        for i in range(CUTS + 1):
            first_copy(zs, i).wait_send()

        @pl.when(zs != z)
        def _():
            for i in range(CUTS + 1):
                second_copy(zs, 1, i).wait_send()

        return carry

    lax.fori_loop(0, n_ep, drain, 0)
    for i in range(len(crossing)):
        over_x(i).wait_send()
    for i in range(relayed):
        over_y(i).wait_send()


def swap_plan(tokens, cotangent, expert_ids, route_weights, w_gate, w_up, w_down):
    n_grp, n_ep = lax.axis_size("grp"), lax.axis_size("ep")
    named = gw_rows(n_grp * n_ep)
    rows, width = tokens.shape
    unit = w_gate.shape[2] // QUARTERS
    any_ref, vmem = pl.BlockSpec(memory_space=pl.ANY), pl.BlockSpec(memory_space=pltpu.VMEM)
    bf16, f32, dma = jnp.bfloat16, jnp.float32, pltpu.SemaphoreType.DMA
    pieces = 2 * (PIECES + 2) + 1
    grad_tokens, grad_weights = pl.pallas_call(
        functools.partial(swap_kernel, n_grp, n_ep),
        out_shape=(
            jax.ShapeDtypeStruct((rows, width), bf16),
            jax.ShapeDtypeStruct(expert_ids.shape[::-1], bf16),
        ),
        in_specs=[any_ref, any_ref, vmem, vmem, any_ref, any_ref, any_ref],
        out_specs=(vmem, vmem),
        scratch_shapes=[
            pltpu.VMEM((n_ep, CORES, rows, width), bf16),
            pltpu.VMEM((n_ep, CORES, rows, width), bf16),
            pltpu.VMEM((n_ep, CORES, 2 * named, LANES), bf16),
            pltpu.VMEM((2, 2, width, 4 * unit), bf16),
            pltpu.VMEM((2, 2, 2 * unit, width), bf16),
            pltpu.VMEM((n_ep, CORES, rows, width), f32),
            pltpu.VMEM((n_ep, 2, CORES * rows, LANES), f32),
            pltpu.VMEM((n_ep, rows, width), bf16),
            pltpu.VMEM((n_ep, named, LANES), bf16),
            pltpu.VMEM((n_ep, rows, width), bf16),
            pltpu.VMEM((n_ep, named, LANES), bf16),
            pltpu.VMEM((n_ep, rows, width), bf16),
            pltpu.VMEM((n_ep, named, LANES), bf16),
            pltpu.VMEM((2, n_ep, rows, width), bf16),
            pltpu.VMEM((2, n_ep, named, LANES), bf16),
            pltpu.VMEM((n_ep, CORES, named, LANES), bf16),
            dma((2 + 3 * QUARTERS,)), dma((4, n_ep, CORES)), dma((4, n_ep, 2)), dma((4, n_ep)),
            dma((pieces,)), dma((pieces,)), dma((pieces,)), dma((pieces,)),
            dma((n_ep, CUTS + 1)), dma((n_ep, CUTS + 1)),
            dma((n_ep, CUTS + 1)), dma((2, n_ep, CUTS + 1)),
        ],
        compiler_params=pltpu.CompilerParams(
            collective_id=0, has_side_effects=True, vmem_limit_bytes=VMEM_ROOM
        ),
    )(tokens, cotangent, expert_ids.T, route_weights.T, w_gate, w_up, w_down)
    return grad_tokens, grad_weights.T


def on_device(tokens, cotangent, expert_ids, route_weights, w_gate, w_up, w_down):
    n_grp, n_ep = lax.axis_size("grp"), lax.axis_size("ep")
    rows, width = tokens.shape
    swaps = lax.axis_size("parts") == 2 and n_grp == 2 * CORES and n_ep == 4
    fits = rows == LANES and width % LANES == 0 and w_gate.shape[2] == QUARTERS * LANES
    held = 2 * (w_gate.size + w_up.size + w_down.size) * 2 + n_ep * rows * width * 28
    plan = swap_plan if swaps and fits and held <= VMEM_ROOM else dispatch_plan
    return plan(tokens, cotangent, expert_ids, route_weights, w_gate, w_up, w_down)


def solution(mesh):
    in_specs = (
        P(("parts", "grp", "ep"), None),
        P(("parts", "grp", "ep"), None),
        P(("parts", "grp", "ep"), None),
        P(("parts", "grp", "ep"), None),
        P(("grp", "ep"), None, None),
        P(("grp", "ep"), None, None),
        P(("grp", "ep"), None, None),
    )
    out_specs = (P(("parts", "grp", "ep"), None), P(("parts", "grp", "ep"), None))
    return jax.shard_map(
        on_device, mesh=mesh, in_specs=in_specs, out_specs=out_specs, check_vma=False
    )
```

```python
import functools

import jax
import jax.numpy as jnp
from jax import lax
from jax.experimental import pallas as pl
from jax.experimental.pallas import tpu as pltpu
from jax.sharding import PartitionSpec as P

LANES = 128
CORES = 2
VMEM_ROOM = 56 * 1024 * 1024


def expert_grads(rows_in, grads_in, w_gate, w_up, w_down):
    contract = (((1,), (1,)), ((), ()))
    gate_pre = jnp.dot(rows_in, w_gate, preferred_element_type=jnp.float32)
    up_pre = jnp.dot(rows_in, w_up, preferred_element_type=jnp.float32)
    hidden_grad = lax.dot_general(grads_in, w_down, contract, preferred_element_type=jnp.float32)
    sigmoid_gate = jax.nn.sigmoid(gate_pre)
    activation = gate_pre * sigmoid_gate
    hidden = activation * up_pre
    weight_grad = jnp.sum(hidden_grad * hidden, axis=-1).astype(jnp.bfloat16)
    grad_up = (hidden_grad * activation).astype(jnp.bfloat16)
    grad_gate = (
        hidden_grad * up_pre * sigmoid_gate * (1.0 + gate_pre * (1.0 - sigmoid_gate))
    ).astype(jnp.bfloat16)
    row_terms = (
        lax.dot_general(grad_gate, w_gate, contract, preferred_element_type=jnp.float32)
        + lax.dot_general(grad_up, w_up, contract, preferred_element_type=jnp.float32)
    ).astype(jnp.bfloat16)
    return (row_terms, weight_grad)


def slot_plan(routes, experts, capacity):
    tok_rows, top_count = routes.shape
    flat_ids = routes.reshape(-1)
    pad_pair = flat_ids.shape[0]
    pair_ids = jnp.arange(pad_pair, dtype=jnp.int32)
    sort_order = jnp.argsort(flat_ids, stable=True)
    sorted_ids = flat_ids[sort_order]
    onehot = (flat_ids[:, None] == jnp.arange(experts, dtype=jnp.int32)[None, :]).astype(jnp.int32)
    counts = jnp.sum(onehot, axis=0)
    earlier = jnp.tri(experts, k=-1, dtype=jnp.int32)
    starts = jnp.sum(earlier * counts[None, :], axis=1)
    sorted_rank = pair_ids - starts[sorted_ids]
    sorted_slot = sorted_ids * capacity + sorted_rank
    slot_of_pair = jnp.zeros((pad_pair,), jnp.int32).at[sort_order].set(sorted_slot)
    slot_pair = jnp.full((experts * capacity,), pad_pair, jnp.int32).at[sorted_slot].set(sort_order)
    slot_token = jnp.where(slot_pair < pad_pair, slot_pair // top_count, tok_rows)
    return (slot_of_pair, slot_token, slot_pair)


def place_rows(source_rows, slot_token):
    padded = jnp.concatenate(
        [source_rows, jnp.zeros((1, source_rows.shape[1]), source_rows.dtype)], 0
    )
    return padded[slot_token]


def dispatch_plan(tokens, cotangent, expert_ids, route_weights, w_gate, w_up, w_down):
    group_count = lax.axis_size("grp")
    lane_count = lax.axis_size("ep")
    experts = group_count * lane_count
    tok_rows, top_count = expert_ids.shape
    model_width = tokens.shape[1]
    capacity = 2 * tok_rows * top_count // experts
    slot_of_pair, slot_token, unused_pairs = slot_plan(expert_ids, experts, capacity)
    send_rows = place_rows(tokens, slot_token).reshape(
        group_count, lane_count, capacity, model_width
    )
    send_grads = place_rows(cotangent, slot_token).reshape(
        group_count, lane_count, capacity, model_width
    )
    send_rows, send_grads = (
        lax.all_to_all(send_rows, "grp", split_axis=0, concat_axis=0, tiled=True),
        lax.all_to_all(send_grads, "grp", split_axis=0, concat_axis=0, tiled=True),
    )
    rows_in = lax.all_to_all(send_rows, "ep", split_axis=1, concat_axis=1, tiled=True)
    grads_in = lax.all_to_all(send_grads, "ep", split_axis=1, concat_axis=1, tiled=True)
    leading = rows_in.shape[:3]
    row_terms, weight_grad = expert_grads(
        rows_in.reshape(-1, model_width),
        grads_in.reshape(-1, model_width),
        w_gate[0],
        w_up[0],
        w_down[0],
    )
    row_terms = row_terms.reshape(leading + (model_width,))
    weight_grad = weight_grad.reshape(leading)
    row_terms, weight_grad = (
        lax.all_to_all(row_terms, "ep", split_axis=1, concat_axis=1, tiled=True),
        lax.all_to_all(weight_grad, "ep", split_axis=1, concat_axis=1, tiled=True),
    )
    row_terms, weight_grad = (
        lax.all_to_all(row_terms, "grp", split_axis=0, concat_axis=0, tiled=True),
        lax.all_to_all(weight_grad, "grp", split_axis=0, concat_axis=0, tiled=True),
    )
    row_terms = row_terms.reshape(experts * capacity, model_width)
    weight_grad = weight_grad.reshape(experts * capacity)
    picked = row_terms[slot_of_pair].reshape(tok_rows, top_count, model_width)
    grad_tokens = jnp.sum(route_weights[:, :, None] * picked.astype(jnp.float32), axis=1)
    grad_weights = weight_grad[slot_of_pair].reshape(tok_rows, top_count)
    return (grad_tokens.astype(jnp.bfloat16), grad_weights)


CUTS = 4
PIECES = 4
QUARTERS = 4
KINDS = (0, 1, 2, 3)


def gw_rows(experts):
    return -(-experts // 16) * 16


def pick(index, values):
    chosen = jnp.int32(values[0])
    for at in range(1, len(values)):
        if values[at] != values[at - 1]:
            chosen = jnp.where(index >= at, jnp.int32(values[at]), chosen)
    return chosen


def swap_kernel(
    n_grp, n_ep, tok_hbm, cot_hbm, ids_ref, route_ref, wg_hbm, wu_hbm, wd_hbm,
    out_ref, gw_ref,
    tok, cot, rts, wgu, wdn, acc, sums, parts, parts_g, r1, r1_g, sent, sent_g, up, up_g, pair_g,
    load_sem, got_sem, z_sem, c_sem, wx_s, wx_r, wy_s, wy_r,
    s1_sem, r1_sem, s2_sem, r2_sem,
):
    rows, width = out_ref.shape
    unit = wgu.shape[3] // QUARTERS
    named = gw_rows(n_grp * n_ep)
    p, g, z = lax.axis_index("parts"), lax.axis_index("grp"), lax.axis_index("ep")
    x, c = g // CORES, g % CORES
    other_c = 1 - c
    experts = (g * n_ep + z, ((1 - x) * CORES + c) * n_ep + z)
    core_peer = {"parts": p, "grp": x * CORES + other_c, "ep": z}
    x_peer = {"parts": p, "grp": (1 - x) * CORES + c, "ep": z}
    y_peer = {"parts": 1 - p, "grp": g, "ep": z}

    def z_peer(step):
        return {"parts": p, "grp": g, "ep": z + step}

    barrier = pltpu.get_barrier_semaphore()

    def greet(peer):
        pl.semaphore_signal(barrier, inc=1, device_id=peer, device_id_type=pl.DeviceIdType.MESH)

    for peer in (core_peer, x_peer, y_peer):
        greet(peer)

    @pl.when(z > 0)
    def _():
        greet(z_peer(-1))

    @pl.when(z < n_ep - 1)
    def _():
        greet(z_peer(1))

    loads = [
        pltpu.make_async_copy(tok_hbm, tok.at[z, c], load_sem.at[0]),
        pltpu.make_async_copy(cot_hbm, cot.at[z, c], load_sem.at[1]),
    ]
    for q in range(QUARTERS):
        span = pl.ds(q * unit, unit)
        for i, (source, target) in enumerate((
            (wg_hbm.at[0, :, span], wgu.at[0, q // 2, :, pl.ds(q % 2 * 2 * unit, unit)]),
            (wu_hbm.at[0, :, span], wgu.at[0, q // 2, :, pl.ds((q % 2 * 2 + 1) * unit, unit)]),
            (wd_hbm.at[0, span, :], wdn.at[0, q // 2, pl.ds(q % 2 * unit, unit)]),
        )):
            loads.append(pltpu.make_async_copy(source, target, load_sem.at[2 + 3 * q + i]))
    for load in loads:
        load.start()

    item = lax.broadcasted_iota(jnp.int32, (named, LANES), 0)
    routed = jnp.zeros((named, LANES), jnp.float32)
    for k in range(ids_ref.shape[0]):
        routed += jnp.where(item == ids_ref[k:k + 1, :], route_ref[k:k + 1, :], 0.0)
    high = routed.astype(jnp.bfloat16)
    rts[z, c, 0:named, :] = high
    rts[z, c, named:2 * named, :] = (routed - high.astype(jnp.float32)).astype(jnp.bfloat16)

    acc[...] = jnp.zeros_like(acc)
    sums[...] = jnp.zeros_like(sums)
    for load in loads:
        load.wait()
    near = jnp.where(z > 0, 1, 0) + jnp.where(z < n_ep - 1, 1, 0)
    pl.semaphore_wait(barrier, 3 + near)

    def remote(source, target, send, recv, peer):
        return pltpu.make_async_remote_copy(
            src_ref=source, dst_ref=target, send_sem=send, recv_sem=recv,
            device_id=peer, device_id_type=pl.DeviceIdType.MESH,
        )

    sides = jnp.minimum(z, n_ep - 1 - z)

    low_half = 2 * z < n_ep - 1

    def place(k):
        step = jnp.where(k % 2 == 1, -((k + 1) // 2), k // 2)
        near_k = jnp.where(low_half, z + step, z - step)
        far_k = jnp.where(low_half, k, n_ep - 1 - k)
        return jnp.where(k <= 2 * sides, near_k, far_k)

    part = rows // 2

    def block(kind, zs, cs):
        if kind == 0:
            return tok.at[zs, cs]
        if kind == 1:
            return rts.at[zs, cs]
        return cot.at[zs, cs, pl.ds((kind - 2) * part, part)]

    def along_z(kind, zs, step):
        here = block(kind, zs, c)
        return remote(here, here, z_sem.at[kind, zs, (step + 1) // 2], got_sem.at[kind, zs, c],
                      z_peer(step))

    def to_core(kind, zs):
        here = block(kind, zs, c)
        return remote(here, here, c_sem.at[kind, zs], got_sem.at[kind, zs, c], core_peer)

    def arrived(kind, zs, cs):
        here = block(kind, zs, cs)
        remote(here, here, c_sem.at[kind, zs], got_sem.at[kind, zs, cs], core_peer).wait_recv()

    def each_z(kind, zs, act):
        @pl.when(jnp.logical_and(zs <= z, z < n_ep - 1))
        def _():
            act(along_z(kind, zs, 1))

        @pl.when(jnp.logical_and(zs >= z, z > 0))
        def _():
            act(along_z(kind, zs, -1))

    def start(copy):
        copy.start()

    def wait_send(copy):
        copy.wait_send()

    def take(k, *group):
        zs = place(k)
        for kind in group:
            arrived(kind, zs, c)
            each_z(kind, zs, start)
            to_core(kind, zs).start()

    def at_ends(act, *args):
        @pl.when(sides == 0)
        def _():
            act(*args)

    def inside(act, *args):
        @pl.when(sides > 0)
        def _():
            act(*args)

    per = PIECES + 2

    def piece(e, j, h, n):
        if n < PIECES:
            span = width // PIECES
            lanes = pl.ds(pl.multiple_of(h * 2 * unit, 2 * unit), 2 * unit)
            return wgu.at[e, j, pl.ds(n * span, span), lanes]
        span = unit // 2
        low = pl.multiple_of(h * unit + (n - PIECES) * span, span)
        return wdn.at[e, j, pl.ds(low, span)]

    crossing = [(j, p, n) for j in range(2) for n in range(per)] + [(1, 1 - p, per - 1)]
    relayed = 2 * per - 1

    def over_x(i):
        return remote(piece(0, *crossing[i]), piece(1, *crossing[i]), wx_s.at[i], wx_r.at[i], x_peer)

    def over_y(i):
        here = piece(1, *crossing[i])
        return remote(here, here, wy_s.at[i], wy_r.at[i], y_peer)

    def relay(i):
        over_x(i).wait_recv()
        over_y(i).start()

    contract = (((1,), (1,)), ((), ()))
    both = CORES * rows

    def scale_of(zs, expert):
        columns = []
        for cs in range(CORES):
            routes = rts[zs, cs, 0:named, :].astype(jnp.float32)
            routes += rts[zs, cs, named:2 * named, :].astype(jnp.float32)
            weight = jnp.sum(jnp.where(item == expert, routes, 0.0), axis=0, keepdims=True)
            columns.append(jnp.broadcast_to(weight, (rows, LANES)).T)
        return jnp.concatenate(columns, axis=0)

    def compute(zs, e, j):
        expert = jnp.where(e == 0, experts[0], experts[1])
        scale = scale_of(zs, expert)
        rows_in = tok[zs].reshape(both, width)
        grads_in = cot[zs].reshape(both, width)
        pres = jnp.dot(rows_in, wgu[e, j], preferred_element_type=jnp.float32)
        hidden_grads = lax.dot_general(grads_in, wdn[e, j], contract, preferred_element_type=jnp.float32)
        lane_sums = jnp.zeros((both, LANES), jnp.float32)
        grads = []
        for h in range(2):
            gate_pre = pres[:, 2 * h * unit:(2 * h + 1) * unit]
            up_pre = pres[:, (2 * h + 1) * unit:(2 * h + 2) * unit]
            hidden_grad = hidden_grads[:, h * unit:(h + 1) * unit]
            sigmoid_gate = 1.0 / (1.0 + jnp.exp(-gate_pre))
            activation = gate_pre * sigmoid_gate
            lane_sums += hidden_grad * (activation * up_pre)
            hidden_grad = hidden_grad * scale
            grads.append((hidden_grad * up_pre * sigmoid_gate
                          * (1.0 + gate_pre * (1.0 - sigmoid_gate))).astype(jnp.bfloat16))
            grads.append((hidden_grad * activation).astype(jnp.bfloat16))
        sums[zs, e] += lane_sums
        terms = lax.dot_general(jnp.concatenate(grads, axis=1), wgu[e, j], contract,
                                preferred_element_type=jnp.float32)
        acc[zs] += terms.reshape(CORES, rows, width)

    cut_rows = rows // CUTS
    cuts = [pl.ds(i * cut_rows, cut_rows) for i in range(CUTS)]

    def first_copy(zs, i):
        if i < CUTS:
            source, target = parts.at[zs, cuts[i]], r1.at[zs, cuts[i]]
        else:
            source, target = parts_g.at[zs], r1_g.at[zs]
        return remote(source, target, s1_sem.at[zs, i], r1_sem.at[zs, i], core_peer)

    def second_copy(zs, step, i):
        way = (step + 1) // 2
        if i < CUTS:
            source, target = sent.at[zs, cuts[i]], up.at[way, zs, cuts[i]]
        else:
            source, target = sent_g.at[zs], up_g.at[way, zs]
        return remote(source, target, s2_sem.at[zs, i], r2_sem.at[way, zs, i], z_peer(step))

    def finish(zs):
        parts[zs] = acc[zs, other_c].astype(jnp.bfloat16)
        for i in range(CUTS):
            first_copy(zs, i).start()
        for cs in range(CORES):
            here = slice(cs * rows, (cs + 1) * rows)
            found = jnp.zeros((named, LANES), jnp.float32)
            for e in range(2):
                weight_grad = jnp.sum(sums[zs, e, here, :].T, axis=0, keepdims=True)
                found += jnp.where(item == experts[e], weight_grad, 0.0)
            pair_g[zs, cs] = found.astype(jnp.bfloat16)
        parts_g[zs] = pair_g[zs, other_c]
        first_copy(zs, CUTS).start()

    def summed(zs, ways, i):
        first_copy(zs, i).wait_recv()
        for way in ways:
            second_copy(zs, 2 * way - 1, i).wait_recv()
        if i < CUTS:
            total = acc[zs, c, cuts[i]] + r1[zs, cuts[i]].astype(jnp.float32)
            for way in ways:
                total += up[way, zs, cuts[i]].astype(jnp.float32)
            return total
        total = pair_g[zs, c].astype(jnp.float32) + r1_g[zs].astype(jnp.float32)
        for way in ways:
            total += up_g[way, zs].astype(jnp.float32)
        return total

    def pass_on(zs, ways, step):
        for i in range(CUTS):
            sent[zs, cuts[i]] = summed(zs, ways, i).astype(jnp.bfloat16)
            second_copy(zs, step, i).start()
        sent_g[zs] = summed(zs, ways, CUTS).astype(jnp.bfloat16)
        second_copy(zs, step, CUTS).start()

    def send_back(k, inner):
        zs = place(k)

        @pl.when(zs > z)
        def _():
            pass_on(zs, [1] if inner else [], 1)

        @pl.when(zs < z)
        def _():
            pass_on(zs, [0] if inner else [], -1)

    def conclude(ways):
        for i in range(CUTS):
            out_ref[cuts[i], :] = summed(z, ways, i).astype(jnp.bfloat16)
        total = summed(z, ways, CUTS)
        for k in range(ids_ref.shape[0]):
            picked = jnp.where(item == ids_ref[k:k + 1, :], total, 0.0)
            gw_ref[k:k + 1, :] = jnp.sum(picked, axis=0, keepdims=True).astype(jnp.bfloat16)

    def own_rest(inward):
        @pl.when(low_half)
        def _():
            along_z(KINDS[3], z, inward).start()

        @pl.when(jnp.logical_not(low_half))
        def _():
            along_z(KINDS[3], z, -inward).start()

    for kind in KINDS[:3]:
        each_z(kind, z, start)
    at_ends(each_z, KINDS[3], z, start)
    inside(own_rest, 1)
    for i in range(len(crossing)):
        over_x(i).start()
    for kind in KINDS:
        to_core(kind, z).start()

    def block_here(k):
        for kind in KINDS:
            arrived(kind, place(k), other_c)

    def half_here(j):
        for i in range(j * per, min((j + 1) * per, relayed)):
            over_y(i).wait_recv()
        if j == 1:
            for i in range(relayed, len(crossing)):
                over_x(i).wait_recv()

    far = n_ep - 1
    tasks = [(0, 0, 0), (0, 0, 1), (far - 1, 0, 0), (far - 1, 0, 1), (0, 1, 0), (far - 1, 1, 0)]
    tasks += [(far, 0, 0), (far, 0, 1), (far, 1, 0), (far, 1, 1), (far - 1, 1, 1)]
    tasks += [(1, 0, 0), (1, 0, 1), (1, 1, 0), (1, 1, 1), (0, 1, 1)]
    events = {
        (0, 0, 0): [(block_here, 0)],
        (0, 0, 1): [(relay, 0)],
        (far - 1, 0, 0): [
            (take, 1, 0, 1), (inside, take, far - 1, 0, 1), (relay, 1),
            (take, 1, 2), (inside, take, far - 1, 2), (relay, 2),
            (inside, take, 1, 3), (inside, take, far - 1, 3), (relay, 3),
            (at_ends, take, far - 1, 0, 1), (relay, 4),
            (inside, take, far, 0, 1), (at_ends, take, far - 1, 2), (relay, 5),
            (inside, take, far, 2), (at_ends, take, far - 1, 3), (relay, 6),
            (block_here, far - 1),
        ],
        (far - 1, 0, 1): [(inside, take, far, 3), (inside, own_rest, -1), (relay, 7)],
        (0, 1, 0): [(half_here, 0)],
        (far - 1, 1, 0): [(at_ends, take, far, 0, 1), (relay, 8)],
        (far, 0, 0): [
            (at_ends, take, far, 2), (relay, 9), (at_ends, take, far, 3), (relay, 10),
            (block_here, far),
        ],
        (far, 1, 0): [(at_ends, take, 1, 3)],
        (far, 1, 1): [(half_here, 1)],
        (1, 0, 0): [(block_here, 1)],
    }
    finals = [i for i, task in enumerate(tasks) if task[1:] == (1, 1)]

    def is_one(i, values):
        return functools.reduce(jnp.logical_or, [i == value for value in values])

    def turn(i, carry):
        for task, acts in events.items():
            @pl.when(i == tasks.index(task))
            def _(acts=acts):
                for act, *args in acts:
                    act(*args)

        k, e, j = (pick(i, [task[field] for task in tasks]) for field in range(3))
        compute(place(k), e, j)

        @pl.when(is_one(i, finals))
        def _():
            finish(place(k))

        for done, later in zip(finals[:-1], finals[1:]):
            @pl.when(jnp.logical_and(i == done + 1, sides == 0))
            def _(done=done):
                send_back(tasks[done][0], False)

        return carry

    lax.fori_loop(0, len(tasks), turn, 0)

    @pl.when(sides > 0)
    def _():
        for k in [n_ep - 1] + list(range(1, n_ep - 1)):
            send_back(k, True)

    @pl.when(sides > 0)
    def _():
        conclude([1, 0])

    @pl.when(z == 0)
    def _():
        conclude([0])

    @pl.when(z == n_ep - 1)
    def _():
        conclude([1])

    def drain(zs, carry):
        for kind in KINDS:
            each_z(kind, zs, wait_send)
            to_core(kind, zs).wait_send()
        for i in range(CUTS + 1):
            first_copy(zs, i).wait_send()

        @pl.when(zs != z)
        def _():
            for i in range(CUTS + 1):
                second_copy(zs, 1, i).wait_send()

        return carry

    lax.fori_loop(0, n_ep, drain, 0)
    for i in range(len(crossing)):
        over_x(i).wait_send()
    for i in range(relayed):
        over_y(i).wait_send()


def swap_plan(tokens, cotangent, expert_ids, route_weights, w_gate, w_up, w_down):
    n_grp, n_ep = lax.axis_size("grp"), lax.axis_size("ep")
    named = gw_rows(n_grp * n_ep)
    rows, width = tokens.shape
    unit = w_gate.shape[2] // QUARTERS
    any_ref, vmem = pl.BlockSpec(memory_space=pl.ANY), pl.BlockSpec(memory_space=pltpu.VMEM)
    bf16, f32, dma = jnp.bfloat16, jnp.float32, pltpu.SemaphoreType.DMA
    pieces = 2 * (PIECES + 2) + 1
    grad_tokens, grad_weights = pl.pallas_call(
        functools.partial(swap_kernel, n_grp, n_ep),
        out_shape=(
            pltpu.VMEM((rows, width), bf16),
            pltpu.VMEM(expert_ids.shape[::-1], bf16),
        ),
        in_specs=[any_ref, any_ref, vmem, vmem, any_ref, any_ref, any_ref],
        out_specs=(vmem, vmem),
        scratch_shapes=[
            pltpu.VMEM((n_ep, CORES, rows, width), bf16),
            pltpu.VMEM((n_ep, CORES, rows, width), bf16),
            pltpu.VMEM((n_ep, CORES, 2 * named, LANES), bf16),
            pltpu.VMEM((2, 2, width, 4 * unit), bf16),
            pltpu.VMEM((2, 2, 2 * unit, width), bf16),
            pltpu.VMEM((n_ep, CORES, rows, width), f32),
            pltpu.VMEM((n_ep, 2, CORES * rows, LANES), f32),
            pltpu.VMEM((n_ep, rows, width), bf16),
            pltpu.VMEM((n_ep, named, LANES), bf16),
            pltpu.VMEM((n_ep, rows, width), bf16),
            pltpu.VMEM((n_ep, named, LANES), bf16),
            pltpu.VMEM((n_ep, rows, width), bf16),
            pltpu.VMEM((n_ep, named, LANES), bf16),
            pltpu.VMEM((2, n_ep, rows, width), bf16),
            pltpu.VMEM((2, n_ep, named, LANES), bf16),
            pltpu.VMEM((n_ep, CORES, named, LANES), bf16),
            dma((2 + 3 * QUARTERS,)), dma((4, n_ep, CORES)), dma((4, n_ep, 2)), dma((4, n_ep)),
            dma((pieces,)), dma((pieces,)), dma((pieces,)), dma((pieces,)),
            dma((n_ep, CUTS + 1)), dma((n_ep, CUTS + 1)),
            dma((n_ep, CUTS + 1)), dma((2, n_ep, CUTS + 1)),
        ],
        compiler_params=pltpu.CompilerParams(
            collective_id=0, has_side_effects=True, vmem_limit_bytes=VMEM_ROOM
        ),
    )(tokens, cotangent, expert_ids.T, route_weights.T, w_gate, w_up, w_down)
    return grad_tokens, grad_weights.T


def on_device(tokens, cotangent, expert_ids, route_weights, w_gate, w_up, w_down):
    n_grp, n_ep = lax.axis_size("grp"), lax.axis_size("ep")
    rows, width = tokens.shape
    swaps = lax.axis_size("parts") == 2 and n_grp == 2 * CORES and n_ep == 4
    fits = rows == LANES and width % LANES == 0 and w_gate.shape[2] == QUARTERS * LANES
    held = 2 * (w_gate.size + w_up.size + w_down.size) * 2 + n_ep * rows * width * 28
    plan = swap_plan if swaps and fits and held <= VMEM_ROOM else dispatch_plan
    return plan(tokens, cotangent, expert_ids, route_weights, w_gate, w_up, w_down)


def solution(mesh):
    in_specs = (
        P(("parts", "grp", "ep"), None),
        P(("parts", "grp", "ep"), None),
        P(("parts", "grp", "ep"), None),
        P(("parts", "grp", "ep"), None),
        P(("grp", "ep"), None, None),
        P(("grp", "ep"), None, None),
        P(("grp", "ep"), None, None),
    )
    out_specs = (P(("parts", "grp", "ep"), None), P(("parts", "grp", "ep"), None))
    return jax.shard_map(
        on_device, mesh=mesh, in_specs=in_specs, out_specs=out_specs, check_vma=False
    )
```

```python
import functools

import jax
import jax.numpy as jnp
from jax import lax
from jax.experimental import pallas as pl
from jax.experimental.pallas import tpu as pltpu
from jax.sharding import PartitionSpec as P

LANES = 128
CORES = 2
VMEM_ROOM = 56 * 1024 * 1024


def expert_grads(rows_in, grads_in, w_gate, w_up, w_down):
    contract = (((1,), (1,)), ((), ()))
    gate_pre = jnp.dot(rows_in, w_gate, preferred_element_type=jnp.float32)
    up_pre = jnp.dot(rows_in, w_up, preferred_element_type=jnp.float32)
    hidden_grad = lax.dot_general(grads_in, w_down, contract, preferred_element_type=jnp.float32)
    sigmoid_gate = jax.nn.sigmoid(gate_pre)
    activation = gate_pre * sigmoid_gate
    hidden = activation * up_pre
    weight_grad = jnp.sum(hidden_grad * hidden, axis=-1).astype(jnp.bfloat16)
    grad_up = (hidden_grad * activation).astype(jnp.bfloat16)
    grad_gate = (
        hidden_grad * up_pre * sigmoid_gate * (1.0 + gate_pre * (1.0 - sigmoid_gate))
    ).astype(jnp.bfloat16)
    row_terms = (
        lax.dot_general(grad_gate, w_gate, contract, preferred_element_type=jnp.float32)
        + lax.dot_general(grad_up, w_up, contract, preferred_element_type=jnp.float32)
    ).astype(jnp.bfloat16)
    return (row_terms, weight_grad)


def slot_plan(routes, experts, capacity):
    tok_rows, top_count = routes.shape
    flat_ids = routes.reshape(-1)
    pad_pair = flat_ids.shape[0]
    pair_ids = jnp.arange(pad_pair, dtype=jnp.int32)
    sort_order = jnp.argsort(flat_ids, stable=True)
    sorted_ids = flat_ids[sort_order]
    onehot = (flat_ids[:, None] == jnp.arange(experts, dtype=jnp.int32)[None, :]).astype(jnp.int32)
    counts = jnp.sum(onehot, axis=0)
    earlier = jnp.tri(experts, k=-1, dtype=jnp.int32)
    starts = jnp.sum(earlier * counts[None, :], axis=1)
    sorted_rank = pair_ids - starts[sorted_ids]
    sorted_slot = sorted_ids * capacity + sorted_rank
    slot_of_pair = jnp.zeros((pad_pair,), jnp.int32).at[sort_order].set(sorted_slot)
    slot_pair = jnp.full((experts * capacity,), pad_pair, jnp.int32).at[sorted_slot].set(sort_order)
    slot_token = jnp.where(slot_pair < pad_pair, slot_pair // top_count, tok_rows)
    return (slot_of_pair, slot_token, slot_pair)


def place_rows(source_rows, slot_token):
    padded = jnp.concatenate(
        [source_rows, jnp.zeros((1, source_rows.shape[1]), source_rows.dtype)], 0
    )
    return padded[slot_token]


def dispatch_plan(tokens, cotangent, expert_ids, route_weights, w_gate, w_up, w_down):
    group_count = lax.axis_size("grp")
    lane_count = lax.axis_size("ep")
    experts = group_count * lane_count
    tok_rows, top_count = expert_ids.shape
    model_width = tokens.shape[1]
    capacity = 2 * tok_rows * top_count // experts
    slot_of_pair, slot_token, unused_pairs = slot_plan(expert_ids, experts, capacity)
    send_rows = place_rows(tokens, slot_token).reshape(
        group_count, lane_count, capacity, model_width
    )
    send_grads = place_rows(cotangent, slot_token).reshape(
        group_count, lane_count, capacity, model_width
    )
    send_rows, send_grads = (
        lax.all_to_all(send_rows, "grp", split_axis=0, concat_axis=0, tiled=True),
        lax.all_to_all(send_grads, "grp", split_axis=0, concat_axis=0, tiled=True),
    )
    rows_in = lax.all_to_all(send_rows, "ep", split_axis=1, concat_axis=1, tiled=True)
    grads_in = lax.all_to_all(send_grads, "ep", split_axis=1, concat_axis=1, tiled=True)
    leading = rows_in.shape[:3]
    row_terms, weight_grad = expert_grads(
        rows_in.reshape(-1, model_width),
        grads_in.reshape(-1, model_width),
        w_gate[0],
        w_up[0],
        w_down[0],
    )
    row_terms = row_terms.reshape(leading + (model_width,))
    weight_grad = weight_grad.reshape(leading)
    row_terms, weight_grad = (
        lax.all_to_all(row_terms, "ep", split_axis=1, concat_axis=1, tiled=True),
        lax.all_to_all(weight_grad, "ep", split_axis=1, concat_axis=1, tiled=True),
    )
    row_terms, weight_grad = (
        lax.all_to_all(row_terms, "grp", split_axis=0, concat_axis=0, tiled=True),
        lax.all_to_all(weight_grad, "grp", split_axis=0, concat_axis=0, tiled=True),
    )
    row_terms = row_terms.reshape(experts * capacity, model_width)
    weight_grad = weight_grad.reshape(experts * capacity)
    picked = row_terms[slot_of_pair].reshape(tok_rows, top_count, model_width)
    grad_tokens = jnp.sum(route_weights[:, :, None] * picked.astype(jnp.float32), axis=1)
    grad_weights = weight_grad[slot_of_pair].reshape(tok_rows, top_count)
    return (grad_tokens.astype(jnp.bfloat16), grad_weights)


CUTS = 4
ORDER = tuple(range(CUTS - 1)) + (CUTS, CUTS - 1)
PIECES = 4
QUARTERS = 4
KINDS = (0, 1, 2, 3)


def gw_rows(experts):
    return -(-experts // 16) * 16


def pick(index, values):
    chosen = jnp.int32(values[0])
    for at in range(1, len(values)):
        if values[at] != values[at - 1]:
            chosen = jnp.where(index >= at, jnp.int32(values[at]), chosen)
    return chosen


def swap_kernel(
    n_grp, n_ep, tok_hbm, cot_hbm, ids_hbm, route_hbm, wg_hbm, wu_hbm, wd_hbm,
    out_ref, gw_ref,
    ids_ref, route_ref, tok, cot, rts, wgu, wdn, acc, sums, parts, parts_g, r1, r1_g, sent, sent_g, up, up_g, pair_g,
    load_sem, got_sem, z_sem, c_sem, wx_s, wx_r, wy_s, wy_r,
    s1_sem, r1_sem, s2_sem, r2_sem,
):
    rows, width = out_ref.shape
    unit = wgu.shape[3] // QUARTERS
    named = gw_rows(n_grp * n_ep)
    p, g, z = lax.axis_index("parts"), lax.axis_index("grp"), lax.axis_index("ep")
    x, c = g // CORES, g % CORES
    other_c = 1 - c
    experts = (g * n_ep + z, ((1 - x) * CORES + c) * n_ep + z)
    core_peer = {"parts": p, "grp": x * CORES + other_c, "ep": z}
    x_peer = {"parts": p, "grp": (1 - x) * CORES + c, "ep": z}
    y_peer = {"parts": 1 - p, "grp": g, "ep": z}

    def z_peer(step):
        return {"parts": p, "grp": g, "ep": z + step}

    barrier = pltpu.get_barrier_semaphore()

    def greet(peer):
        pl.semaphore_signal(barrier, inc=1, device_id=peer, device_id_type=pl.DeviceIdType.MESH)

    for peer in (core_peer, x_peer, y_peer):
        greet(peer)

    @pl.when(z > 0)
    def _():
        greet(z_peer(-1))

    @pl.when(z < n_ep - 1)
    def _():
        greet(z_peer(1))

    small = [
        pltpu.make_async_copy(ids_hbm, ids_ref, load_sem.at[2 + 3 * QUARTERS]),
        pltpu.make_async_copy(route_hbm, route_ref, load_sem.at[3 + 3 * QUARTERS]),
    ]
    for load in small:
        load.start()
    loads = [
        pltpu.make_async_copy(tok_hbm, tok.at[z, c], load_sem.at[0]),
        pltpu.make_async_copy(cot_hbm, cot.at[z, c], load_sem.at[1]),
    ]
    for q in range(QUARTERS):
        span = pl.ds(q * unit, unit)
        for i, (source, target) in enumerate((
            (wg_hbm.at[0, :, span], wgu.at[0, q // 2, :, pl.ds(q % 2 * 2 * unit, unit)]),
            (wu_hbm.at[0, :, span], wgu.at[0, q // 2, :, pl.ds((q % 2 * 2 + 1) * unit, unit)]),
            (wd_hbm.at[0, span, :], wdn.at[0, q // 2, pl.ds(q % 2 * unit, unit)]),
        )):
            loads.append(pltpu.make_async_copy(source, target, load_sem.at[2 + 3 * q + i]))
    for load in loads:
        load.start()

    acc[...] = jnp.zeros_like(acc)
    sums[...] = jnp.zeros_like(sums)
    for load in small:
        load.wait()
    item = lax.broadcasted_iota(jnp.int32, (named, LANES), 0)
    routed = jnp.zeros((named, LANES), jnp.float32)
    for k in range(ids_ref.shape[0]):
        routed += jnp.where(item == ids_ref[k:k + 1, :], route_ref[k:k + 1, :], 0.0)
    high = routed.astype(jnp.bfloat16)
    rts[z, c, 0:named, :] = high
    rts[z, c, named:2 * named, :] = (routed - high.astype(jnp.float32)).astype(jnp.bfloat16)

    for load in loads:
        load.wait()
    near = jnp.where(z > 0, 1, 0) + jnp.where(z < n_ep - 1, 1, 0)
    pl.semaphore_wait(barrier, 3 + near)

    def remote(source, target, send, recv, peer):
        return pltpu.make_async_remote_copy(
            src_ref=source, dst_ref=target, send_sem=send, recv_sem=recv,
            device_id=peer, device_id_type=pl.DeviceIdType.MESH,
        )

    sides = jnp.minimum(z, n_ep - 1 - z)

    low_half = 2 * z < n_ep - 1

    def place(k):
        step = jnp.where(k % 2 == 1, -((k + 1) // 2), k // 2)
        near_k = jnp.where(low_half, z + step, z - step)
        far_k = jnp.where(low_half, k, n_ep - 1 - k)
        return jnp.where(k <= 2 * sides, near_k, far_k)

    part = rows // 2

    def block(kind, zs, cs):
        if kind == 0:
            return tok.at[zs, cs]
        if kind == 1:
            return rts.at[zs, cs]
        return cot.at[zs, cs, pl.ds((kind - 2) * part, part)]

    def along_z(kind, zs, step):
        here = block(kind, zs, c)
        return remote(here, here, z_sem.at[kind, zs, (step + 1) // 2], got_sem.at[kind, zs, c],
                      z_peer(step))

    def to_core(kind, zs):
        here = block(kind, zs, c)
        return remote(here, here, c_sem.at[kind, zs], got_sem.at[kind, zs, c], core_peer)

    def arrived(kind, zs, cs):
        here = block(kind, zs, cs)
        remote(here, here, c_sem.at[kind, zs], got_sem.at[kind, zs, cs], core_peer).wait_recv()

    def each_z(kind, zs, act):
        @pl.when(jnp.logical_and(zs <= z, z < n_ep - 1))
        def _():
            act(along_z(kind, zs, 1))

        @pl.when(jnp.logical_and(zs >= z, z > 0))
        def _():
            act(along_z(kind, zs, -1))

    def start(copy):
        copy.start()

    def wait_send(copy):
        copy.wait_send()

    def take(k, *group):
        zs = place(k)
        for kind in group:
            arrived(kind, zs, c)
            each_z(kind, zs, start)
            to_core(kind, zs).start()

    def at_ends(act, *args):
        @pl.when(sides == 0)
        def _():
            act(*args)

    def inside(act, *args):
        @pl.when(sides > 0)
        def _():
            act(*args)

    downs = PIECES // 2
    tall, flat = width // PIECES, unit // downs

    def gate_up(e, j, h, at):
        lanes = pl.ds(pl.multiple_of(h * 2 * unit, 2 * unit), 2 * unit)
        return wgu.at[e, j, pl.ds(pl.multiple_of(at * tall, tall), tall), lanes]

    def down(e, j, h, at):
        return wdn.at[e, j, pl.ds(pl.multiple_of(h * unit + at * flat, flat), flat)]

    crossing = [(gate_up, 0, p, n) for n in range(PIECES)] + [(down, 0, p, n) for n in range(downs)]
    early = len(crossing)
    for h in range(2):
        crossing += [(gate_up, 1, h, p * downs + n) for n in range(downs)]
        crossing += [(down, 1, h, p * (downs // 2) + n) for n in range(downs // 2)]
    crossing += [(down, 1, 1, (1 - p) * (downs // 2) + n) for n in range(downs // 2)]
    middle, relayed = early + downs + downs // 2, len(crossing) - downs

    def piece(e, i):
        part, *place_of = crossing[i]
        return part(e, *place_of)

    def over_x(i):
        return remote(piece(0, i), piece(1, i), wx_s.at[i], wx_r.at[i], x_peer)

    def over_y(i):
        return remote(piece(1, i), piece(1, i), wy_s.at[i], wy_r.at[i], y_peer)

    def relay(i):
        over_x(i).wait_recv()
        over_y(i).start()

    contract = (((1,), (1,)), ((), ()))
    both = CORES * rows

    def scale_of(zs, expert):
        columns = []
        for cs in range(CORES):
            routes = rts[zs, cs, 0:named, :].astype(jnp.float32)
            routes += rts[zs, cs, named:2 * named, :].astype(jnp.float32)
            weight = jnp.sum(jnp.where(item == expert, routes, 0.0), axis=0, keepdims=True)
            columns.append(jnp.broadcast_to(weight, (rows, LANES)).T)
        return jnp.concatenate(columns, axis=0)

    def compute(zs, e, j, halves):
        expert = jnp.where(e == 0, experts[0], experts[1])
        scale = scale_of(zs, expert)
        rows_in = tok[zs].reshape(both, width)
        grads_in = cot[zs].reshape(both, width)
        low, high = halves[0] * unit, (halves[-1] + 1) * unit
        pres = jnp.dot(rows_in, wgu[e, j, :, 2 * low:2 * high], preferred_element_type=jnp.float32)
        hidden_grads = lax.dot_general(grads_in, wdn[e, j, low:high], contract,
                                       preferred_element_type=jnp.float32)
        lane_sums = jnp.zeros((both, LANES), jnp.float32)
        grads = []
        for at in range(len(halves)):
            gate_pre = pres[:, 2 * at * unit:(2 * at + 1) * unit]
            up_pre = pres[:, (2 * at + 1) * unit:(2 * at + 2) * unit]
            hidden_grad = hidden_grads[:, at * unit:(at + 1) * unit]
            sigmoid_gate = 1.0 / (1.0 + jnp.exp(-gate_pre))
            activation = gate_pre * sigmoid_gate
            lane_sums += hidden_grad * (activation * up_pre)
            hidden_grad = hidden_grad * scale
            grads.append((hidden_grad * up_pre * sigmoid_gate
                          * (1.0 + gate_pre * (1.0 - sigmoid_gate))).astype(jnp.bfloat16))
            grads.append((hidden_grad * activation).astype(jnp.bfloat16))
        sums[zs, e] += lane_sums
        terms = lax.dot_general(jnp.concatenate(grads, axis=1), wgu[e, j, :, 2 * low:2 * high],
                                contract, preferred_element_type=jnp.float32)
        acc[zs] += terms.reshape(CORES, rows, width)

    cut_rows = rows // CUTS
    cuts = [pl.ds(i * cut_rows, cut_rows) for i in range(CUTS)]

    def first_copy(zs, i):
        if i < CUTS:
            source, target = parts.at[zs, cuts[i]], r1.at[zs, cuts[i]]
        else:
            source, target = parts_g.at[zs], r1_g.at[zs]
        return remote(source, target, s1_sem.at[zs, i], r1_sem.at[zs, i], core_peer)

    def second_copy(zs, step, i):
        way = (step + 1) // 2
        if i < CUTS:
            source, target = sent.at[zs, cuts[i]], up.at[way, zs, cuts[i]]
        else:
            source, target = sent_g.at[zs], up_g.at[way, zs]
        return remote(source, target, s2_sem.at[zs, i], r2_sem.at[way, zs, i], z_peer(step))

    def finish(zs):
        parts[zs] = acc[zs, other_c].astype(jnp.bfloat16)
        for i in range(CUTS):
            first_copy(zs, i).start()
        for cs in range(CORES):
            here = slice(cs * rows, (cs + 1) * rows)
            found = jnp.zeros((named, LANES), jnp.float32)
            for e in range(2):
                weight_grad = jnp.sum(sums[zs, e, here, :].T, axis=0, keepdims=True)
                found += jnp.where(item == experts[e], weight_grad, 0.0)
            pair_g[zs, cs] = found.astype(jnp.bfloat16)
        parts_g[zs] = pair_g[zs, other_c]
        first_copy(zs, CUTS).start()

    def summed(zs, ways, i):
        first_copy(zs, i).wait_recv()
        for way in ways:
            second_copy(zs, 2 * way - 1, i).wait_recv()
        if i < CUTS:
            total = acc[zs, c, cuts[i]] + r1[zs, cuts[i]].astype(jnp.float32)
            for way in ways:
                total += up[way, zs, cuts[i]].astype(jnp.float32)
            return total
        total = pair_g[zs, c].astype(jnp.float32) + r1_g[zs].astype(jnp.float32)
        for way in ways:
            total += up_g[way, zs].astype(jnp.float32)
        return total

    def pass_on(zs, ways, step):
        for i in ORDER:
            total = summed(zs, ways, i).astype(jnp.bfloat16)
            if i < CUTS:
                sent[zs, cuts[i]] = total
            else:
                sent_g[zs] = total
            second_copy(zs, step, i).start()

    def send_back(k, inner):
        zs = place(k)

        @pl.when(zs > z)
        def _():
            pass_on(zs, [1] if inner else [], 1)

        @pl.when(zs < z)
        def _():
            pass_on(zs, [0] if inner else [], -1)

    def conclude(ways):
        for i in ORDER:
            total = summed(z, ways, i)
            if i < CUTS:
                out_ref[cuts[i], :] = total.astype(jnp.bfloat16)
            else:
                for k in range(ids_ref.shape[0]):
                    picked = jnp.where(item == ids_ref[k:k + 1, :], total, 0.0)
                    gw_ref[k:k + 1, :] = jnp.sum(picked, axis=0, keepdims=True).astype(jnp.bfloat16)

    def own_rest(inward):
        @pl.when(low_half)
        def _():
            along_z(KINDS[3], z, inward).start()

        @pl.when(jnp.logical_not(low_half))
        def _():
            along_z(KINDS[3], z, -inward).start()

    over_x(0).start()
    for kind in KINDS[:3]:
        each_z(kind, z, start)
    at_ends(each_z, KINDS[3], z, start)
    inside(own_rest, -1)
    for i in range(1, len(crossing)):
        over_x(i).start()
    for kind in KINDS:
        to_core(kind, z).start()

    def block_here(k):
        for kind in KINDS:
            arrived(kind, place(k), other_c)

    steps = (0, early, middle, relayed)

    def units_here(step):
        for i in range(steps[step], steps[step + 1]):
            over_y(i).wait_recv()
        if step == 2:
            for i in range(relayed, len(crossing)):
                over_x(i).wait_recv()

    far = n_ep - 1
    start_events = [
        ((0, 0, 0), [(block_here, 0)]),
        ((0, 0, 1), []),
    ]
    end_plan = start_events + [
        ((1, 0, 0), [
            (relay, 0), (take, 1, 0, 1), (relay, 1), (take, 1, 2), (relay, 2),
            (take, 1, 3), (relay, 3), (block_here, 1),
        ]),
        ((1, 0, 1), [(relay, 4)]),
        ((0, 1, 0), [
            (take, far - 1, 0, 1), (relay, 5), (relay, 6),
            (units_here, 0), (take, far, 0, 1), (relay, 7),
        ]),
        ((1, 1, 0), []),
        ((far, 0, 0), [
            (relay, 8), (take, far, 2), (relay, 9), (take, far, 3),
            (block_here, far),
        ]),
        ((far, 0, 1), [(relay, 10), (take, far - 1, 2)]),
        ((far, 1, 0), []),
        ((far, 1, 2), [(units_here, 1)]),
        ((1, 1, 2), [(take, far - 1, 3)]),
        ((far, 1, 3), [(units_here, 2)]),
        ((far - 1, 0, 0), [(block_here, far - 1)]),
        ((far - 1, 0, 1), []), ((far - 1, 1, 0), []), ((far - 1, 1, 2), []),
        ((far - 1, 1, 3), []), ((1, 1, 3), []), ((0, 1, 1), []),
    ]
    inner_plan = start_events + [
        ((1, 0, 0), [
            (relay, 0), (take, 1, 0, 1), (take, far - 1, 0, 1), (relay, 1),
            (take, 1, 2), (relay, 2), (take, 1, 3), (own_rest, 1), (relay, 3),
            (block_here, 1),
        ]),
        ((1, 0, 1), [(take, far, 0, 1), (relay, 4)]),
        ((0, 1, 0), [
            (take, far, 2), (relay, 5), (take, far, 3), (take, far - 1, 2),
            (relay, 6), (units_here, 0), (take, far - 1, 3), (relay, 7),
        ]),
        ((1, 1, 0), []),
        ((far - 1, 0, 0), [(block_here, far - 1), (relay, 8)]),
        ((far - 1, 0, 1), []),
        ((far - 1, 1, 0), [(relay, 9)]),
        ((far, 0, 0), [(block_here, far)]),
        ((far, 0, 1), [(relay, 10)]),
        ((far, 1, 0), []),
        ((far, 1, 2), [(units_here, 1)]),
        ((far - 1, 1, 2), []), ((1, 1, 2), []),
        ((far, 1, 3), [(units_here, 2)]),
        ((far - 1, 1, 3), []), ((1, 1, 3), []), ((0, 1, 1), []),
    ]

    def run_events(acts):
        for act, *args in acts:
            act(*args)

    def turn(i, carry):
        for plan, role in ((end_plan, sides == 0), (inner_plan, sides > 0)):
            for at, (task, acts) in enumerate(plan):
                if acts:
                    @pl.when(jnp.logical_and(role, i == at))
                    def _(acts=acts):
                        run_events(acts)

        k, e, j = (
            jnp.where(sides == 0, *(pick(i, [task[field] for task, acts in plan])
                                    for plan in (end_plan, inner_plan)))
            for field in range(3)
        )

        @pl.when(j < 2)
        def _():
            compute(place(k), e, j, (0, 1))

        for half in range(2):
            @pl.when(j == 2 + half)
            def _(half=half):
                compute(place(k), e, 1, (half,))

        whole = jnp.logical_and(k == 0, jnp.logical_and(e == 1, j == 1))

        @pl.when(jnp.logical_or(j == 3, whole))
        def _():
            finish(place(k))

        for at, (task, acts) in enumerate(end_plan):
            if task[2] == 3:
                @pl.when(jnp.logical_and(i == at + 1, sides == 0))
                def _(task=task):
                    send_back(task[0], False)

        return carry

    assert len(end_plan) == len(inner_plan)
    lax.fori_loop(0, len(end_plan), turn, 0)

    @pl.when(sides > 0)
    def _():
        for k in [n_ep - 1] + list(range(1, n_ep - 1)):
            send_back(k, True)

    def drain(zs, carry):
        for kind in KINDS:
            each_z(kind, zs, wait_send)
            to_core(kind, zs).wait_send()
        for i in range(CUTS + 1):
            first_copy(zs, i).wait_send()
        return carry

    def drain_back(zs, carry):
        @pl.when(zs != z)
        def _():
            for i in range(CUTS + 1):
                second_copy(zs, 1, i).wait_send()

        return carry

    for i in range(len(crossing)):
        over_x(i).wait_send()
    for i in range(relayed):
        over_y(i).wait_send()
    lax.fori_loop(0, n_ep, drain, 0)

    @pl.when(sides > 0)
    def _():
        lax.fori_loop(0, n_ep, drain_back, 0)
        conclude([1, 0])

    @pl.when(z == 0)
    def _():
        conclude([0])

    @pl.when(z == n_ep - 1)
    def _():
        conclude([1])

    @pl.when(sides == 0)
    def _():
        lax.fori_loop(0, n_ep, drain_back, 0)


def swap_plan(tokens, cotangent, expert_ids, route_weights, w_gate, w_up, w_down):
    n_grp, n_ep = lax.axis_size("grp"), lax.axis_size("ep")
    named = gw_rows(n_grp * n_ep)
    rows, width = tokens.shape
    unit = w_gate.shape[2] // QUARTERS
    any_ref, vmem = pl.BlockSpec(memory_space=pl.ANY), pl.BlockSpec(memory_space=pltpu.VMEM)
    bf16, f32, dma = jnp.bfloat16, jnp.float32, pltpu.SemaphoreType.DMA
    pieces = 3 * PIECES + PIECES // 4
    grad_tokens, grad_weights = pl.pallas_call(
        functools.partial(swap_kernel, n_grp, n_ep),
        out_shape=(
            pltpu.VMEM((rows, width), bf16),
            pltpu.VMEM(expert_ids.shape[::-1], bf16),
        ),
        in_specs=[any_ref] * 7,
        out_specs=(vmem, vmem),
        scratch_shapes=[
            pltpu.VMEM(expert_ids.shape[::-1], jnp.int32),
            pltpu.VMEM(route_weights.shape[::-1], f32),
            pltpu.VMEM((n_ep, CORES, rows, width), bf16),
            pltpu.VMEM((n_ep, CORES, rows, width), bf16),
            pltpu.VMEM((n_ep, CORES, 2 * named, LANES), bf16),
            pltpu.VMEM((2, 2, width, 4 * unit), bf16),
            pltpu.VMEM((2, 2, 2 * unit, width), bf16),
            pltpu.VMEM((n_ep, CORES, rows, width), f32),
            pltpu.VMEM((n_ep, 2, CORES * rows, LANES), f32),
            pltpu.VMEM((n_ep, rows, width), bf16),
            pltpu.VMEM((n_ep, named, LANES), bf16),
            pltpu.VMEM((n_ep, rows, width), bf16),
            pltpu.VMEM((n_ep, named, LANES), bf16),
            pltpu.VMEM((n_ep, rows, width), bf16),
            pltpu.VMEM((n_ep, named, LANES), bf16),
            pltpu.VMEM((2, n_ep, rows, width), bf16),
            pltpu.VMEM((2, n_ep, named, LANES), bf16),
            pltpu.VMEM((n_ep, CORES, named, LANES), bf16),
            dma((4 + 3 * QUARTERS,)), dma((4, n_ep, CORES)), dma((4, n_ep, 2)), dma((4, n_ep)),
            dma((pieces,)), dma((pieces,)), dma((pieces,)), dma((pieces,)),
            dma((n_ep, CUTS + 1)), dma((n_ep, CUTS + 1)),
            dma((n_ep, CUTS + 1)), dma((2, n_ep, CUTS + 1)),
        ],
        compiler_params=pltpu.CompilerParams(
            collective_id=0, has_side_effects=True, vmem_limit_bytes=VMEM_ROOM
        ),
    )(tokens, cotangent, expert_ids.T, route_weights.T, w_gate, w_up, w_down)
    return grad_tokens, grad_weights.T


def on_device(tokens, cotangent, expert_ids, route_weights, w_gate, w_up, w_down):
    n_grp, n_ep = lax.axis_size("grp"), lax.axis_size("ep")
    rows, width = tokens.shape
    swaps = lax.axis_size("parts") == 2 and n_grp == 2 * CORES and n_ep == 4
    fits = rows == LANES and width % LANES == 0 and w_gate.shape[2] == QUARTERS * LANES
    held = 2 * (w_gate.size + w_up.size + w_down.size) * 2 + n_ep * rows * width * 28
    plan = swap_plan if swaps and fits and held <= VMEM_ROOM else dispatch_plan
    return plan(tokens, cotangent, expert_ids, route_weights, w_gate, w_up, w_down)


def solution(mesh):
    in_specs = (
        P(("parts", "grp", "ep"), None),
        P(("parts", "grp", "ep"), None),
        P(("parts", "grp", "ep"), None),
        P(("parts", "grp", "ep"), None),
        P(("grp", "ep"), None, None),
        P(("grp", "ep"), None, None),
        P(("grp", "ep"), None, None),
    )
    out_specs = (P(("parts", "grp", "ep"), None), P(("parts", "grp", "ep"), None))
    return jax.shard_map(
        on_device, mesh=mesh, in_specs=in_specs, out_specs=out_specs, check_vma=False
    )
```

```python
import functools

import jax
import jax.numpy as jnp
from jax import lax
from jax.experimental import pallas as pl
from jax.experimental.pallas import tpu as pltpu
from jax.sharding import PartitionSpec as P

LANES = 128
CORES = 2
VMEM_ROOM = 56 * 1024 * 1024


def expert_grads(rows_in, grads_in, w_gate, w_up, w_down):
    contract = (((1,), (1,)), ((), ()))
    gate_pre = jnp.dot(rows_in, w_gate, preferred_element_type=jnp.float32)
    up_pre = jnp.dot(rows_in, w_up, preferred_element_type=jnp.float32)
    hidden_grad = lax.dot_general(grads_in, w_down, contract, preferred_element_type=jnp.float32)
    sigmoid_gate = jax.nn.sigmoid(gate_pre)
    activation = gate_pre * sigmoid_gate
    hidden = activation * up_pre
    weight_grad = jnp.sum(hidden_grad * hidden, axis=-1).astype(jnp.bfloat16)
    grad_up = (hidden_grad * activation).astype(jnp.bfloat16)
    grad_gate = (
        hidden_grad * up_pre * sigmoid_gate * (1.0 + gate_pre * (1.0 - sigmoid_gate))
    ).astype(jnp.bfloat16)
    row_terms = (
        lax.dot_general(grad_gate, w_gate, contract, preferred_element_type=jnp.float32)
        + lax.dot_general(grad_up, w_up, contract, preferred_element_type=jnp.float32)
    ).astype(jnp.bfloat16)
    return (row_terms, weight_grad)


def slot_plan(routes, experts, capacity):
    tok_rows, top_count = routes.shape
    flat_ids = routes.reshape(-1)
    pad_pair = flat_ids.shape[0]
    pair_ids = jnp.arange(pad_pair, dtype=jnp.int32)
    sort_order = jnp.argsort(flat_ids, stable=True)
    sorted_ids = flat_ids[sort_order]
    onehot = (flat_ids[:, None] == jnp.arange(experts, dtype=jnp.int32)[None, :]).astype(jnp.int32)
    counts = jnp.sum(onehot, axis=0)
    earlier = jnp.tri(experts, k=-1, dtype=jnp.int32)
    starts = jnp.sum(earlier * counts[None, :], axis=1)
    sorted_rank = pair_ids - starts[sorted_ids]
    sorted_slot = sorted_ids * capacity + sorted_rank
    slot_of_pair = jnp.zeros((pad_pair,), jnp.int32).at[sort_order].set(sorted_slot)
    slot_pair = jnp.full((experts * capacity,), pad_pair, jnp.int32).at[sorted_slot].set(sort_order)
    slot_token = jnp.where(slot_pair < pad_pair, slot_pair // top_count, tok_rows)
    return (slot_of_pair, slot_token, slot_pair)


def place_rows(source_rows, slot_token):
    padded = jnp.concatenate(
        [source_rows, jnp.zeros((1, source_rows.shape[1]), source_rows.dtype)], 0
    )
    return padded[slot_token]


def dispatch_plan(tokens, cotangent, expert_ids, route_weights, w_gate, w_up, w_down):
    group_count = lax.axis_size("grp")
    lane_count = lax.axis_size("ep")
    experts = group_count * lane_count
    tok_rows, top_count = expert_ids.shape
    model_width = tokens.shape[1]
    capacity = 2 * tok_rows * top_count // experts
    slot_of_pair, slot_token, unused_pairs = slot_plan(expert_ids, experts, capacity)
    send_rows = place_rows(tokens, slot_token).reshape(
        group_count, lane_count, capacity, model_width
    )
    send_grads = place_rows(cotangent, slot_token).reshape(
        group_count, lane_count, capacity, model_width
    )
    send_rows, send_grads = (
        lax.all_to_all(send_rows, "grp", split_axis=0, concat_axis=0, tiled=True),
        lax.all_to_all(send_grads, "grp", split_axis=0, concat_axis=0, tiled=True),
    )
    rows_in = lax.all_to_all(send_rows, "ep", split_axis=1, concat_axis=1, tiled=True)
    grads_in = lax.all_to_all(send_grads, "ep", split_axis=1, concat_axis=1, tiled=True)
    leading = rows_in.shape[:3]
    row_terms, weight_grad = expert_grads(
        rows_in.reshape(-1, model_width),
        grads_in.reshape(-1, model_width),
        w_gate[0],
        w_up[0],
        w_down[0],
    )
    row_terms = row_terms.reshape(leading + (model_width,))
    weight_grad = weight_grad.reshape(leading)
    row_terms, weight_grad = (
        lax.all_to_all(row_terms, "ep", split_axis=1, concat_axis=1, tiled=True),
        lax.all_to_all(weight_grad, "ep", split_axis=1, concat_axis=1, tiled=True),
    )
    row_terms, weight_grad = (
        lax.all_to_all(row_terms, "grp", split_axis=0, concat_axis=0, tiled=True),
        lax.all_to_all(weight_grad, "grp", split_axis=0, concat_axis=0, tiled=True),
    )
    row_terms = row_terms.reshape(experts * capacity, model_width)
    weight_grad = weight_grad.reshape(experts * capacity)
    picked = row_terms[slot_of_pair].reshape(tok_rows, top_count, model_width)
    grad_tokens = jnp.sum(route_weights[:, :, None] * picked.astype(jnp.float32), axis=1)
    grad_weights = weight_grad[slot_of_pair].reshape(tok_rows, top_count)
    return (grad_tokens.astype(jnp.bfloat16), grad_weights)


CUTS = 4
ORDER = tuple(range(CUTS - 1)) + (CUTS, CUTS - 1)
PIECES = 4
QUARTERS = 4
KINDS = (0, 1, 2, 3)


def gw_rows(experts):
    return -(-experts // 16) * 16


def pick(index, values):
    chosen = jnp.int32(values[0])
    for at in range(1, len(values)):
        if values[at] != values[at - 1]:
            chosen = jnp.where(index >= at, jnp.int32(values[at]), chosen)
    return chosen


def swap_kernel(
    n_grp, n_ep, tok_hbm, cot_hbm, ids_hbm, route_hbm, wg_hbm, wu_hbm, wd_hbm,
    out_ref, gw_ref,
    ids_ref, route_ref, tok, cot, rts, wgu, wdn, acc, sums, parts, parts_g, r1, r1_g, sent, sent_g, up, up_g, pair_g,
    load_sem, got_sem, z_sem, c_sem, wx_s, wx_r, wy_s, wy_r,
    s1_sem, r1_sem, s2_sem, r2_sem,
):
    rows, width = out_ref.shape
    unit = wgu.shape[3] // QUARTERS
    named = gw_rows(n_grp * n_ep)
    p, g, z = lax.axis_index("parts"), lax.axis_index("grp"), lax.axis_index("ep")
    x, c = g // CORES, g % CORES
    other_c = 1 - c
    experts = (g * n_ep + z, ((1 - x) * CORES + c) * n_ep + z)
    core_peer = {"parts": p, "grp": x * CORES + other_c, "ep": z}
    x_peer = {"parts": p, "grp": (1 - x) * CORES + c, "ep": z}
    y_peer = {"parts": 1 - p, "grp": g, "ep": z}

    def z_peer(step):
        return {"parts": p, "grp": g, "ep": z + step}

    barrier = pltpu.get_barrier_semaphore()

    def greet(peer):
        pl.semaphore_signal(barrier, inc=1, device_id=peer, device_id_type=pl.DeviceIdType.MESH)

    for peer in (core_peer, x_peer, y_peer):
        greet(peer)

    @pl.when(z > 0)
    def _():
        greet(z_peer(-1))

    @pl.when(z < n_ep - 1)
    def _():
        greet(z_peer(1))

    small = [
        pltpu.make_async_copy(ids_hbm, ids_ref, load_sem.at[2 + 3 * QUARTERS]),
        pltpu.make_async_copy(route_hbm, route_ref, load_sem.at[3 + 3 * QUARTERS]),
    ]
    for load in small:
        load.start()
    loads = [
        pltpu.make_async_copy(tok_hbm, tok.at[z, c], load_sem.at[0]),
        pltpu.make_async_copy(cot_hbm, cot.at[z, c], load_sem.at[1]),
    ]
    for q in range(QUARTERS):
        span = pl.ds(q * unit, unit)
        for i, (source, target) in enumerate((
            (wg_hbm.at[0, :, span], wgu.at[0, q // 2, :, pl.ds(q % 2 * 2 * unit, unit)]),
            (wu_hbm.at[0, :, span], wgu.at[0, q // 2, :, pl.ds((q % 2 * 2 + 1) * unit, unit)]),
            (wd_hbm.at[0, span, :], wdn.at[0, q // 2, pl.ds(q % 2 * unit, unit)]),
        )):
            loads.append(pltpu.make_async_copy(source, target, load_sem.at[2 + 3 * q + i]))
    for load in loads:
        load.start()

    acc[...] = jnp.zeros_like(acc)
    sums[...] = jnp.zeros_like(sums)
    for load in small:
        load.wait()
    item = lax.broadcasted_iota(jnp.int32, (named, LANES), 0)
    routed = jnp.zeros((named, LANES), jnp.float32)
    for k in range(ids_ref.shape[0]):
        routed += jnp.where(item == ids_ref[k:k + 1, :], route_ref[k:k + 1, :], 0.0)
    high = routed.astype(jnp.bfloat16)
    rts[z, c, 0:named, :] = high
    rts[z, c, named:2 * named, :] = (routed - high.astype(jnp.float32)).astype(jnp.bfloat16)

    for load in loads:
        load.wait()
    near = jnp.where(z > 0, 1, 0) + jnp.where(z < n_ep - 1, 1, 0)
    pl.semaphore_wait(barrier, 3 + near)

    def remote(source, target, send, recv, peer):
        return pltpu.make_async_remote_copy(
            src_ref=source, dst_ref=target, send_sem=send, recv_sem=recv,
            device_id=peer, device_id_type=pl.DeviceIdType.MESH,
        )

    sides = jnp.minimum(z, n_ep - 1 - z)

    low_half = 2 * z < n_ep - 1

    def place(k):
        step = jnp.where(k % 2 == 1, -((k + 1) // 2), k // 2)
        near_k = jnp.where(low_half, z + step, z - step)
        far_k = jnp.where(low_half, k, n_ep - 1 - k)
        return jnp.where(k <= 2 * sides, near_k, far_k)

    part = rows // 2

    def block(kind, zs, cs):
        if kind == 0:
            return tok.at[zs, cs]
        if kind == 1:
            return rts.at[zs, cs]
        return cot.at[zs, cs, pl.ds((kind - 2) * part, part)]

    def along_z(kind, zs, step):
        here = block(kind, zs, c)
        return remote(here, here, z_sem.at[kind, zs, (step + 1) // 2], got_sem.at[kind, zs, c],
                      z_peer(step))

    def to_core(kind, zs):
        here = block(kind, zs, c)
        return remote(here, here, c_sem.at[kind, zs], got_sem.at[kind, zs, c], core_peer)

    def arrived(kind, zs, cs):
        here = block(kind, zs, cs)
        remote(here, here, c_sem.at[kind, zs], got_sem.at[kind, zs, cs], core_peer).wait_recv()

    def each_z(kind, zs, act):
        @pl.when(jnp.logical_and(zs <= z, z < n_ep - 1))
        def _():
            act(along_z(kind, zs, 1))

        @pl.when(jnp.logical_and(zs >= z, z > 0))
        def _():
            act(along_z(kind, zs, -1))

    def start(copy):
        copy.start()

    def wait_send(copy):
        copy.wait_send()

    def take(k, *group):
        zs = place(k)
        for kind in group:
            arrived(kind, zs, c)
            each_z(kind, zs, start)
            to_core(kind, zs).start()

    def at_ends(act, *args):
        @pl.when(sides == 0)
        def _():
            act(*args)

    def inside(act, *args):
        @pl.when(sides > 0)
        def _():
            act(*args)

    downs = PIECES // 2
    tall, flat = width // PIECES, unit // downs

    def gate_up(e, j, h, at):
        lanes = pl.ds(pl.multiple_of(h * 2 * unit, 2 * unit), 2 * unit)
        return wgu.at[e, j, pl.ds(pl.multiple_of(at * tall, tall), tall), lanes]

    def down(e, j, h, at):
        return wdn.at[e, j, pl.ds(pl.multiple_of(h * unit + at * flat, flat), flat)]

    crossing = [(gate_up, 0, p, n) for n in range(PIECES)] + [(down, 0, p, n) for n in range(downs)]
    early = len(crossing)
    for h in range(2):
        crossing += [(gate_up, 1, h, p * downs + n) for n in range(downs)]
        crossing += [(down, 1, h, p * (downs // 2) + n) for n in range(downs // 2)]
    crossing += [(down, 1, 1, (1 - p) * (downs // 2) + n) for n in range(downs // 2)]
    middle, relayed = early + downs + downs // 2, len(crossing) - downs

    def piece(e, i):
        part, *place_of = crossing[i]
        return part(e, *place_of)

    def over_x(i):
        return remote(piece(0, i), piece(1, i), wx_s.at[i], wx_r.at[i], x_peer)

    def over_y(i):
        return remote(piece(1, i), piece(1, i), wy_s.at[i], wy_r.at[i], y_peer)

    def relay(i):
        over_x(i).wait_recv()
        over_y(i).start()

    contract = (((1,), (1,)), ((), ()))
    both = CORES * rows

    def scale_of(zs, expert):
        columns = []
        for cs in range(CORES):
            routes = rts[zs, cs, 0:named, :].astype(jnp.float32)
            routes += rts[zs, cs, named:2 * named, :].astype(jnp.float32)
            weight = jnp.sum(jnp.where(item == expert, routes, 0.0), axis=0, keepdims=True)
            columns.append(jnp.broadcast_to(weight, (rows, LANES)).T)
        return jnp.concatenate(columns, axis=0)

    def compute(zs, e, j, halves):
        expert = jnp.where(e == 0, experts[0], experts[1])
        scale = scale_of(zs, expert)
        rows_in = tok[zs].reshape(both, width)
        grads_in = cot[zs].reshape(both, width)
        low, high = halves[0] * unit, (halves[-1] + 1) * unit
        pres = jnp.dot(rows_in, wgu[e, j, :, 2 * low:2 * high], preferred_element_type=jnp.float32)
        hidden_grads = lax.dot_general(grads_in, wdn[e, j, low:high], contract,
                                       preferred_element_type=jnp.float32)
        lane_sums = jnp.zeros((both, LANES), jnp.float32)
        grads = []
        for at in range(len(halves)):
            gate_pre = pres[:, 2 * at * unit:(2 * at + 1) * unit]
            up_pre = pres[:, (2 * at + 1) * unit:(2 * at + 2) * unit]
            hidden_grad = hidden_grads[:, at * unit:(at + 1) * unit]
            sigmoid_gate = 1.0 / (1.0 + jnp.exp(-gate_pre))
            activation = gate_pre * sigmoid_gate
            lane_sums += hidden_grad * (activation * up_pre)
            hidden_grad = hidden_grad * scale
            grads.append((hidden_grad * up_pre * sigmoid_gate
                          * (1.0 + gate_pre * (1.0 - sigmoid_gate))).astype(jnp.bfloat16))
            grads.append((hidden_grad * activation).astype(jnp.bfloat16))
        sums[zs, e] += lane_sums
        terms = lax.dot_general(jnp.concatenate(grads, axis=1), wgu[e, j, :, 2 * low:2 * high],
                                contract, preferred_element_type=jnp.float32)
        acc[zs] += terms.reshape(CORES, rows, width)

    cut_rows = rows // CUTS
    cuts = [pl.ds(i * cut_rows, cut_rows) for i in range(CUTS)]

    def first_copy(zs, i):
        if i < CUTS:
            source, target = parts.at[zs, cuts[i]], r1.at[zs, cuts[i]]
        else:
            source, target = parts_g.at[zs], r1_g.at[zs]
        return remote(source, target, s1_sem.at[zs, i], r1_sem.at[zs, i], core_peer)

    def second_copy(zs, step, i):
        way = (step + 1) // 2
        if i < CUTS:
            source, target = sent.at[zs, cuts[i]], up.at[way, zs, cuts[i]]
        else:
            source, target = sent_g.at[zs], up_g.at[way, zs]
        return remote(source, target, s2_sem.at[zs, i], r2_sem.at[way, zs, i], z_peer(step))

    def finish(zs):
        parts[zs] = acc[zs, other_c].astype(jnp.bfloat16)
        for i in range(CUTS):
            first_copy(zs, i).start()
        lanes = sums[zs].reshape(2 * both, LANES)
        high = lanes.astype(jnp.bfloat16)
        low = (lanes - high.astype(jnp.float32)).astype(jnp.bfloat16)
        ones = jnp.ones((16, LANES), jnp.bfloat16)
        totals = lax.dot_general(ones, high, contract, preferred_element_type=jnp.float32)
        totals += lax.dot_general(ones, low, contract, preferred_element_type=jnp.float32)
        for cs in range(CORES):
            found = jnp.zeros((named, LANES), jnp.float32)
            for e in range(2):
                at = e * both + cs * rows
                found += jnp.where(item == experts[e], totals[0:1, at:at + rows], 0.0)
            pair_g[zs, cs] = found.astype(jnp.bfloat16)
        parts_g[zs] = pair_g[zs, other_c]
        first_copy(zs, CUTS).start()

    def summed(zs, ways, i):
        first_copy(zs, i).wait_recv()
        for way in ways:
            second_copy(zs, 2 * way - 1, i).wait_recv()
        if i < CUTS:
            total = acc[zs, c, cuts[i]] + r1[zs, cuts[i]].astype(jnp.float32)
            for way in ways:
                total += up[way, zs, cuts[i]].astype(jnp.float32)
            return total
        total = pair_g[zs, c].astype(jnp.float32) + r1_g[zs].astype(jnp.float32)
        for way in ways:
            total += up_g[way, zs].astype(jnp.float32)
        return total

    def pass_on(zs, ways, step):
        for i in ORDER:
            total = summed(zs, ways, i).astype(jnp.bfloat16)
            if i < CUTS:
                sent[zs, cuts[i]] = total
            else:
                sent_g[zs] = total
            second_copy(zs, step, i).start()

    def send_back(k, inner):
        zs = place(k)

        @pl.when(zs > z)
        def _():
            pass_on(zs, [1] if inner else [], 1)

        @pl.when(zs < z)
        def _():
            pass_on(zs, [0] if inner else [], -1)

    def conclude(ways):
        for i in ORDER:
            total = summed(z, ways, i)
            if i < CUTS:
                out_ref[cuts[i], :] = total.astype(jnp.bfloat16)
            else:
                for k in range(ids_ref.shape[0]):
                    picked = jnp.where(item == ids_ref[k:k + 1, :], total, 0.0)
                    gw_ref[k:k + 1, :] = jnp.sum(picked, axis=0, keepdims=True).astype(jnp.bfloat16)

    def own_rest(inward):
        @pl.when(low_half)
        def _():
            along_z(KINDS[3], z, inward).start()

        @pl.when(jnp.logical_not(low_half))
        def _():
            along_z(KINDS[3], z, -inward).start()

    over_x(0).start()
    for kind in KINDS[:3]:
        each_z(kind, z, start)
    at_ends(each_z, KINDS[3], z, start)
    inside(own_rest, -1)
    for i in range(1, len(crossing)):
        over_x(i).start()
    for kind in KINDS:
        to_core(kind, z).start()

    def block_here(k):
        for kind in KINDS:
            arrived(kind, place(k), other_c)

    steps = (0, early, middle, relayed)

    def units_here(step):
        for i in range(steps[step], steps[step + 1]):
            over_y(i).wait_recv()
        if step == 2:
            for i in range(relayed, len(crossing)):
                over_x(i).wait_recv()

    far = n_ep - 1
    start_events = [
        ((0, 0, 0), [(block_here, 0)]),
        ((0, 0, 1), []),
    ]
    end_plan = start_events + [
        ((1, 0, 0), [
            (relay, 0), (take, 1, 0, 1), (relay, 1), (take, 1, 2), (relay, 2),
            (take, 1, 3), (relay, 3), (block_here, 1),
        ]),
        ((1, 0, 1), [(relay, 4)]),
        ((0, 1, 0), [
            (take, far - 1, 0, 1), (relay, 5), (relay, 6),
            (units_here, 0), (take, far, 0, 1), (relay, 7),
        ]),
        ((1, 1, 0), []),
        ((far, 0, 0), [
            (relay, 8), (take, far, 2), (relay, 9), (take, far, 3),
            (block_here, far),
        ]),
        ((far, 0, 1), [(relay, 10), (take, far - 1, 2)]),
        ((far, 1, 0), []),
        ((far, 1, 2), [(units_here, 1)]),
        ((1, 1, 2), []),
        ((0, 1, 2), [(take, far - 1, 3)]),
        ((far, 1, 3), [(units_here, 2)]),
        ((far - 1, 0, 0), [(block_here, far - 1)]),
        ((far - 1, 0, 1), []), ((far - 1, 1, 0), []), ((far - 1, 1, 1), []),
        ((1, 1, 3), []), ((0, 1, 3), []),
    ]
    inner_plan = start_events + [
        ((1, 0, 0), [
            (relay, 0), (take, 1, 0, 1), (take, far - 1, 0, 1), (relay, 1),
            (take, 1, 2), (relay, 2), (take, 1, 3), (own_rest, 1), (relay, 3),
            (block_here, 1),
        ]),
        ((1, 0, 1), [(take, far, 0, 1), (relay, 4)]),
        ((0, 1, 0), [
            (take, far, 2), (relay, 5), (take, far, 3), (take, far - 1, 2),
            (relay, 6), (units_here, 0), (take, far - 1, 3), (relay, 7),
        ]),
        ((1, 1, 0), []),
        ((far - 1, 0, 0), [(block_here, far - 1), (relay, 8)]),
        ((far - 1, 0, 1), []),
        ((far - 1, 1, 0), [(relay, 9)]),
        ((far, 0, 0), [(block_here, far)]),
        ((far, 0, 1), [(relay, 10)]),
        ((far, 1, 0), []),
        ((far, 1, 2), [(units_here, 1)]),
        ((1, 1, 2), []), ((0, 1, 2), []),
        ((far, 1, 3), [(units_here, 2)]),
        ((far - 1, 1, 1), []), ((1, 1, 3), []), ((0, 1, 3), []),
    ]

    def run_events(acts):
        for act, *args in acts:
            act(*args)

    def turn(i, carry):
        def step_of(plan, low, high):
            if high - low == 1:
                run_events(plan[low][1])
                return
            cut = (low + high) // 2
            for first_at, last_at, here in ((low, cut, i < cut), (cut, high, i >= cut)):
                if any(acts for task, acts in plan[first_at:last_at]):
                    @pl.when(here)
                    def _(first_at=first_at, last_at=last_at):
                        step_of(plan, first_at, last_at)

        at_ends(step_of, end_plan, 0, len(end_plan))
        inside(step_of, inner_plan, 0, len(inner_plan))

        k, e, j = (
            jnp.where(sides == 0, *(pick(i, [task[field] for task, acts in plan])
                                    for plan in (end_plan, inner_plan)))
            for field in range(3)
        )

        @pl.when(j < 2)
        def _():
            compute(place(k), e, j, (0, 1))

        for half in range(2):
            @pl.when(j == 2 + half)
            def _(half=half):
                compute(place(k), e, 1, (half,))

        tails = [(at, task) for at, (task, acts) in enumerate(end_plan)
                 if task[0] and task[1:] in ((1, 1), (1, 3))]

        @pl.when(jnp.logical_and(i > tails[0][0], sides == 0))
        def _():
            for at, task in tails:
                @pl.when(i == at + 1)
                def _(task=task):
                    send_back(task[0], False)

        whole = jnp.logical_and(e == 1, j == 1)

        @pl.when(jnp.logical_or(j == 3, whole))
        def _():
            finish(place(k))

        return carry

    assert len(end_plan) == len(inner_plan)
    lax.fori_loop(0, len(end_plan), turn, 0)

    @pl.when(sides > 0)
    def _():
        for k in [n_ep - 1] + list(range(1, n_ep - 1)):
            send_back(k, True)

    def drain(zs, carry):
        for kind in KINDS:
            each_z(kind, zs, wait_send)
            to_core(kind, zs).wait_send()
        for i in range(CUTS + 1):
            first_copy(zs, i).wait_send()
        return carry

    def drain_back(zs, carry):
        @pl.when(zs != z)
        def _():
            for i in range(CUTS + 1):
                second_copy(zs, 1, i).wait_send()

        return carry

    for i in range(len(crossing)):
        over_x(i).wait_send()
    for i in range(relayed):
        over_y(i).wait_send()
    lax.fori_loop(0, n_ep, drain, 0)

    @pl.when(sides > 0)
    def _():
        lax.fori_loop(0, n_ep, drain_back, 0)
        conclude([1, 0])

    @pl.when(z == 0)
    def _():
        conclude([0])

    @pl.when(z == n_ep - 1)
    def _():
        conclude([1])

    @pl.when(sides == 0)
    def _():
        lax.fori_loop(0, n_ep, drain_back, 0)


def swap_plan(tokens, cotangent, expert_ids, route_weights, w_gate, w_up, w_down):
    n_grp, n_ep = lax.axis_size("grp"), lax.axis_size("ep")
    named = gw_rows(n_grp * n_ep)
    rows, width = tokens.shape
    unit = w_gate.shape[2] // QUARTERS
    any_ref, vmem = pl.BlockSpec(memory_space=pl.ANY), pl.BlockSpec(memory_space=pltpu.VMEM)
    bf16, f32, dma = jnp.bfloat16, jnp.float32, pltpu.SemaphoreType.DMA
    pieces = 3 * PIECES + PIECES // 4
    grad_tokens, grad_weights = pl.pallas_call(
        functools.partial(swap_kernel, n_grp, n_ep),
        out_shape=(
            pltpu.VMEM((rows, width), bf16),
            pltpu.VMEM(expert_ids.shape[::-1], bf16),
        ),
        in_specs=[any_ref] * 7,
        out_specs=(vmem, vmem),
        scratch_shapes=[
            pltpu.VMEM(expert_ids.shape[::-1], jnp.int32),
            pltpu.VMEM(route_weights.shape[::-1], f32),
            pltpu.VMEM((n_ep, CORES, rows, width), bf16),
            pltpu.VMEM((n_ep, CORES, rows, width), bf16),
            pltpu.VMEM((n_ep, CORES, 2 * named, LANES), bf16),
            pltpu.VMEM((2, 2, width, 4 * unit), bf16),
            pltpu.VMEM((2, 2, 2 * unit, width), bf16),
            pltpu.VMEM((n_ep, CORES, rows, width), f32),
            pltpu.VMEM((n_ep, 2, CORES * rows, LANES), f32),
            pltpu.VMEM((n_ep, rows, width), bf16),
            pltpu.VMEM((n_ep, named, LANES), bf16),
            pltpu.VMEM((n_ep, rows, width), bf16),
            pltpu.VMEM((n_ep, named, LANES), bf16),
            pltpu.VMEM((n_ep, rows, width), bf16),
            pltpu.VMEM((n_ep, named, LANES), bf16),
            pltpu.VMEM((2, n_ep, rows, width), bf16),
            pltpu.VMEM((2, n_ep, named, LANES), bf16),
            pltpu.VMEM((n_ep, CORES, named, LANES), bf16),
            dma((4 + 3 * QUARTERS,)), dma((4, n_ep, CORES)), dma((4, n_ep, 2)), dma((4, n_ep)),
            dma((pieces,)), dma((pieces,)), dma((pieces,)), dma((pieces,)),
            dma((n_ep, CUTS + 1)), dma((n_ep, CUTS + 1)),
            dma((n_ep, CUTS + 1)), dma((2, n_ep, CUTS + 1)),
        ],
        compiler_params=pltpu.CompilerParams(
            collective_id=0, has_side_effects=True, vmem_limit_bytes=VMEM_ROOM
        ),
    )(tokens, cotangent, expert_ids.T, route_weights.T, w_gate, w_up, w_down)
    return grad_tokens, grad_weights.T


def on_device(tokens, cotangent, expert_ids, route_weights, w_gate, w_up, w_down):
    n_grp, n_ep = lax.axis_size("grp"), lax.axis_size("ep")
    rows, width = tokens.shape
    swaps = lax.axis_size("parts") == 2 and n_grp == 2 * CORES and n_ep == 4
    fits = rows == LANES and width % LANES == 0 and w_gate.shape[2] == QUARTERS * LANES
    held = 2 * (w_gate.size + w_up.size + w_down.size) * 2 + n_ep * rows * width * 28
    plan = swap_plan if swaps and fits and held <= VMEM_ROOM else dispatch_plan
    return plan(tokens, cotangent, expert_ids, route_weights, w_gate, w_up, w_down)


def solution(mesh):
    in_specs = (
        P(("parts", "grp", "ep"), None),
        P(("parts", "grp", "ep"), None),
        P(("parts", "grp", "ep"), None),
        P(("parts", "grp", "ep"), None),
        P(("grp", "ep"), None, None),
        P(("grp", "ep"), None, None),
        P(("grp", "ep"), None, None),
    )
    out_specs = (P(("parts", "grp", "ep"), None), P(("parts", "grp", "ep"), None))
    return jax.shard_map(
        on_device, mesh=mesh, in_specs=in_specs, out_specs=out_specs, check_vma=False
    )
```

```python
import functools

import jax
import jax.numpy as jnp
from jax import lax
from jax.experimental import pallas as pl
from jax.experimental.pallas import tpu as pltpu
from jax.sharding import PartitionSpec as P

LANES = 128
CORES = 2
VMEM_ROOM = 56 * 1024 * 1024


def expert_grads(rows_in, grads_in, w_gate, w_up, w_down):
    contract = (((1,), (1,)), ((), ()))
    gate_pre = jnp.dot(rows_in, w_gate, preferred_element_type=jnp.float32)
    up_pre = jnp.dot(rows_in, w_up, preferred_element_type=jnp.float32)
    hidden_grad = lax.dot_general(grads_in, w_down, contract, preferred_element_type=jnp.float32)
    sigmoid_gate = jax.nn.sigmoid(gate_pre)
    activation = gate_pre * sigmoid_gate
    hidden = activation * up_pre
    weight_grad = jnp.sum(hidden_grad * hidden, axis=-1).astype(jnp.bfloat16)
    grad_up = (hidden_grad * activation).astype(jnp.bfloat16)
    grad_gate = (
        hidden_grad * up_pre * sigmoid_gate * (1.0 + gate_pre * (1.0 - sigmoid_gate))
    ).astype(jnp.bfloat16)
    row_terms = (
        lax.dot_general(grad_gate, w_gate, contract, preferred_element_type=jnp.float32)
        + lax.dot_general(grad_up, w_up, contract, preferred_element_type=jnp.float32)
    ).astype(jnp.bfloat16)
    return (row_terms, weight_grad)


def slot_plan(routes, experts, capacity):
    tok_rows, top_count = routes.shape
    flat_ids = routes.reshape(-1)
    pad_pair = flat_ids.shape[0]
    pair_ids = jnp.arange(pad_pair, dtype=jnp.int32)
    sort_order = jnp.argsort(flat_ids, stable=True)
    sorted_ids = flat_ids[sort_order]
    onehot = (flat_ids[:, None] == jnp.arange(experts, dtype=jnp.int32)[None, :]).astype(jnp.int32)
    counts = jnp.sum(onehot, axis=0)
    earlier = jnp.tri(experts, k=-1, dtype=jnp.int32)
    starts = jnp.sum(earlier * counts[None, :], axis=1)
    sorted_rank = pair_ids - starts[sorted_ids]
    sorted_slot = sorted_ids * capacity + sorted_rank
    slot_of_pair = jnp.zeros((pad_pair,), jnp.int32).at[sort_order].set(sorted_slot)
    slot_pair = jnp.full((experts * capacity,), pad_pair, jnp.int32).at[sorted_slot].set(sort_order)
    slot_token = jnp.where(slot_pair < pad_pair, slot_pair // top_count, tok_rows)
    return (slot_of_pair, slot_token, slot_pair)


def place_rows(source_rows, slot_token):
    padded = jnp.concatenate(
        [source_rows, jnp.zeros((1, source_rows.shape[1]), source_rows.dtype)], 0
    )
    return padded[slot_token]


def dispatch_plan(tokens, cotangent, expert_ids, route_weights, w_gate, w_up, w_down):
    group_count = lax.axis_size("grp")
    lane_count = lax.axis_size("ep")
    experts = group_count * lane_count
    tok_rows, top_count = expert_ids.shape
    model_width = tokens.shape[1]
    capacity = 2 * tok_rows * top_count // experts
    slot_of_pair, slot_token, unused_pairs = slot_plan(expert_ids, experts, capacity)
    send_rows = place_rows(tokens, slot_token).reshape(
        group_count, lane_count, capacity, model_width
    )
    send_grads = place_rows(cotangent, slot_token).reshape(
        group_count, lane_count, capacity, model_width
    )
    send_rows, send_grads = (
        lax.all_to_all(send_rows, "grp", split_axis=0, concat_axis=0, tiled=True),
        lax.all_to_all(send_grads, "grp", split_axis=0, concat_axis=0, tiled=True),
    )
    rows_in = lax.all_to_all(send_rows, "ep", split_axis=1, concat_axis=1, tiled=True)
    grads_in = lax.all_to_all(send_grads, "ep", split_axis=1, concat_axis=1, tiled=True)
    leading = rows_in.shape[:3]
    row_terms, weight_grad = expert_grads(
        rows_in.reshape(-1, model_width),
        grads_in.reshape(-1, model_width),
        w_gate[0],
        w_up[0],
        w_down[0],
    )
    row_terms = row_terms.reshape(leading + (model_width,))
    weight_grad = weight_grad.reshape(leading)
    row_terms, weight_grad = (
        lax.all_to_all(row_terms, "ep", split_axis=1, concat_axis=1, tiled=True),
        lax.all_to_all(weight_grad, "ep", split_axis=1, concat_axis=1, tiled=True),
    )
    row_terms, weight_grad = (
        lax.all_to_all(row_terms, "grp", split_axis=0, concat_axis=0, tiled=True),
        lax.all_to_all(weight_grad, "grp", split_axis=0, concat_axis=0, tiled=True),
    )
    row_terms = row_terms.reshape(experts * capacity, model_width)
    weight_grad = weight_grad.reshape(experts * capacity)
    picked = row_terms[slot_of_pair].reshape(tok_rows, top_count, model_width)
    grad_tokens = jnp.sum(route_weights[:, :, None] * picked.astype(jnp.float32), axis=1)
    grad_weights = weight_grad[slot_of_pair].reshape(tok_rows, top_count)
    return (grad_tokens.astype(jnp.bfloat16), grad_weights)


CUTS = 2
ORDER = tuple(range(CUTS - 1)) + (CUTS, CUTS - 1)
PIECES = 4
QUARTERS = 4
KINDS = (0, 1, 2, 3)


def gw_rows(experts):
    return -(-experts // 16) * 16


def pick(index, values):
    chosen = jnp.int32(values[0])
    for at in range(1, len(values)):
        if values[at] != values[at - 1]:
            chosen = jnp.where(index >= at, jnp.int32(values[at]), chosen)
    return chosen


def swap_kernel(
    n_grp, n_ep, tok_hbm, cot_hbm, ids_hbm, route_hbm, wg_hbm, wu_hbm, wd_hbm,
    out_ref, gw_ref,
    ids_ref, route_ref, tok, cot, rts, wgu, wdn, acc, sums, parts, parts_g, r1, r1_g, sent, sent_g, up, up_g, pair_g,
    load_sem, got_sem, z_sem, c_sem, wx_s, wx_r, wy_s, wy_r,
    s1_sem, r1_sem, s2_sem, r2_sem,
):
    rows, width = out_ref.shape
    unit = wgu.shape[3] // QUARTERS
    named = gw_rows(n_grp * n_ep)
    p, g, z = lax.axis_index("parts"), lax.axis_index("grp"), lax.axis_index("ep")
    x, c = g // CORES, g % CORES
    other_c = 1 - c
    experts = (g * n_ep + z, ((1 - x) * CORES + c) * n_ep + z)
    core_peer = {"parts": p, "grp": x * CORES + other_c, "ep": z}
    x_peer = {"parts": p, "grp": (1 - x) * CORES + c, "ep": z}
    y_peer = {"parts": 1 - p, "grp": g, "ep": z}

    def z_peer(step):
        return {"parts": p, "grp": g, "ep": z + step}

    barrier = pltpu.get_barrier_semaphore()

    def greet(peer):
        pl.semaphore_signal(barrier, inc=1, device_id=peer, device_id_type=pl.DeviceIdType.MESH)

    for peer in (core_peer, x_peer, y_peer):
        greet(peer)

    @pl.when(z > 0)
    def _():
        greet(z_peer(-1))

    @pl.when(z < n_ep - 1)
    def _():
        greet(z_peer(1))

    small = [
        pltpu.make_async_copy(ids_hbm, ids_ref, load_sem.at[2 + 3 * QUARTERS]),
        pltpu.make_async_copy(route_hbm, route_ref, load_sem.at[3 + 3 * QUARTERS]),
    ]
    for load in small:
        load.start()
    loads = [
        pltpu.make_async_copy(tok_hbm, tok.at[z, c], load_sem.at[0]),
        pltpu.make_async_copy(cot_hbm, cot.at[z, c], load_sem.at[1]),
    ]
    for q in range(QUARTERS):
        span = pl.ds(q * unit, unit)
        for i, (source, target) in enumerate((
            (wg_hbm.at[0, :, span], wgu.at[0, q // 2, :, pl.ds(q % 2 * 2 * unit, unit)]),
            (wu_hbm.at[0, :, span], wgu.at[0, q // 2, :, pl.ds((q % 2 * 2 + 1) * unit, unit)]),
            (wd_hbm.at[0, span, :], wdn.at[0, q // 2, pl.ds(q % 2 * unit, unit)]),
        )):
            loads.append(pltpu.make_async_copy(source, target, load_sem.at[2 + 3 * q + i]))
    for load in loads:
        load.start()

    acc[...] = jnp.zeros_like(acc)
    sums[...] = jnp.zeros_like(sums)
    for load in small:
        load.wait()
    item = lax.broadcasted_iota(jnp.int32, (named, LANES), 0)
    routed = jnp.zeros((named, LANES), jnp.float32)
    for k in range(ids_ref.shape[0]):
        routed += jnp.where(item == ids_ref[k:k + 1, :], route_ref[k:k + 1, :], 0.0)
    high = routed.astype(jnp.bfloat16)
    rts[z, c, 0:named, :] = high
    rts[z, c, named:2 * named, :] = (routed - high.astype(jnp.float32)).astype(jnp.bfloat16)

    for load in loads:
        load.wait()
    near = jnp.where(z > 0, 1, 0) + jnp.where(z < n_ep - 1, 1, 0)
    pl.semaphore_wait(barrier, 3 + near)

    def remote(source, target, send, recv, peer):
        return pltpu.make_async_remote_copy(
            src_ref=source, dst_ref=target, send_sem=send, recv_sem=recv,
            device_id=peer, device_id_type=pl.DeviceIdType.MESH,
        )

    sides = jnp.minimum(z, n_ep - 1 - z)

    low_half = 2 * z < n_ep - 1

    def place(k):
        step = jnp.where(k % 2 == 1, -((k + 1) // 2), k // 2)
        near_k = jnp.where(low_half, z + step, z - step)
        far_k = jnp.where(low_half, k, n_ep - 1 - k)
        return jnp.where(k <= 2 * sides, near_k, far_k)

    part = rows // 2

    def block(kind, zs, cs):
        if kind == 0:
            return tok.at[zs, cs]
        if kind == 1:
            return rts.at[zs, cs]
        return cot.at[zs, cs, pl.ds((kind - 2) * part, part)]

    def along_z(kind, zs, step):
        here = block(kind, zs, c)
        return remote(here, here, z_sem.at[kind, zs, (step + 1) // 2], got_sem.at[kind, zs, c],
                      z_peer(step))

    def to_core(kind, zs):
        here = block(kind, zs, c)
        return remote(here, here, c_sem.at[kind, zs], got_sem.at[kind, zs, c], core_peer)

    def arrived(kind, zs, cs):
        here = block(kind, zs, cs)
        remote(here, here, c_sem.at[kind, zs], got_sem.at[kind, zs, cs], core_peer).wait_recv()

    def each_z(kind, zs, act):
        @pl.when(jnp.logical_and(zs <= z, z < n_ep - 1))
        def _():
            act(along_z(kind, zs, 1))

        @pl.when(jnp.logical_and(zs >= z, z > 0))
        def _():
            act(along_z(kind, zs, -1))

    def start(copy):
        copy.start()

    def wait_send(copy):
        copy.wait_send()

    def take(k, *group):
        zs = place(k)
        for kind in group:
            arrived(kind, zs, c)
            each_z(kind, zs, start)
            to_core(kind, zs).start()

    def at_ends(act, *args):
        @pl.when(sides == 0)
        def _():
            act(*args)

    def inside(act, *args):
        @pl.when(sides > 0)
        def _():
            act(*args)

    downs = PIECES // 2
    tall, flat = width // PIECES, unit // downs

    def gate_up(e, j, h, at):
        lanes = pl.ds(pl.multiple_of(h * 2 * unit, 2 * unit), 2 * unit)
        return wgu.at[e, j, pl.ds(pl.multiple_of(at * tall, tall), tall), lanes]

    def down(e, j, h, at):
        return wdn.at[e, j, pl.ds(pl.multiple_of(h * unit + at * flat, flat), flat)]

    crossing = [(gate_up, 0, p, n) for n in range(PIECES)] + [(down, 0, p, n) for n in range(downs)]
    early = len(crossing)
    for h in range(2):
        crossing += [(gate_up, 1, h, p * downs + n) for n in range(downs)]
        crossing += [(down, 1, h, p * (downs // 2) + n) for n in range(downs // 2)]
    crossing += [(down, 1, 1, (1 - p) * (downs // 2) + n) for n in range(downs // 2)]
    middle, relayed = early + downs + downs // 2, len(crossing) - downs

    def piece(e, i):
        part, *place_of = crossing[i]
        return part(e, *place_of)

    def over_x(i):
        return remote(piece(0, i), piece(1, i), wx_s.at[i], wx_r.at[i], x_peer)

    def over_y(i):
        return remote(piece(1, i), piece(1, i), wy_s.at[i], wy_r.at[i], y_peer)

    def relay(i):
        over_x(i).wait_recv()
        over_y(i).start()

    contract = (((1,), (1,)), ((), ()))
    both = CORES * rows

    def scale_of(zs, expert):
        columns = []
        for cs in range(CORES):
            routes = rts[zs, cs, 0:named, :].astype(jnp.float32)
            routes += rts[zs, cs, named:2 * named, :].astype(jnp.float32)
            weight = jnp.sum(jnp.where(item == expert, routes, 0.0), axis=0, keepdims=True)
            columns.append(jnp.broadcast_to(weight, (rows, LANES)).T)
        return jnp.concatenate(columns, axis=0)

    def compute(zs, e, j, halves):
        expert = jnp.where(e == 0, experts[0], experts[1])
        scale = scale_of(zs, expert)
        rows_in = tok[zs].reshape(both, width)
        grads_in = cot[zs].reshape(both, width)
        low, high = halves[0] * unit, (halves[-1] + 1) * unit
        pres = jnp.dot(rows_in, wgu[e, j, :, 2 * low:2 * high], preferred_element_type=jnp.float32)
        hidden_grads = lax.dot_general(grads_in, wdn[e, j, low:high], contract,
                                       preferred_element_type=jnp.float32)
        lane_sums = jnp.zeros((both, LANES), jnp.float32)
        grads = []
        for at in range(len(halves)):
            gate_pre = pres[:, 2 * at * unit:(2 * at + 1) * unit]
            up_pre = pres[:, (2 * at + 1) * unit:(2 * at + 2) * unit]
            hidden_grad = hidden_grads[:, at * unit:(at + 1) * unit]
            sigmoid_gate = 1.0 / (1.0 + jnp.exp(-gate_pre))
            activation = gate_pre * sigmoid_gate
            lane_sums += hidden_grad * (activation * up_pre)
            hidden_grad = hidden_grad * scale
            grads.append((hidden_grad * up_pre * sigmoid_gate
                          * (1.0 + gate_pre * (1.0 - sigmoid_gate))).astype(jnp.bfloat16))
            grads.append((hidden_grad * activation).astype(jnp.bfloat16))
        sums[zs, e] += lane_sums
        terms = lax.dot_general(jnp.concatenate(grads, axis=1), wgu[e, j, :, 2 * low:2 * high],
                                contract, preferred_element_type=jnp.float32)
        acc[zs] += terms.reshape(CORES, rows, width)

    cut_rows = rows // CUTS
    cuts = [pl.ds(i * cut_rows, cut_rows) for i in range(CUTS)]

    def first_copy(zs, i):
        if i < CUTS:
            source, target = parts.at[zs, cuts[i]], r1.at[zs, cuts[i]]
        else:
            source, target = parts_g.at[zs], r1_g.at[zs]
        return remote(source, target, s1_sem.at[zs, i], r1_sem.at[zs, i], core_peer)

    def second_copy(zs, step, i):
        way = (step + 1) // 2
        if i < CUTS:
            source, target = sent.at[zs, cuts[i]], up.at[way, zs, cuts[i]]
        else:
            source, target = sent_g.at[zs], up_g.at[way, zs]
        return remote(source, target, s2_sem.at[zs, i], r2_sem.at[way, zs, i], z_peer(step))

    def finish(zs):
        parts[zs] = acc[zs, other_c].astype(jnp.bfloat16)
        for i in range(CUTS):
            first_copy(zs, i).start()
        lanes = sums[zs].reshape(2 * both, LANES)
        high = lanes.astype(jnp.bfloat16)
        low = (lanes - high.astype(jnp.float32)).astype(jnp.bfloat16)
        ones = jnp.ones((16, LANES), jnp.bfloat16)
        totals = lax.dot_general(ones, high, contract, preferred_element_type=jnp.float32)
        totals += lax.dot_general(ones, low, contract, preferred_element_type=jnp.float32)
        for cs in range(CORES):
            found = jnp.zeros((named, LANES), jnp.float32)
            for e in range(2):
                at = e * both + cs * rows
                found += jnp.where(item == experts[e], totals[0:1, at:at + rows], 0.0)
            pair_g[zs, cs] = found.astype(jnp.bfloat16)
        parts_g[zs] = pair_g[zs, other_c]
        first_copy(zs, CUTS).start()

    def summed(zs, ways, i):
        first_copy(zs, i).wait_recv()
        for way in ways:
            second_copy(zs, 2 * way - 1, i).wait_recv()
        if i < CUTS:
            total = acc[zs, c, cuts[i]] + r1[zs, cuts[i]].astype(jnp.float32)
            for way in ways:
                total += up[way, zs, cuts[i]].astype(jnp.float32)
            return total
        total = pair_g[zs, c].astype(jnp.float32) + r1_g[zs].astype(jnp.float32)
        for way in ways:
            total += up_g[way, zs].astype(jnp.float32)
        return total

    def pass_on(zs, ways, step):
        for i in ORDER:
            total = summed(zs, ways, i).astype(jnp.bfloat16)
            if i < CUTS:
                sent[zs, cuts[i]] = total
            else:
                sent_g[zs] = total
            second_copy(zs, step, i).start()

    def send_back(k, inner):
        zs = place(k)

        @pl.when(zs > z)
        def _():
            pass_on(zs, [1] if inner else [], 1)

        @pl.when(zs < z)
        def _():
            pass_on(zs, [0] if inner else [], -1)

    def conclude(ways):
        for i in ORDER:
            total = summed(z, ways, i)
            if i < CUTS:
                out_ref[cuts[i], :] = total.astype(jnp.bfloat16)
            else:
                for k in range(ids_ref.shape[0]):
                    picked = jnp.where(item == ids_ref[k:k + 1, :], total, 0.0)
                    gw_ref[k:k + 1, :] = jnp.sum(picked, axis=0, keepdims=True).astype(jnp.bfloat16)

    def own_rest(inward):
        @pl.when(low_half)
        def _():
            along_z(KINDS[3], z, inward).start()

        @pl.when(jnp.logical_not(low_half))
        def _():
            along_z(KINDS[3], z, -inward).start()

    over_x(0).start()
    for kind in KINDS[:3]:
        each_z(kind, z, start)
    at_ends(each_z, KINDS[3], z, start)
    inside(own_rest, -1)
    for i in range(1, len(crossing)):
        over_x(i).start()
    for kind in KINDS:
        to_core(kind, z).start()

    def block_here(k):
        for kind in KINDS:
            arrived(kind, place(k), other_c)

    steps = (0, early, middle, relayed)

    def units_here(step):
        for i in range(steps[step], steps[step + 1]):
            over_y(i).wait_recv()
        if step == 2:
            for i in range(relayed, len(crossing)):
                over_x(i).wait_recv()

    far = n_ep - 1
    start_events = [
        ((0, 0, 0), [(block_here, 0)]),
        ((0, 0, 1), []),
    ]
    end_plan = start_events + [
        ((1, 0, 0), [
            (relay, 0), (take, 1, 0, 1), (relay, 1), (take, 1, 2), (relay, 2),
            (take, 1, 3), (relay, 3), (block_here, 1),
        ]),
        ((1, 0, 1), [(relay, 4)]),
        ((0, 1, 0), [
            (take, far - 1, 0, 1), (relay, 5), (relay, 6),
            (units_here, 0), (take, far, 0, 1), (relay, 7),
        ]),
        ((1, 1, 0), []),
        ((far, 0, 0), [
            (relay, 8), (take, far, 2), (relay, 9), (take, far, 3),
            (block_here, far),
        ]),
        ((far, 0, 1), [(relay, 10), (take, far - 1, 2)]),
        ((far, 1, 0), []),
        ((far, 1, 2), [(units_here, 1)]),
        ((1, 1, 2), []),
        ((0, 1, 2), [(take, far - 1, 3)]),
        ((far, 1, 3), [(units_here, 2)]),
        ((far - 1, 0, 0), [(block_here, far - 1)]),
        ((far - 1, 0, 1), []), ((far - 1, 1, 0), []), ((far - 1, 1, 1), []),
        ((1, 1, 3), []), ((0, 1, 3), []),
    ]
    inner_plan = start_events + [
        ((1, 0, 0), [
            (relay, 0), (take, 1, 0, 1), (take, far - 1, 0, 1), (relay, 1),
            (take, 1, 2), (relay, 2), (take, 1, 3), (own_rest, 1), (relay, 3),
            (block_here, 1),
        ]),
        ((1, 0, 1), [(take, far, 0, 1), (relay, 4)]),
        ((0, 1, 0), [
            (take, far, 2), (relay, 5), (take, far, 3), (take, far - 1, 2),
            (relay, 6), (units_here, 0), (take, far - 1, 3), (relay, 7),
        ]),
        ((1, 1, 0), []),
        ((far - 1, 0, 0), [(block_here, far - 1), (relay, 8)]),
        ((far - 1, 0, 1), []),
        ((far - 1, 1, 0), [(relay, 9)]),
        ((far, 0, 0), [(block_here, far)]),
        ((far, 0, 1), [(relay, 10)]),
        ((far, 1, 0), []),
        ((far, 1, 2), [(units_here, 1)]),
        ((1, 1, 2), []), ((0, 1, 2), []),
        ((far, 1, 3), [(units_here, 2)]),
        ((far - 1, 1, 1), []), ((1, 1, 3), []), ((0, 1, 3), []),
    ]

    def run_events(acts):
        for act, *args in acts:
            act(*args)

    def turn(i, carry):
        def step_of(plan, low, high):
            if high - low == 1:
                run_events(plan[low][1])
                return
            cut = (low + high) // 2
            for first_at, last_at, here in ((low, cut, i < cut), (cut, high, i >= cut)):
                if any(acts for task, acts in plan[first_at:last_at]):
                    @pl.when(here)
                    def _(first_at=first_at, last_at=last_at):
                        step_of(plan, first_at, last_at)

        at_ends(step_of, end_plan, 0, len(end_plan))
        inside(step_of, inner_plan, 0, len(inner_plan))

        k, e, j = (
            jnp.where(sides == 0, *(pick(i, [task[field] for task, acts in plan])
                                    for plan in (end_plan, inner_plan)))
            for field in range(3)
        )

        @pl.when(j < 2)
        def _():
            compute(place(k), e, j, (0, 1))

        for half in range(2):
            @pl.when(j == 2 + half)
            def _(half=half):
                compute(place(k), e, 1, (half,))

        tails = [(at, task) for at, (task, acts) in enumerate(end_plan)
                 if task[0] and task[1:] in ((1, 1), (1, 3))]

        @pl.when(jnp.logical_and(i > tails[0][0], sides == 0))
        def _():
            for at, task in tails:
                @pl.when(i == at + 1)
                def _(task=task):
                    send_back(task[0], False)

        whole = jnp.logical_and(e == 1, j == 1)

        @pl.when(jnp.logical_or(j == 3, whole))
        def _():
            finish(place(k))

        return carry

    assert len(end_plan) == len(inner_plan)
    lax.fori_loop(0, len(end_plan), turn, 0)

    @pl.when(sides > 0)
    def _():
        for k in [n_ep - 1] + list(range(1, n_ep - 1)):
            send_back(k, True)

    def drain(zs, carry):
        for kind in KINDS:
            each_z(kind, zs, wait_send)
            to_core(kind, zs).wait_send()
        for i in range(CUTS + 1):
            first_copy(zs, i).wait_send()
        return carry

    def drain_back(zs, carry):
        @pl.when(zs != z)
        def _():
            for i in range(CUTS + 1):
                second_copy(zs, 1, i).wait_send()

        return carry

    for i in range(len(crossing)):
        over_x(i).wait_send()
    for i in range(relayed):
        over_y(i).wait_send()
    lax.fori_loop(0, n_ep, drain, 0)

    @pl.when(sides > 0)
    def _():
        lax.fori_loop(0, n_ep, drain_back, 0)
        conclude([1, 0])

    @pl.when(z == 0)
    def _():
        conclude([0])

    @pl.when(z == n_ep - 1)
    def _():
        conclude([1])

    @pl.when(sides == 0)
    def _():
        lax.fori_loop(0, n_ep, drain_back, 0)


def swap_plan(tokens, cotangent, expert_ids, route_weights, w_gate, w_up, w_down):
    n_grp, n_ep = lax.axis_size("grp"), lax.axis_size("ep")
    named = gw_rows(n_grp * n_ep)
    rows, width = tokens.shape
    unit = w_gate.shape[2] // QUARTERS
    any_ref, vmem = pl.BlockSpec(memory_space=pl.ANY), pl.BlockSpec(memory_space=pltpu.VMEM)
    bf16, f32, dma = jnp.bfloat16, jnp.float32, pltpu.SemaphoreType.DMA
    pieces = 3 * PIECES + PIECES // 4
    grad_tokens, grad_weights = pl.pallas_call(
        functools.partial(swap_kernel, n_grp, n_ep),
        out_shape=(
            pltpu.VMEM((rows, width), bf16),
            pltpu.VMEM(expert_ids.shape[::-1], bf16),
        ),
        in_specs=[any_ref] * 7,
        out_specs=(vmem, vmem),
        scratch_shapes=[
            pltpu.VMEM(expert_ids.shape[::-1], jnp.int32),
            pltpu.VMEM(route_weights.shape[::-1], f32),
            pltpu.VMEM((n_ep, CORES, rows, width), bf16),
            pltpu.VMEM((n_ep, CORES, rows, width), bf16),
            pltpu.VMEM((n_ep, CORES, 2 * named, LANES), bf16),
            pltpu.VMEM((2, 2, width, 4 * unit), bf16),
            pltpu.VMEM((2, 2, 2 * unit, width), bf16),
            pltpu.VMEM((n_ep, CORES, rows, width), f32),
            pltpu.VMEM((n_ep, 2, CORES * rows, LANES), f32),
            pltpu.VMEM((n_ep, rows, width), bf16),
            pltpu.VMEM((n_ep, named, LANES), bf16),
            pltpu.VMEM((n_ep, rows, width), bf16),
            pltpu.VMEM((n_ep, named, LANES), bf16),
            pltpu.VMEM((n_ep, rows, width), bf16),
            pltpu.VMEM((n_ep, named, LANES), bf16),
            pltpu.VMEM((2, n_ep, rows, width), bf16),
            pltpu.VMEM((2, n_ep, named, LANES), bf16),
            pltpu.VMEM((n_ep, CORES, named, LANES), bf16),
            dma((4 + 3 * QUARTERS,)), dma((4, n_ep, CORES)), dma((4, n_ep, 2)), dma((4, n_ep)),
            dma((pieces,)), dma((pieces,)), dma((pieces,)), dma((pieces,)),
            dma((n_ep, CUTS + 1)), dma((n_ep, CUTS + 1)),
            dma((n_ep, CUTS + 1)), dma((2, n_ep, CUTS + 1)),
        ],
        compiler_params=pltpu.CompilerParams(
            collective_id=0, has_side_effects=True, vmem_limit_bytes=VMEM_ROOM
        ),
    )(tokens, cotangent, expert_ids.T, route_weights.T, w_gate, w_up, w_down)
    return grad_tokens, grad_weights.T


def on_device(tokens, cotangent, expert_ids, route_weights, w_gate, w_up, w_down):
    n_grp, n_ep = lax.axis_size("grp"), lax.axis_size("ep")
    rows, width = tokens.shape
    swaps = lax.axis_size("parts") == 2 and n_grp == 2 * CORES and n_ep == 4
    fits = rows == LANES and width % LANES == 0 and w_gate.shape[2] == QUARTERS * LANES
    held = 2 * (w_gate.size + w_up.size + w_down.size) * 2 + n_ep * rows * width * 28
    plan = swap_plan if swaps and fits and held <= VMEM_ROOM else dispatch_plan
    return plan(tokens, cotangent, expert_ids, route_weights, w_gate, w_up, w_down)


def solution(mesh):
    in_specs = (
        P(("parts", "grp", "ep"), None),
        P(("parts", "grp", "ep"), None),
        P(("parts", "grp", "ep"), None),
        P(("parts", "grp", "ep"), None),
        P(("grp", "ep"), None, None),
        P(("grp", "ep"), None, None),
        P(("grp", "ep"), None, None),
    )
    out_specs = (P(("parts", "grp", "ep"), None), P(("parts", "grp", "ep"), None))
    return jax.shard_map(
        on_device, mesh=mesh, in_specs=in_specs, out_specs=out_specs, check_vma=False
    )
```

```python
import functools

import jax
import jax.numpy as jnp
from jax import lax
from jax.experimental import pallas as pl
from jax.experimental.pallas import tpu as pltpu
from jax.sharding import PartitionSpec as P

LANES = 128
CORES = 2
VMEM_ROOM = 56 * 1024 * 1024


def expert_grads(rows_in, grads_in, w_gate, w_up, w_down):
    contract = (((1,), (1,)), ((), ()))
    gate_pre = jnp.dot(rows_in, w_gate, preferred_element_type=jnp.float32)
    up_pre = jnp.dot(rows_in, w_up, preferred_element_type=jnp.float32)
    hidden_grad = lax.dot_general(grads_in, w_down, contract, preferred_element_type=jnp.float32)
    sigmoid_gate = jax.nn.sigmoid(gate_pre)
    activation = gate_pre * sigmoid_gate
    hidden = activation * up_pre
    weight_grad = jnp.sum(hidden_grad * hidden, axis=-1).astype(jnp.bfloat16)
    grad_up = (hidden_grad * activation).astype(jnp.bfloat16)
    grad_gate = (
        hidden_grad * up_pre * sigmoid_gate * (1.0 + gate_pre * (1.0 - sigmoid_gate))
    ).astype(jnp.bfloat16)
    row_terms = (
        lax.dot_general(grad_gate, w_gate, contract, preferred_element_type=jnp.float32)
        + lax.dot_general(grad_up, w_up, contract, preferred_element_type=jnp.float32)
    ).astype(jnp.bfloat16)
    return (row_terms, weight_grad)


def slot_plan(routes, experts, capacity):
    tok_rows, top_count = routes.shape
    flat_ids = routes.reshape(-1)
    pad_pair = flat_ids.shape[0]
    pair_ids = jnp.arange(pad_pair, dtype=jnp.int32)
    sort_order = jnp.argsort(flat_ids, stable=True)
    sorted_ids = flat_ids[sort_order]
    onehot = (flat_ids[:, None] == jnp.arange(experts, dtype=jnp.int32)[None, :]).astype(jnp.int32)
    counts = jnp.sum(onehot, axis=0)
    earlier = jnp.tri(experts, k=-1, dtype=jnp.int32)
    starts = jnp.sum(earlier * counts[None, :], axis=1)
    sorted_rank = pair_ids - starts[sorted_ids]
    sorted_slot = sorted_ids * capacity + sorted_rank
    slot_of_pair = jnp.zeros((pad_pair,), jnp.int32).at[sort_order].set(sorted_slot)
    slot_pair = jnp.full((experts * capacity,), pad_pair, jnp.int32).at[sorted_slot].set(sort_order)
    slot_token = jnp.where(slot_pair < pad_pair, slot_pair // top_count, tok_rows)
    return (slot_of_pair, slot_token, slot_pair)


def place_rows(source_rows, slot_token):
    padded = jnp.concatenate(
        [source_rows, jnp.zeros((1, source_rows.shape[1]), source_rows.dtype)], 0
    )
    return padded[slot_token]


def dispatch_plan(tokens, cotangent, expert_ids, route_weights, w_gate, w_up, w_down):
    group_count = lax.axis_size("grp")
    lane_count = lax.axis_size("ep")
    experts = group_count * lane_count
    tok_rows, top_count = expert_ids.shape
    model_width = tokens.shape[1]
    capacity = 2 * tok_rows * top_count // experts
    slot_of_pair, slot_token, unused_pairs = slot_plan(expert_ids, experts, capacity)
    send_rows = place_rows(tokens, slot_token).reshape(
        group_count, lane_count, capacity, model_width
    )
    send_grads = place_rows(cotangent, slot_token).reshape(
        group_count, lane_count, capacity, model_width
    )
    send_rows, send_grads = (
        lax.all_to_all(send_rows, "grp", split_axis=0, concat_axis=0, tiled=True),
        lax.all_to_all(send_grads, "grp", split_axis=0, concat_axis=0, tiled=True),
    )
    rows_in = lax.all_to_all(send_rows, "ep", split_axis=1, concat_axis=1, tiled=True)
    grads_in = lax.all_to_all(send_grads, "ep", split_axis=1, concat_axis=1, tiled=True)
    leading = rows_in.shape[:3]
    row_terms, weight_grad = expert_grads(
        rows_in.reshape(-1, model_width),
        grads_in.reshape(-1, model_width),
        w_gate[0],
        w_up[0],
        w_down[0],
    )
    row_terms = row_terms.reshape(leading + (model_width,))
    weight_grad = weight_grad.reshape(leading)
    row_terms, weight_grad = (
        lax.all_to_all(row_terms, "ep", split_axis=1, concat_axis=1, tiled=True),
        lax.all_to_all(weight_grad, "ep", split_axis=1, concat_axis=1, tiled=True),
    )
    row_terms, weight_grad = (
        lax.all_to_all(row_terms, "grp", split_axis=0, concat_axis=0, tiled=True),
        lax.all_to_all(weight_grad, "grp", split_axis=0, concat_axis=0, tiled=True),
    )
    row_terms = row_terms.reshape(experts * capacity, model_width)
    weight_grad = weight_grad.reshape(experts * capacity)
    picked = row_terms[slot_of_pair].reshape(tok_rows, top_count, model_width)
    grad_tokens = jnp.sum(route_weights[:, :, None] * picked.astype(jnp.float32), axis=1)
    grad_weights = weight_grad[slot_of_pair].reshape(tok_rows, top_count)
    return (grad_tokens.astype(jnp.bfloat16), grad_weights)


CUTS = 2
ORDER = tuple(range(CUTS - 1)) + (CUTS, CUTS - 1)
PIECES = 4
QUARTERS = 4
KINDS = (0, 1, 2, 3)


def gw_rows(experts):
    return -(-experts // 16) * 16


def pick(index, values):
    chosen = jnp.int32(values[0])
    for at in range(1, len(values)):
        if values[at] != values[at - 1]:
            chosen = jnp.where(index >= at, jnp.int32(values[at]), chosen)
    return chosen


def swap_kernel(
    n_grp, n_ep, tok_hbm, cot_hbm, ids_hbm, route_hbm, wg_hbm, wu_hbm, wd_hbm,
    out_ref, gw_ref,
    ids_ref, route_ref, tok, cot, rts, wgu, wdn, acc, sums, parts, parts_g, r1, r1_g, sent, sent_g, up, up_g, pair_g,
    load_sem, got_sem, z_sem, c_sem, wx_s, wx_r, wy_s, wy_r,
    s1_sem, r1_sem, s2_sem, r2_sem,
):
    rows, width = out_ref.shape
    unit = wgu.shape[3] // QUARTERS
    named = gw_rows(n_grp * n_ep)
    p, g, z = lax.axis_index("parts"), lax.axis_index("grp"), lax.axis_index("ep")
    x, c = g // CORES, g % CORES
    other_c = 1 - c
    experts = (g * n_ep + z, ((1 - x) * CORES + c) * n_ep + z)
    core_peer = {"parts": p, "grp": x * CORES + other_c, "ep": z}
    x_peer = {"parts": p, "grp": (1 - x) * CORES + c, "ep": z}
    y_peer = {"parts": 1 - p, "grp": g, "ep": z}

    def z_peer(step):
        return {"parts": p, "grp": g, "ep": z + step}

    barrier = pltpu.get_barrier_semaphore()

    def greet(peer):
        pl.semaphore_signal(barrier, inc=1, device_id=peer, device_id_type=pl.DeviceIdType.MESH)

    for peer in (core_peer, x_peer, y_peer):
        greet(peer)

    @pl.when(z > 0)
    def _():
        greet(z_peer(-1))

    @pl.when(z < n_ep - 1)
    def _():
        greet(z_peer(1))

    small = [
        pltpu.make_async_copy(ids_hbm, ids_ref, load_sem.at[2 + 3 * QUARTERS]),
        pltpu.make_async_copy(route_hbm, route_ref, load_sem.at[3 + 3 * QUARTERS]),
    ]
    for load in small:
        load.start()
    loads = [
        pltpu.make_async_copy(tok_hbm, tok.at[z, c], load_sem.at[0]),
        pltpu.make_async_copy(cot_hbm, cot.at[z, c], load_sem.at[1]),
    ]
    for q in range(QUARTERS):
        span = pl.ds(q * unit, unit)
        for i, (source, target) in enumerate((
            (wg_hbm.at[0, :, span], wgu.at[0, q // 2, :, pl.ds(q % 2 * 2 * unit, unit)]),
            (wu_hbm.at[0, :, span], wgu.at[0, q // 2, :, pl.ds((q % 2 * 2 + 1) * unit, unit)]),
            (wd_hbm.at[0, span, :], wdn.at[0, q // 2, pl.ds(q % 2 * unit, unit)]),
        )):
            loads.append(pltpu.make_async_copy(source, target, load_sem.at[2 + 3 * q + i]))
    for load in loads:
        load.start()

    acc[...] = jnp.zeros_like(acc)
    sums[...] = jnp.zeros_like(sums)
    for load in small:
        load.wait()
    item = lax.broadcasted_iota(jnp.int32, (named, LANES), 0)
    routed = jnp.zeros((named, LANES), jnp.float32)
    for k in range(ids_ref.shape[0]):
        routed += jnp.where(item == ids_ref[k:k + 1, :], route_ref[k:k + 1, :], 0.0)
    high = routed.astype(jnp.bfloat16)
    rts[z, c, 0:named, :] = high
    rts[z, c, named:2 * named, :] = (routed - high.astype(jnp.float32)).astype(jnp.bfloat16)

    for load in loads:
        load.wait()
    near = jnp.where(z > 0, 1, 0) + jnp.where(z < n_ep - 1, 1, 0)
    pl.semaphore_wait(barrier, 3 + near)

    def remote(source, target, send, recv, peer):
        return pltpu.make_async_remote_copy(
            src_ref=source, dst_ref=target, send_sem=send, recv_sem=recv,
            device_id=peer, device_id_type=pl.DeviceIdType.MESH,
        )

    sides = jnp.minimum(z, n_ep - 1 - z)

    low_half = 2 * z < n_ep - 1

    def place(k):
        step = jnp.where(k % 2 == 1, -((k + 1) // 2), k // 2)
        near_k = jnp.where(low_half, z + step, z - step)
        far_k = jnp.where(low_half, k, n_ep - 1 - k)
        return jnp.where(k <= 2 * sides, near_k, far_k)

    part = rows // 2

    def block(kind, zs, cs):
        if kind == 0:
            return tok.at[zs, cs]
        if kind == 1:
            return rts.at[zs, cs]
        return cot.at[zs, cs, pl.ds((kind - 2) * part, part)]

    def along_z(kind, zs, step):
        here = block(kind, zs, c)
        return remote(here, here, z_sem.at[kind, zs, (step + 1) // 2], got_sem.at[kind, zs, c],
                      z_peer(step))

    def to_core(kind, zs):
        here = block(kind, zs, c)
        return remote(here, here, c_sem.at[kind, zs], got_sem.at[kind, zs, c], core_peer)

    def arrived(kind, zs, cs):
        here = block(kind, zs, cs)
        remote(here, here, c_sem.at[kind, zs], got_sem.at[kind, zs, cs], core_peer).wait_recv()

    def each_z(kind, zs, act):
        @pl.when(jnp.logical_and(zs <= z, z < n_ep - 1))
        def _():
            act(along_z(kind, zs, 1))

        @pl.when(jnp.logical_and(zs >= z, z > 0))
        def _():
            act(along_z(kind, zs, -1))

    def start(copy):
        copy.start()

    def wait_send(copy):
        copy.wait_send()

    def take(k, *group):
        zs = place(k)
        for kind in group:
            arrived(kind, zs, c)
            each_z(kind, zs, start)
            to_core(kind, zs).start()

    def at_ends(act, *args):
        @pl.when(sides == 0)
        def _():
            act(*args)

    def inside(act, *args):
        @pl.when(sides > 0)
        def _():
            act(*args)

    downs = PIECES // 2
    tall, flat = width // PIECES, unit // downs

    def gate_up(e, j, h, at):
        lanes = pl.ds(pl.multiple_of(h * 2 * unit, 2 * unit), 2 * unit)
        return wgu.at[e, j, pl.ds(pl.multiple_of(at * tall, tall), tall), lanes]

    def down(e, j, h, at):
        return wdn.at[e, j, pl.ds(pl.multiple_of(h * unit + at * flat, flat), flat)]

    crossing = [(gate_up, 0, p, n) for n in range(PIECES)] + [(down, 0, p, n) for n in range(downs)]
    early = len(crossing)
    for h in range(2):
        crossing += [(gate_up, 1, h, p * downs + n) for n in range(downs)]
        crossing += [(down, 1, h, p * (downs // 2) + n) for n in range(downs // 2)]
    crossing += [(down, 1, 1, (1 - p) * (downs // 2) + n) for n in range(downs // 2)]
    middle, relayed = early + downs + downs // 2, len(crossing) - downs

    def piece(e, i):
        part, *place_of = crossing[i]
        return part(e, *place_of)

    def over_x(i):
        return remote(piece(0, i), piece(1, i), wx_s.at[i], wx_r.at[i], x_peer)

    def over_y(i):
        return remote(piece(1, i), piece(1, i), wy_s.at[i], wy_r.at[i], y_peer)

    def relay(i):
        over_x(i).wait_recv()
        over_y(i).start()

    contract = (((1,), (1,)), ((), ()))
    both = CORES * rows

    def scale_of(zs, expert):
        columns = []
        for cs in range(CORES):
            routes = rts[zs, cs, 0:named, :].astype(jnp.float32)
            routes += rts[zs, cs, named:2 * named, :].astype(jnp.float32)
            weight = jnp.sum(jnp.where(item == expert, routes, 0.0), axis=0, keepdims=True)
            columns.append(jnp.broadcast_to(weight, (rows, LANES)).T)
        return jnp.concatenate(columns, axis=0)

    def compute(zs, e, j, halves):
        expert = jnp.where(e == 0, experts[0], experts[1])
        scale = scale_of(zs, expert)
        rows_in = tok[zs].reshape(both, width)
        grads_in = cot[zs].reshape(both, width)
        low, high = halves[0] * unit, (halves[-1] + 1) * unit
        pres = jnp.dot(rows_in, wgu[e, j, :, 2 * low:2 * high], preferred_element_type=jnp.float32)
        hidden_grads = lax.dot_general(grads_in, wdn[e, j, low:high], contract,
                                       preferred_element_type=jnp.float32)
        lane_sums = jnp.zeros((both, LANES), jnp.float32)
        grads = []
        for at in range(len(halves)):
            gate_pre = pres[:, 2 * at * unit:(2 * at + 1) * unit]
            up_pre = pres[:, (2 * at + 1) * unit:(2 * at + 2) * unit]
            hidden_grad = hidden_grads[:, at * unit:(at + 1) * unit]
            sigmoid_gate = 1.0 / (1.0 + jnp.exp(-gate_pre))
            activation = gate_pre * sigmoid_gate
            lane_sums += hidden_grad * (activation * up_pre)
            hidden_grad = hidden_grad * scale
            grads.append((hidden_grad * up_pre * sigmoid_gate
                          * (1.0 + gate_pre * (1.0 - sigmoid_gate))).astype(jnp.bfloat16))
            grads.append((hidden_grad * activation).astype(jnp.bfloat16))
        sums[zs, e] += lane_sums
        terms = lax.dot_general(jnp.concatenate(grads, axis=1), wgu[e, j, :, 2 * low:2 * high],
                                contract, preferred_element_type=jnp.float32)
        acc[zs] += terms.reshape(CORES, rows, width)

    cut_rows = rows // CUTS
    cuts = [pl.ds(i * cut_rows, cut_rows) for i in range(CUTS)]

    def first_copy(zs, i):
        if i < CUTS:
            source, target = parts.at[zs, cuts[i]], r1.at[zs, cuts[i]]
        else:
            source, target = parts_g.at[zs], r1_g.at[zs]
        return remote(source, target, s1_sem.at[zs, i], r1_sem.at[zs, i], core_peer)

    def second_copy(zs, step, i, peer):
        way = (step + 1) // 2
        if i < CUTS:
            source, target = sent.at[zs, cuts[i]], up.at[way, zs, cuts[i]]
        else:
            source, target = sent_g.at[zs], up_g.at[way, zs]
        return remote(source, target, s2_sem.at[zs, i], r2_sem.at[way, zs, i], peer)

    def finish(zs):
        parts[zs] = acc[zs, other_c].astype(jnp.bfloat16)
        for i in range(CUTS):
            first_copy(zs, i).start()
        lanes = sums[zs].reshape(2 * both, LANES)
        high = lanes.astype(jnp.bfloat16)
        low = (lanes - high.astype(jnp.float32)).astype(jnp.bfloat16)
        ones = jnp.ones((16, LANES), jnp.bfloat16)
        totals = lax.dot_general(ones, high, contract, preferred_element_type=jnp.float32)
        totals += lax.dot_general(ones, low, contract, preferred_element_type=jnp.float32)
        for cs in range(CORES):
            found = jnp.zeros((named, LANES), jnp.float32)
            for e in range(2):
                at = e * both + cs * rows
                found += jnp.where(item == experts[e], totals[0:1, at:at + rows], 0.0)
            pair_g[zs, cs] = found.astype(jnp.bfloat16)
        parts_g[zs] = pair_g[zs, other_c]
        first_copy(zs, CUTS).start()

    def summed(zs, ways, i):
        first_copy(zs, i).wait_recv()
        for way in ways:
            second_copy(zs, 2 * way - 1, i, core_peer).wait_recv()
        if i < CUTS:
            total = acc[zs, c, cuts[i]] + r1[zs, cuts[i]].astype(jnp.float32)
            for way in ways:
                total += up[way, zs, cuts[i]].astype(jnp.float32)
            return total
        total = pair_g[zs, c].astype(jnp.float32) + r1_g[zs].astype(jnp.float32)
        for way in ways:
            total += up_g[way, zs].astype(jnp.float32)
        return total

    def pass_on(zs, ways, step):
        for i in ORDER:
            total = summed(zs, ways, i).astype(jnp.bfloat16)
            if i < CUTS:
                sent[zs, cuts[i]] = total
            else:
                sent_g[zs] = total
            second_copy(zs, step, i, z_peer(step)).start()

    def send_back(k, inner):
        zs = place(k)

        @pl.when(zs > z)
        def _():
            pass_on(zs, [1] if inner else [], 1)

        @pl.when(zs < z)
        def _():
            pass_on(zs, [0] if inner else [], -1)

    def conclude(ways):
        for i in ORDER:
            total = summed(z, ways, i)
            if i < CUTS:
                out_ref[cuts[i], :] = total.astype(jnp.bfloat16)
            else:
                for k in range(ids_ref.shape[0]):
                    picked = jnp.where(item == ids_ref[k:k + 1, :], total, 0.0)
                    gw_ref[k:k + 1, :] = jnp.sum(picked, axis=0, keepdims=True).astype(jnp.bfloat16)

    def own_rest(inward):
        @pl.when(low_half)
        def _():
            along_z(KINDS[3], z, inward).start()

        @pl.when(jnp.logical_not(low_half))
        def _():
            along_z(KINDS[3], z, -inward).start()

    over_x(0).start()
    for kind in KINDS[:3]:
        each_z(kind, z, start)
    at_ends(each_z, KINDS[3], z, start)
    inside(own_rest, -1)
    for i in range(1, len(crossing)):
        over_x(i).start()
    for kind in KINDS:
        to_core(kind, z).start()

    def block_here(k):
        for kind in KINDS:
            arrived(kind, place(k), other_c)

    steps = (0, early, middle, relayed)

    def units_here(step):
        for i in range(steps[step], steps[step + 1]):
            over_y(i).wait_recv()
        if step == 2:
            for i in range(relayed, len(crossing)):
                over_x(i).wait_recv()

    far = n_ep - 1
    start_events = [
        ((0, 0, 0), [(block_here, 0)]),
        ((0, 0, 1), []),
    ]
    end_plan = start_events + [
        ((1, 0, 0), [
            (relay, 0), (take, 1, 0, 1), (relay, 1), (take, 1, 2), (relay, 2),
            (take, 1, 3), (relay, 3), (block_here, 1),
        ]),
        ((1, 0, 1), [(relay, 4)]),
        ((0, 1, 0), [
            (take, far - 1, 0, 1), (relay, 5), (relay, 6),
            (units_here, 0), (take, far, 0, 1), (relay, 7),
        ]),
        ((1, 1, 0), []),
        ((far, 0, 0), [
            (relay, 8), (take, far, 2), (relay, 9), (take, far, 3),
            (block_here, far),
        ]),
        ((far, 0, 1), [(relay, 10), (take, far - 1, 2)]),
        ((far, 1, 0), []),
        ((far, 1, 2), [(units_here, 1)]),
        ((1, 1, 2), []),
        ((0, 1, 2), [(take, far - 1, 3)]),
        ((far, 1, 3), [(units_here, 2)]),
        ((far - 1, 0, 0), [(block_here, far - 1)]),
        ((far - 1, 0, 1), []), ((far - 1, 1, 0), []), ((far - 1, 1, 1), []),
        ((1, 1, 3), []), ((0, 1, 3), []),
    ]
    inner_plan = start_events + [
        ((1, 0, 0), [
            (relay, 0), (take, 1, 0, 1), (take, far - 1, 0, 1), (relay, 1),
            (take, 1, 2), (relay, 2), (take, 1, 3), (own_rest, 1), (relay, 3),
            (block_here, 1),
        ]),
        ((1, 0, 1), [(take, far, 0, 1), (relay, 4)]),
        ((0, 1, 0), [
            (take, far, 2), (relay, 5), (take, far, 3), (take, far - 1, 2),
            (relay, 6), (units_here, 0), (take, far - 1, 3), (relay, 7),
        ]),
        ((1, 1, 0), []),
        ((far - 1, 0, 0), [(block_here, far - 1), (relay, 8)]),
        ((far - 1, 0, 1), []),
        ((far - 1, 1, 0), [(relay, 9)]),
        ((far, 0, 0), [(block_here, far)]),
        ((far, 0, 1), [(relay, 10)]),
        ((far, 1, 0), []),
        ((far, 1, 2), [(units_here, 1)]),
        ((1, 1, 2), []), ((0, 1, 2), []),
        ((far, 1, 3), [(units_here, 2)]),
        ((far - 1, 1, 1), []), ((1, 1, 3), []), ((0, 1, 3), []),
    ]

    def run_events(acts):
        for act, *args in acts:
            act(*args)

    def turn(i, carry):
        def step_of(plan, low, high):
            if high - low == 1:
                run_events(plan[low][1])
                return
            cut = (low + high) // 2
            for first_at, last_at, here in ((low, cut, i < cut), (cut, high, i >= cut)):
                if any(acts for task, acts in plan[first_at:last_at]):
                    @pl.when(here)
                    def _(first_at=first_at, last_at=last_at):
                        step_of(plan, first_at, last_at)

        at_ends(step_of, end_plan, 0, len(end_plan))
        inside(step_of, inner_plan, 0, len(inner_plan))

        k, e, j = (
            jnp.where(sides == 0, *(pick(i, [task[field] for task, acts in plan])
                                    for plan in (end_plan, inner_plan)))
            for field in range(3)
        )

        @pl.when(j < 2)
        def _():
            compute(place(k), e, j, (0, 1))

        for half in range(2):
            @pl.when(j == 2 + half)
            def _(half=half):
                compute(place(k), e, 1, (half,))

        tails = [(at, task) for at, (task, acts) in enumerate(end_plan)
                 if task[0] and task[1:] in ((1, 1), (1, 3))]

        @pl.when(jnp.logical_and(i > tails[0][0], sides == 0))
        def _():
            for at, task in tails:
                @pl.when(i == at + 1)
                def _(task=task):
                    send_back(task[0], False)

        whole = jnp.logical_and(e == 1, j == 1)

        @pl.when(jnp.logical_or(j == 3, whole))
        def _():
            finish(place(k))

        return carry

    assert len(end_plan) == len(inner_plan)
    lax.fori_loop(0, len(end_plan), turn, 0)

    @pl.when(sides > 0)
    def _():
        for k in [n_ep - 1] + list(range(1, n_ep - 1)):
            send_back(k, True)

    def drain(zs, carry):
        for kind in KINDS:
            each_z(kind, zs, wait_send)
            to_core(kind, zs).wait_send()
        for i in range(CUTS + 1):
            first_copy(zs, i).wait_send()
        return carry

    def drain_back(zs, carry):
        @pl.when(zs != z)
        def _():
            for i in range(CUTS + 1):
                second_copy(zs, 1, i, core_peer).wait_send()

        return carry

    for i in range(len(crossing)):
        over_x(i).wait_send()
    for i in range(relayed):
        over_y(i).wait_send()
    lax.fori_loop(0, n_ep, drain, 0)

    @pl.when(sides > 0)
    def _():
        lax.fori_loop(0, n_ep, drain_back, 0)
        conclude([1, 0])

    @pl.when(z == 0)
    def _():
        conclude([0])

    @pl.when(z == n_ep - 1)
    def _():
        conclude([1])

    @pl.when(sides == 0)
    def _():
        lax.fori_loop(0, n_ep, drain_back, 0)


def swap_plan(tokens, cotangent, expert_ids, route_weights, w_gate, w_up, w_down):
    n_grp, n_ep = lax.axis_size("grp"), lax.axis_size("ep")
    named = gw_rows(n_grp * n_ep)
    rows, width = tokens.shape
    unit = w_gate.shape[2] // QUARTERS
    any_ref, vmem = pl.BlockSpec(memory_space=pl.ANY), pl.BlockSpec(memory_space=pltpu.VMEM)
    bf16, f32, dma = jnp.bfloat16, jnp.float32, pltpu.SemaphoreType.DMA
    pieces = 3 * PIECES + PIECES // 4
    grad_tokens, grad_weights = pl.pallas_call(
        functools.partial(swap_kernel, n_grp, n_ep),
        out_shape=(
            pltpu.VMEM((rows, width), bf16),
            pltpu.VMEM(expert_ids.shape[::-1], bf16),
        ),
        in_specs=[any_ref] * 7,
        out_specs=(vmem, vmem),
        scratch_shapes=[
            pltpu.VMEM(expert_ids.shape[::-1], jnp.int32),
            pltpu.VMEM(route_weights.shape[::-1], f32),
            pltpu.VMEM((n_ep, CORES, rows, width), bf16),
            pltpu.VMEM((n_ep, CORES, rows, width), bf16),
            pltpu.VMEM((n_ep, CORES, 2 * named, LANES), bf16),
            pltpu.VMEM((2, 2, width, 4 * unit), bf16),
            pltpu.VMEM((2, 2, 2 * unit, width), bf16),
            pltpu.VMEM((n_ep, CORES, rows, width), f32),
            pltpu.VMEM((n_ep, 2, CORES * rows, LANES), f32),
            pltpu.VMEM((n_ep, rows, width), bf16),
            pltpu.VMEM((n_ep, named, LANES), bf16),
            pltpu.VMEM((n_ep, rows, width), bf16),
            pltpu.VMEM((n_ep, named, LANES), bf16),
            pltpu.VMEM((n_ep, rows, width), bf16),
            pltpu.VMEM((n_ep, named, LANES), bf16),
            pltpu.VMEM((2, n_ep, rows, width), bf16),
            pltpu.VMEM((2, n_ep, named, LANES), bf16),
            pltpu.VMEM((n_ep, CORES, named, LANES), bf16),
            dma((4 + 3 * QUARTERS,)), dma((4, n_ep, CORES)), dma((4, n_ep, 2)), dma((4, n_ep)),
            dma((pieces,)), dma((pieces,)), dma((pieces,)), dma((pieces,)),
            dma((n_ep, CUTS + 1)), dma((n_ep, CUTS + 1)),
            dma((n_ep, CUTS + 1)), dma((2, n_ep, CUTS + 1)),
        ],
        compiler_params=pltpu.CompilerParams(
            collective_id=0, has_side_effects=True, vmem_limit_bytes=VMEM_ROOM
        ),
    )(tokens, cotangent, expert_ids.T, route_weights.T, w_gate, w_up, w_down)
    return grad_tokens, grad_weights.T


def on_device(tokens, cotangent, expert_ids, route_weights, w_gate, w_up, w_down):
    n_grp, n_ep = lax.axis_size("grp"), lax.axis_size("ep")
    rows, width = tokens.shape
    swaps = lax.axis_size("parts") == 2 and n_grp == 2 * CORES and n_ep == 4
    fits = rows == LANES and width % LANES == 0 and w_gate.shape[2] == QUARTERS * LANES
    held = 2 * (w_gate.size + w_up.size + w_down.size) * 2 + n_ep * rows * width * 28
    plan = swap_plan if swaps and fits and held <= VMEM_ROOM else dispatch_plan
    return plan(tokens, cotangent, expert_ids, route_weights, w_gate, w_up, w_down)


def solution(mesh):
    in_specs = (
        P(("parts", "grp", "ep"), None),
        P(("parts", "grp", "ep"), None),
        P(("parts", "grp", "ep"), None),
        P(("parts", "grp", "ep"), None),
        P(("grp", "ep"), None, None),
        P(("grp", "ep"), None, None),
        P(("grp", "ep"), None, None),
    )
    out_specs = (P(("parts", "grp", "ep"), None), P(("parts", "grp", "ep"), None))
    return jax.shard_map(
        on_device, mesh=mesh, in_specs=in_specs, out_specs=out_specs, check_vma=False
    )
```

```python
import functools

import jax
import jax.numpy as jnp
from jax import lax
from jax.experimental import pallas as pl
from jax.experimental.pallas import tpu as pltpu
from jax.sharding import PartitionSpec as P

LANES = 128
CORES = 2
VMEM_ROOM = 56 * 1024 * 1024


def expert_grads(rows_in, grads_in, w_gate, w_up, w_down):
    contract = (((1,), (1,)), ((), ()))
    gate_pre = jnp.dot(rows_in, w_gate, preferred_element_type=jnp.float32)
    up_pre = jnp.dot(rows_in, w_up, preferred_element_type=jnp.float32)
    hidden_grad = lax.dot_general(grads_in, w_down, contract, preferred_element_type=jnp.float32)
    sigmoid_gate = jax.nn.sigmoid(gate_pre)
    activation = gate_pre * sigmoid_gate
    hidden = activation * up_pre
    weight_grad = jnp.sum(hidden_grad * hidden, axis=-1).astype(jnp.bfloat16)
    grad_up = (hidden_grad * activation).astype(jnp.bfloat16)
    grad_gate = (
        hidden_grad * up_pre * sigmoid_gate * (1.0 + gate_pre * (1.0 - sigmoid_gate))
    ).astype(jnp.bfloat16)
    row_terms = (
        lax.dot_general(grad_gate, w_gate, contract, preferred_element_type=jnp.float32)
        + lax.dot_general(grad_up, w_up, contract, preferred_element_type=jnp.float32)
    ).astype(jnp.bfloat16)
    return (row_terms, weight_grad)


def slot_plan(routes, experts, capacity):
    tok_rows, top_count = routes.shape
    flat_ids = routes.reshape(-1)
    pad_pair = flat_ids.shape[0]
    pair_ids = jnp.arange(pad_pair, dtype=jnp.int32)
    sort_order = jnp.argsort(flat_ids, stable=True)
    sorted_ids = flat_ids[sort_order]
    onehot = (flat_ids[:, None] == jnp.arange(experts, dtype=jnp.int32)[None, :]).astype(jnp.int32)
    counts = jnp.sum(onehot, axis=0)
    earlier = jnp.tri(experts, k=-1, dtype=jnp.int32)
    starts = jnp.sum(earlier * counts[None, :], axis=1)
    sorted_rank = pair_ids - starts[sorted_ids]
    sorted_slot = sorted_ids * capacity + sorted_rank
    slot_of_pair = jnp.zeros((pad_pair,), jnp.int32).at[sort_order].set(sorted_slot)
    slot_pair = jnp.full((experts * capacity,), pad_pair, jnp.int32).at[sorted_slot].set(sort_order)
    slot_token = jnp.where(slot_pair < pad_pair, slot_pair // top_count, tok_rows)
    return (slot_of_pair, slot_token, slot_pair)


def place_rows(source_rows, slot_token):
    padded = jnp.concatenate(
        [source_rows, jnp.zeros((1, source_rows.shape[1]), source_rows.dtype)], 0
    )
    return padded[slot_token]


def dispatch_plan(tokens, cotangent, expert_ids, route_weights, w_gate, w_up, w_down):
    group_count = lax.axis_size("grp")
    lane_count = lax.axis_size("ep")
    experts = group_count * lane_count
    tok_rows, top_count = expert_ids.shape
    model_width = tokens.shape[1]
    capacity = 2 * tok_rows * top_count // experts
    slot_of_pair, slot_token, unused_pairs = slot_plan(expert_ids, experts, capacity)
    send_rows = place_rows(tokens, slot_token).reshape(
        group_count, lane_count, capacity, model_width
    )
    send_grads = place_rows(cotangent, slot_token).reshape(
        group_count, lane_count, capacity, model_width
    )
    send_rows, send_grads = (
        lax.all_to_all(send_rows, "grp", split_axis=0, concat_axis=0, tiled=True),
        lax.all_to_all(send_grads, "grp", split_axis=0, concat_axis=0, tiled=True),
    )
    rows_in = lax.all_to_all(send_rows, "ep", split_axis=1, concat_axis=1, tiled=True)
    grads_in = lax.all_to_all(send_grads, "ep", split_axis=1, concat_axis=1, tiled=True)
    leading = rows_in.shape[:3]
    row_terms, weight_grad = expert_grads(
        rows_in.reshape(-1, model_width),
        grads_in.reshape(-1, model_width),
        w_gate[0],
        w_up[0],
        w_down[0],
    )
    row_terms = row_terms.reshape(leading + (model_width,))
    weight_grad = weight_grad.reshape(leading)
    row_terms, weight_grad = (
        lax.all_to_all(row_terms, "ep", split_axis=1, concat_axis=1, tiled=True),
        lax.all_to_all(weight_grad, "ep", split_axis=1, concat_axis=1, tiled=True),
    )
    row_terms, weight_grad = (
        lax.all_to_all(row_terms, "grp", split_axis=0, concat_axis=0, tiled=True),
        lax.all_to_all(weight_grad, "grp", split_axis=0, concat_axis=0, tiled=True),
    )
    row_terms = row_terms.reshape(experts * capacity, model_width)
    weight_grad = weight_grad.reshape(experts * capacity)
    picked = row_terms[slot_of_pair].reshape(tok_rows, top_count, model_width)
    grad_tokens = jnp.sum(route_weights[:, :, None] * picked.astype(jnp.float32), axis=1)
    grad_weights = weight_grad[slot_of_pair].reshape(tok_rows, top_count)
    return (grad_tokens.astype(jnp.bfloat16), grad_weights)


CUTS = 2
ORDER = tuple(range(CUTS - 1)) + (CUTS, CUTS - 1)
PIECES = 4
QUARTERS = 4
KINDS = (0, 1, 2, 3)


def gw_rows(experts):
    return -(-experts // 16) * 16


def pick(index, values):
    chosen = jnp.int32(values[0])
    for at in range(1, len(values)):
        if values[at] != values[at - 1]:
            chosen = jnp.where(index >= at, jnp.int32(values[at]), chosen)
    return chosen


def swap_kernel(
    n_grp, n_ep, tok_hbm, cot_hbm, ids_hbm, route_hbm, wg_hbm, wu_hbm, wd_hbm,
    out_ref, gw_ref,
    ids_ref, route_ref, tok, cot, rts, wgu, wdn, acc, sums, parts, parts_g, r1, r1_g, sent, sent_g, up, up_g, pair_g,
    load_sem, got_sem, z_sem, c_sem, wx_s, wx_r, wy_s, wy_r,
    s1_sem, r1_sem, s2_sem, r2_sem,
):
    rows, width = out_ref.shape
    unit = wgu.shape[3] // QUARTERS
    named = gw_rows(n_grp * n_ep)
    p, g, z = lax.axis_index("parts"), lax.axis_index("grp"), lax.axis_index("ep")
    x, c = g // CORES, g % CORES
    other_c = 1 - c
    experts = (g * n_ep + z, ((1 - x) * CORES + c) * n_ep + z)
    core_peer = {"parts": p, "grp": x * CORES + other_c, "ep": z}
    x_peer = {"parts": p, "grp": (1 - x) * CORES + c, "ep": z}
    y_peer = {"parts": 1 - p, "grp": g, "ep": z}

    def z_peer(step):
        return {"parts": p, "grp": g, "ep": z + step}

    barrier = pltpu.get_barrier_semaphore()

    def greet(peer):
        pl.semaphore_signal(barrier, inc=1, device_id=peer, device_id_type=pl.DeviceIdType.MESH)

    for peer in (core_peer, x_peer, y_peer):
        greet(peer)

    @pl.when(z > 0)
    def _():
        greet(z_peer(-1))

    @pl.when(z < n_ep - 1)
    def _():
        greet(z_peer(1))

    small = [
        pltpu.make_async_copy(ids_hbm, ids_ref, load_sem.at[2 + 3 * QUARTERS]),
        pltpu.make_async_copy(route_hbm, route_ref, load_sem.at[3 + 3 * QUARTERS]),
    ]
    for load in small:
        load.start()
    loads = [
        pltpu.make_async_copy(tok_hbm, tok.at[z, c], load_sem.at[0]),
        pltpu.make_async_copy(cot_hbm, cot.at[z, c], load_sem.at[1]),
    ]
    for q in range(QUARTERS):
        span = pl.ds(q * unit, unit)
        for i, (source, target) in enumerate((
            (wg_hbm.at[0, :, span], wgu.at[0, q // 2, :, pl.ds(q % 2 * 2 * unit, unit)]),
            (wu_hbm.at[0, :, span], wgu.at[0, q // 2, :, pl.ds((q % 2 * 2 + 1) * unit, unit)]),
            (wd_hbm.at[0, span, :], wdn.at[0, q // 2, pl.ds(q % 2 * unit, unit)]),
        )):
            loads.append(pltpu.make_async_copy(source, target, load_sem.at[2 + 3 * q + i]))
    for load in loads:
        load.start()

    acc[...] = jnp.zeros_like(acc)
    sums[...] = jnp.zeros_like(sums)
    for load in small:
        load.wait()
    item = lax.broadcasted_iota(jnp.int32, (named, LANES), 0)
    routed = jnp.zeros((named, LANES), jnp.float32)
    for k in range(ids_ref.shape[0]):
        routed += jnp.where(item == ids_ref[k:k + 1, :], route_ref[k:k + 1, :], 0.0)
    high = routed.astype(jnp.bfloat16)
    rts[z, c, 0:named, :] = high
    rts[z, c, named:2 * named, :] = (routed - high.astype(jnp.float32)).astype(jnp.bfloat16)

    for load in loads:
        load.wait()
    near = jnp.where(z > 0, 1, 0) + jnp.where(z < n_ep - 1, 1, 0)
    pl.semaphore_wait(barrier, 3 + near)

    def remote(source, target, send, recv, peer):
        return pltpu.make_async_remote_copy(
            src_ref=source, dst_ref=target, send_sem=send, recv_sem=recv,
            device_id=peer, device_id_type=pl.DeviceIdType.MESH,
        )

    sides = jnp.minimum(z, n_ep - 1 - z)

    low_half = 2 * z < n_ep - 1

    def place(k):
        step = jnp.where(k % 2 == 1, -((k + 1) // 2), k // 2)
        near_k = jnp.where(low_half, z + step, z - step)
        far_k = jnp.where(low_half, k, n_ep - 1 - k)
        return jnp.where(k <= 2 * sides, near_k, far_k)

    part = rows // 2

    def block(kind, zs, cs):
        if kind == 0:
            return tok.at[zs, cs]
        if kind == 1:
            return rts.at[zs, cs]
        return cot.at[zs, cs, pl.ds((kind - 2) * part, part)]

    def along_z(kind, zs, step):
        here = block(kind, zs, c)
        return remote(here, here, z_sem.at[kind, zs, (step + 1) // 2], got_sem.at[kind, zs, c],
                      z_peer(step))

    def to_core(kind, zs):
        here = block(kind, zs, c)
        return remote(here, here, c_sem.at[kind, zs], got_sem.at[kind, zs, c], core_peer)

    def arrived(kind, zs, cs):
        here = block(kind, zs, cs)
        remote(here, here, c_sem.at[kind, zs], got_sem.at[kind, zs, cs], core_peer).wait_recv()

    def each_z(kind, zs, act):
        @pl.when(jnp.logical_and(zs <= z, z < n_ep - 1))
        def _():
            act(along_z(kind, zs, 1))

        @pl.when(jnp.logical_and(zs >= z, z > 0))
        def _():
            act(along_z(kind, zs, -1))

    def start(copy):
        copy.start()

    def wait_send(copy):
        copy.wait_send()

    def take(k, *group):
        zs = place(k)
        for kind in group:
            arrived(kind, zs, c)
            each_z(kind, zs, start)
            to_core(kind, zs).start()

    def at_ends(act, *args):
        @pl.when(sides == 0)
        def _():
            act(*args)

    def inside(act, *args):
        @pl.when(sides > 0)
        def _():
            act(*args)

    downs = PIECES // 2
    tall, flat = width // PIECES, unit // downs

    def gate_up(e, j, h, at):
        lanes = pl.ds(pl.multiple_of(h * 2 * unit, 2 * unit), 2 * unit)
        return wgu.at[e, j, pl.ds(pl.multiple_of(at * tall, tall), tall), lanes]

    def down(e, j, h, at):
        return wdn.at[e, j, pl.ds(pl.multiple_of(h * unit + at * flat, flat), flat)]

    crossing = [(gate_up, 0, p, n) for n in range(PIECES)] + [(down, 0, p, n) for n in range(downs)]
    early = len(crossing)
    for h in range(2):
        crossing += [(gate_up, 1, h, p * downs + n) for n in range(downs)]
        crossing += [(down, 1, h, p * (downs // 2) + n) for n in range(downs // 2)]
    crossing += [(down, 1, 1, (1 - p) * (downs // 2) + n) for n in range(downs // 2)]
    middle, relayed = early + downs + downs // 2, len(crossing) - downs

    def piece(e, i):
        part, *place_of = crossing[i]
        return part(e, *place_of)

    def over_x(i):
        return remote(piece(0, i), piece(1, i), wx_s.at[i], wx_r.at[i], x_peer)

    def over_y(i):
        return remote(piece(1, i), piece(1, i), wy_s.at[i], wy_r.at[i], y_peer)

    def relay(i):
        over_x(i).wait_recv()
        over_y(i).start()

    contract = (((1,), (1,)), ((), ()))
    both = CORES * rows

    def scale_of(zs, expert):
        columns = []
        for cs in range(CORES):
            routes = rts[zs, cs, 0:named, :].astype(jnp.float32)
            routes += rts[zs, cs, named:2 * named, :].astype(jnp.float32)
            weight = jnp.sum(jnp.where(item == expert, routes, 0.0), axis=0, keepdims=True)
            columns.append(jnp.broadcast_to(weight, (rows, LANES)).T)
        return jnp.concatenate(columns, axis=0)

    def compute(zs, e, j, halves):
        expert = jnp.where(e == 0, experts[0], experts[1])
        scale = scale_of(zs, expert)
        rows_in = tok[zs].reshape(both, width)
        grads_in = cot[zs].reshape(both, width)
        low, high = halves[0] * unit, (halves[-1] + 1) * unit
        pres = jnp.dot(rows_in, wgu[e, j, :, 2 * low:2 * high], preferred_element_type=jnp.float32)
        hidden_grads = lax.dot_general(grads_in, wdn[e, j, low:high], contract,
                                       preferred_element_type=jnp.float32)
        lane_sums = jnp.zeros((both, LANES), jnp.float32)
        grads = []
        for at in range(len(halves)):
            gate_pre = pres[:, 2 * at * unit:(2 * at + 1) * unit]
            up_pre = pres[:, (2 * at + 1) * unit:(2 * at + 2) * unit]
            hidden_grad = hidden_grads[:, at * unit:(at + 1) * unit]
            sigmoid_gate = 1.0 / (1.0 + jnp.exp(-gate_pre))
            activation = gate_pre * sigmoid_gate
            lane_sums += hidden_grad * (activation * up_pre)
            hidden_grad = hidden_grad * scale
            grads.append((hidden_grad * up_pre * sigmoid_gate
                          * (1.0 + gate_pre * (1.0 - sigmoid_gate))).astype(jnp.bfloat16))
            grads.append((hidden_grad * activation).astype(jnp.bfloat16))
        sums[zs, e] += lane_sums
        terms = lax.dot_general(jnp.concatenate(grads, axis=1), wgu[e, j, :, 2 * low:2 * high],
                                contract, preferred_element_type=jnp.float32)
        acc[zs] += terms.reshape(CORES, rows, width)

    cut_rows = rows // CUTS
    cuts = [pl.ds(i * cut_rows, cut_rows) for i in range(CUTS)]

    def first_copy(zs, i):
        if i < CUTS:
            source, target = parts.at[zs, cuts[i]], r1.at[zs, cuts[i]]
        else:
            source, target = parts_g.at[zs], r1_g.at[zs]
        return remote(source, target, s1_sem.at[zs, i], r1_sem.at[zs, i], core_peer)

    def second_copy(zs, step, i):
        way = (step + 1) // 2
        if i < CUTS:
            source, target = sent.at[zs, cuts[i]], up.at[way, zs, cuts[i]]
        else:
            source, target = sent_g.at[zs], up_g.at[way, zs]
        return remote(source, target, s2_sem.at[zs, i], r2_sem.at[way, zs, i], z_peer(step))

    def finish(zs):
        parts[zs] = acc[zs, other_c].astype(jnp.bfloat16)
        for i in range(CUTS):
            first_copy(zs, i).start()
        lanes = sums[zs].reshape(2 * both, LANES)
        high = lanes.astype(jnp.bfloat16)
        low = (lanes - high.astype(jnp.float32)).astype(jnp.bfloat16)
        ones = jnp.ones((16, LANES), jnp.bfloat16)
        totals = lax.dot_general(ones, high, contract, preferred_element_type=jnp.float32)
        totals += lax.dot_general(ones, low, contract, preferred_element_type=jnp.float32)
        for cs in range(CORES):
            found = jnp.zeros((named, LANES), jnp.float32)
            for e in range(2):
                at = e * both + cs * rows
                found += jnp.where(item == experts[e], totals[0:1, at:at + rows], 0.0)
            pair_g[zs, cs] = found.astype(jnp.bfloat16)
        parts_g[zs] = pair_g[zs, other_c]
        first_copy(zs, CUTS).start()

    def summed(zs, ways, i):
        first_copy(zs, i).wait_recv()
        for way in ways:
            second_copy(zs, 2 * way - 1, i).wait_recv()
        if i < CUTS:
            total = acc[zs, c, cuts[i]] + r1[zs, cuts[i]].astype(jnp.float32)
            for way in ways:
                total += up[way, zs, cuts[i]].astype(jnp.float32)
            return total
        total = pair_g[zs, c].astype(jnp.float32) + r1_g[zs].astype(jnp.float32)
        for way in ways:
            total += up_g[way, zs].astype(jnp.float32)
        return total

    def pass_on(zs, ways, step):
        for i in ORDER:
            total = summed(zs, ways, i).astype(jnp.bfloat16)
            if i < CUTS:
                sent[zs, cuts[i]] = total
            else:
                sent_g[zs] = total
            second_copy(zs, step, i).start()

    def send_back(k, inner):
        zs = place(k)

        @pl.when(zs > z)
        def _():
            pass_on(zs, [1] if inner else [], 1)

        @pl.when(zs < z)
        def _():
            pass_on(zs, [0] if inner else [], -1)

    def conclude(ways):
        for i in ORDER:
            total = summed(z, ways, i)
            if i < CUTS:
                out_ref[cuts[i], :] = total.astype(jnp.bfloat16)
            else:
                for k in range(ids_ref.shape[0]):
                    picked = jnp.where(item == ids_ref[k:k + 1, :], total, 0.0)
                    gw_ref[k:k + 1, :] = jnp.sum(picked, axis=0, keepdims=True).astype(jnp.bfloat16)

    def own_rest(inward):
        @pl.when(low_half)
        def _():
            along_z(KINDS[3], z, inward).start()

        @pl.when(jnp.logical_not(low_half))
        def _():
            along_z(KINDS[3], z, -inward).start()

    over_x(0).start()
    for kind in KINDS[:3]:
        each_z(kind, z, start)
    at_ends(each_z, KINDS[3], z, start)
    inside(own_rest, -1)
    for kind in KINDS:
        to_core(kind, z).start()
    for i in range(1, len(crossing)):
        over_x(i).start()

    def block_here(k):
        for kind in KINDS:
            arrived(kind, place(k), other_c)

    steps = (0, early, middle, relayed)

    def units_here(step):
        for i in range(steps[step], steps[step + 1]):
            over_y(i).wait_recv()
        if step == 2:
            for i in range(relayed, len(crossing)):
                over_x(i).wait_recv()

    far = n_ep - 1
    start_events = [
        ((0, 0, 0), [(block_here, 0)]),
        ((0, 0, 1), []),
    ]
    end_plan = start_events + [
        ((1, 0, 0), [
            (relay, 0), (take, 1, 0, 1), (relay, 1), (take, 1, 2), (relay, 2),
            (take, 1, 3), (relay, 3), (block_here, 1),
        ]),
        ((1, 0, 1), [(relay, 4)]),
        ((0, 1, 0), [
            (take, far - 1, 0, 1), (relay, 5), (relay, 6),
            (units_here, 0), (take, far, 0, 1), (relay, 7),
        ]),
        ((1, 1, 0), []),
        ((far, 0, 0), [
            (relay, 8), (take, far, 2), (relay, 9), (take, far, 3),
            (block_here, far),
        ]),
        ((far, 0, 1), [(relay, 10), (take, far - 1, 2)]),
        ((far, 1, 0), []),
        ((far, 1, 2), [(units_here, 1)]),
        ((1, 1, 2), []),
        ((0, 1, 2), [(take, far - 1, 3)]),
        ((far, 1, 3), [(units_here, 2)]),
        ((far - 1, 0, 0), [(block_here, far - 1)]),
        ((far - 1, 0, 1), []), ((far - 1, 1, 0), []), ((far - 1, 1, 1), []),
        ((1, 1, 3), []), ((0, 1, 3), []),
    ]
    inner_plan = start_events + [
        ((1, 0, 0), [
            (relay, 0), (take, 1, 0, 1), (take, far - 1, 0, 1), (relay, 1),
            (take, 1, 2), (relay, 2), (take, 1, 3), (own_rest, 1), (relay, 3),
            (block_here, 1),
        ]),
        ((1, 0, 1), [(take, far, 0, 1), (relay, 4)]),
        ((0, 1, 0), [
            (take, far, 2), (relay, 5), (take, far, 3), (take, far - 1, 2),
            (relay, 6), (units_here, 0), (take, far - 1, 3), (relay, 7),
        ]),
        ((1, 1, 0), []),
        ((far - 1, 0, 0), [(block_here, far - 1), (relay, 8)]),
        ((far - 1, 0, 1), []),
        ((far - 1, 1, 0), [(relay, 9)]),
        ((far, 0, 0), [(block_here, far)]),
        ((far, 0, 1), [(relay, 10)]),
        ((far, 1, 0), []),
        ((far, 1, 2), [(units_here, 1)]),
        ((1, 1, 2), []), ((0, 1, 2), []),
        ((far, 1, 3), [(units_here, 2)]),
        ((far - 1, 1, 1), []), ((1, 1, 3), []), ((0, 1, 3), []),
    ]

    def run_events(acts):
        for act, *args in acts:
            act(*args)

    def turn(i, carry):
        def step_of(plan, low, high):
            if high - low == 1:
                run_events(plan[low][1])
                return
            cut = (low + high) // 2
            for first_at, last_at, here in ((low, cut, i < cut), (cut, high, i >= cut)):
                if any(acts for task, acts in plan[first_at:last_at]):
                    @pl.when(here)
                    def _(first_at=first_at, last_at=last_at):
                        step_of(plan, first_at, last_at)

        at_ends(step_of, end_plan, 0, len(end_plan))
        inside(step_of, inner_plan, 0, len(inner_plan))

        k, e, j = (
            jnp.where(sides == 0, *(pick(i, [task[field] for task, acts in plan])
                                    for plan in (end_plan, inner_plan)))
            for field in range(3)
        )

        @pl.when(j < 2)
        def _():
            compute(place(k), e, j, (0, 1))

        for half in range(2):
            @pl.when(j == 2 + half)
            def _(half=half):
                compute(place(k), e, 1, (half,))

        tails = [(at, task) for at, (task, acts) in enumerate(end_plan)
                 if task[0] and task[1:] in ((1, 1), (1, 3))]

        @pl.when(jnp.logical_and(i > tails[0][0], sides == 0))
        def _():
            for at, task in tails:
                @pl.when(i == at + 1)
                def _(task=task):
                    send_back(task[0], False)

        whole = jnp.logical_and(e == 1, j == 1)

        @pl.when(jnp.logical_or(j == 3, whole))
        def _():
            finish(place(k))

        return carry

    assert len(end_plan) == len(inner_plan)
    lax.fori_loop(0, len(end_plan), turn, 0)

    @pl.when(sides > 0)
    def _():
        for k in [n_ep - 1] + list(range(1, n_ep - 1)):
            send_back(k, True)

    def drain(zs, carry):
        for kind in KINDS:
            each_z(kind, zs, wait_send)
            to_core(kind, zs).wait_send()
        for i in range(CUTS + 1):
            first_copy(zs, i).wait_send()
        return carry

    def drain_back(zs, carry):
        @pl.when(zs != z)
        def _():
            for i in range(CUTS + 1):
                second_copy(zs, 1, i).wait_send()

        return carry

    for i in range(len(crossing)):
        over_x(i).wait_send()
    for i in range(relayed):
        over_y(i).wait_send()
    lax.fori_loop(0, n_ep, drain, 0)

    @pl.when(sides > 0)
    def _():
        lax.fori_loop(0, n_ep, drain_back, 0)
        conclude([1, 0])

    @pl.when(z == 0)
    def _():
        conclude([0])

    @pl.when(z == n_ep - 1)
    def _():
        conclude([1])

    @pl.when(sides == 0)
    def _():
        lax.fori_loop(0, n_ep, drain_back, 0)


def swap_plan(tokens, cotangent, expert_ids, route_weights, w_gate, w_up, w_down):
    n_grp, n_ep = lax.axis_size("grp"), lax.axis_size("ep")
    named = gw_rows(n_grp * n_ep)
    rows, width = tokens.shape
    unit = w_gate.shape[2] // QUARTERS
    any_ref, vmem = pl.BlockSpec(memory_space=pl.ANY), pl.BlockSpec(memory_space=pltpu.VMEM)
    bf16, f32, dma = jnp.bfloat16, jnp.float32, pltpu.SemaphoreType.DMA
    pieces = 3 * PIECES + PIECES // 4
    grad_tokens, grad_weights = pl.pallas_call(
        functools.partial(swap_kernel, n_grp, n_ep),
        out_shape=(
            pltpu.VMEM((rows, width), bf16),
            pltpu.VMEM(expert_ids.shape[::-1], bf16),
        ),
        in_specs=[any_ref] * 7,
        out_specs=(vmem, vmem),
        scratch_shapes=[
            pltpu.VMEM(expert_ids.shape[::-1], jnp.int32),
            pltpu.VMEM(route_weights.shape[::-1], f32),
            pltpu.VMEM((n_ep, CORES, rows, width), bf16),
            pltpu.VMEM((n_ep, CORES, rows, width), bf16),
            pltpu.VMEM((n_ep, CORES, 2 * named, LANES), bf16),
            pltpu.VMEM((2, 2, width, 4 * unit), bf16),
            pltpu.VMEM((2, 2, 2 * unit, width), bf16),
            pltpu.VMEM((n_ep, CORES, rows, width), f32),
            pltpu.VMEM((n_ep, 2, CORES * rows, LANES), f32),
            pltpu.VMEM((n_ep, rows, width), bf16),
            pltpu.VMEM((n_ep, named, LANES), bf16),
            pltpu.VMEM((n_ep, rows, width), bf16),
            pltpu.VMEM((n_ep, named, LANES), bf16),
            pltpu.VMEM((n_ep, rows, width), bf16),
            pltpu.VMEM((n_ep, named, LANES), bf16),
            pltpu.VMEM((2, n_ep, rows, width), bf16),
            pltpu.VMEM((2, n_ep, named, LANES), bf16),
            pltpu.VMEM((n_ep, CORES, named, LANES), bf16),
            dma((4 + 3 * QUARTERS,)), dma((4, n_ep, CORES)), dma((4, n_ep, 2)), dma((4, n_ep)),
            dma((pieces,)), dma((pieces,)), dma((pieces,)), dma((pieces,)),
            dma((n_ep, CUTS + 1)), dma((n_ep, CUTS + 1)),
            dma((n_ep, CUTS + 1)), dma((2, n_ep, CUTS + 1)),
        ],
        compiler_params=pltpu.CompilerParams(
            collective_id=0, has_side_effects=True, vmem_limit_bytes=VMEM_ROOM
        ),
    )(tokens, cotangent, expert_ids.T, route_weights.T, w_gate, w_up, w_down)
    return grad_tokens, grad_weights.T


def on_device(tokens, cotangent, expert_ids, route_weights, w_gate, w_up, w_down):
    n_grp, n_ep = lax.axis_size("grp"), lax.axis_size("ep")
    rows, width = tokens.shape
    swaps = lax.axis_size("parts") == 2 and n_grp == 2 * CORES and n_ep == 4
    fits = rows == LANES and width % LANES == 0 and w_gate.shape[2] == QUARTERS * LANES
    held = 2 * (w_gate.size + w_up.size + w_down.size) * 2 + n_ep * rows * width * 28
    plan = swap_plan if swaps and fits and held <= VMEM_ROOM else dispatch_plan
    return plan(tokens, cotangent, expert_ids, route_weights, w_gate, w_up, w_down)


def solution(mesh):
    in_specs = (
        P(("parts", "grp", "ep"), None),
        P(("parts", "grp", "ep"), None),
        P(("parts", "grp", "ep"), None),
        P(("parts", "grp", "ep"), None),
        P(("grp", "ep"), None, None),
        P(("grp", "ep"), None, None),
        P(("grp", "ep"), None, None),
    )
    out_specs = (P(("parts", "grp", "ep"), None), P(("parts", "grp", "ep"), None))
    return jax.shard_map(
        on_device, mesh=mesh, in_specs=in_specs, out_specs=out_specs, check_vma=False
    )
```
